32 devices in a mesh: ctx: 16 (over z, y, x), head: 2 (over core).
Axes of the slice: x: 2, y: 2, z: 4, core: 2. Of those that a mesh axis runs over, the one named last changes fastest.
Arguments:
- q_nope: bfloat16 [2048, 8192], P('ctx', 'head'), may hold values from -6 to 6
- q_rope: bfloat16 [2048, 4096], P('ctx', 'head'), may hold values from -16 to 16
- latent: bfloat16 [2048, 512], P('ctx'), may hold values from -6 to 6
- k_rope: bfloat16 [2048, 64], P('ctx'), may hold values from -16 to 16
- d_out: bfloat16 [2048, 8192], P('ctx', 'head'), may hold values from -6 to 6
- out_heads: bfloat16 [2048, 8192], P('ctx', 'head'), may hold values from -6 to 6
- lse_rest: float32 [2048, 64], P('ctx', 'head'), may hold values from 3 to 7
- key_up_weight: bfloat16 [512, 8192], P(None, 'head'), may hold values from -0.5 to 0.5
- value_up_weight: bfloat16 [512, 8192], P(None, 'head'), may hold values from -0.5 to 0.5
Outputs:
- d_q_nope: bfloat16 [2048, 8192], P('ctx', 'head')
- d_q_rope: bfloat16 [2048, 4096], P('ctx', 'head')
- latent_gradient: float32 [2048, 512], P('ctx')
- d_k_rope: float32 [2048, 64], P('ctx')
The draws below stay inside these ranges and needn't reach their ends.
All inputs are finite; a program needn't handle non-finite values.
Results may differ from the reference program's by a relative error of at most 0.0076.
Values may be sent and summed in bfloat16 or wider, within the bound.
No kernel may reach another device: no remote copies, remote signals or barrier semaphores. Data moves between devices by JAX's collectives and lax.ppermute only.
A program may use at most 64 MiB of HBM per device.

```python
import jax
import jax.numpy as jnp
from jax import lax

LATENT_WIDTH = 512
ROTARY_WIDTH = 64
HEAD_WIDTH = 128
LOCAL_HEAD_COUNT = 64
HOPS = 3
SPAN = 64
TOKEN_COUNT = 2048
N_CTX = 16


def draw_q_rope(key, part):
    values = jax.random.normal(jax.random.fold_in(key, 3), (TOKEN_COUNT, LOCAL_HEAD_COUNT, ROTARY_WIDTH), jnp.float32)
    return jnp.clip(values, -16.0, 16.0).reshape(TOKEN_COUNT, LOCAL_HEAD_COUNT * ROTARY_WIDTH).astype(jnp.bfloat16)


def draw_k_rope(key, part):
    values = jax.random.normal(jax.random.fold_in(key, 13), (TOKEN_COUNT, ROTARY_WIDTH), jnp.float32)
    return jnp.clip(values, -16.0, 16.0).astype(jnp.bfloat16)


def steps_of(rng, dims, split, low, top_value):
    gain, own = 1.0, jax.random.fold_in(rng, 6)
    for position, shards_of in split:
        heights = jnp.exp(jax.random.uniform(jax.random.fold_in(own, position), (shards_of,), jnp.float32, low / len(split), top_value / len(split)))
        gain = gain * jnp.repeat(heights, dims[position] // shards_of).reshape([-1 if axis == position else 1 for axis in range(len(dims))])
    return gain


def gaussian(own_key, shape, spread, reach, shards=(), held_as=jnp.bfloat16):
    values = spread * jax.random.normal(own_key, shape, jnp.float32)
    if shards:
        values = values * steps_of(own_key, shape, shards, -0.22, 0.18)
    return jnp.clip(values, -reach, reach).astype(held_as)


def setup_inputs(seed: int = 0) -> dict:
    key_list = jax.random.split(jax.random.key(seed), 10)
    return {
        "q_nope": gaussian(key_list[0], (TOKEN_COUNT, LOCAL_HEAD_COUNT * HEAD_WIDTH), 1.0, 6.0, ((0, 16), (1, 2))),
        "q_rope": draw_q_rope(jax.random.fold_in(key_list[9], 71), 0),
        "latent": gaussian(key_list[2], (TOKEN_COUNT, LATENT_WIDTH), 1.0, 6.0, ((0, 16),)),
        "k_rope": draw_k_rope(jax.random.fold_in(key_list[9], 71), 0),
        "d_out": gaussian(key_list[4], (TOKEN_COUNT, LOCAL_HEAD_COUNT * HEAD_WIDTH), 1.0, 6.0, ((0, 16), (1, 2))),
        "out_heads": gaussian(key_list[5], (TOKEN_COUNT, LOCAL_HEAD_COUNT * HEAD_WIDTH), 1.0, 6.0, ((0, 16), (1, 2))),
        "lse_rest": jnp.clip(3.0 + 4.0 * jax.random.uniform(key_list[6], (TOKEN_COUNT, LOCAL_HEAD_COUNT), jnp.float32) ** steps_of(key_list[6], (TOKEN_COUNT, LOCAL_HEAD_COUNT), ((0, 16), (1, 2)), -0.2, 0.2), 3.0, 7.0),
        "key_up_weight": gaussian(key_list[7], (LATENT_WIDTH, LOCAL_HEAD_COUNT * HEAD_WIDTH), HEAD_WIDTH ** -0.5, 0.5, ((1, 2),)),
        "value_up_weight": gaussian(key_list[8], (LATENT_WIDTH, LOCAL_HEAD_COUNT * HEAD_WIDTH), HEAD_WIDTH ** -0.5, 0.5, ((1, 2),)),
    }


def rounded(values):
    return lax.optimization_barrier(values.astype(jnp.bfloat16)).astype(jnp.float32)


def scores_of(query_abs, query_rot, key_lat, key_rot, softmax_scale):
    highest = lax.Precision.HIGHEST
    return (jnp.einsum("...qhl,...kl->...hqk", query_abs, key_lat, precision=highest)
            + jnp.einsum("...qhr,...kr->...hqk", query_rot, key_rot, precision=highest)) * softmax_scale


def backward_terms(scores, row_lse, row_delta, query_abs, query_rot, query_do, key_lat, key_rot, softmax_scale):
    highest = lax.Precision.HIGHEST
    weights = jnp.exp(scores - row_lse[..., None])
    weights_b = rounded(weights)
    d_weights = jnp.einsum("...qhl,...kl->...hqk", query_do, key_lat, precision=highest)
    d_scores = rounded(weights * (d_weights - row_delta[..., None]) * softmax_scale)
    dq_abs = jnp.einsum("...hqk,...kl->...qhl", d_scores, key_lat, precision=highest)
    dq_rot = jnp.einsum("...hqk,...kr->...qhr", d_scores, key_rot, precision=highest)
    dkey_lat = (jnp.einsum("...hqk,...qhl->...kl", d_scores, query_abs, precision=highest)
                + jnp.einsum("...hqk,...qhl->...kl", weights_b, query_do, precision=highest))
    dkey_rot = jnp.einsum("...hqk,...qhr->...kr", d_scores, query_rot, precision=highest)
    return dq_abs, dq_rot, dkey_lat, dkey_rot


def reference(q_nope, q_rope, latent, k_rope, d_out, out_heads, lse_rest, key_up_weight, value_up_weight):
    highest = lax.Precision.HIGHEST
    softmax_scale = (HEAD_WIDTH + ROTARY_WIDTH) ** -0.5
    count_rows = 2 * SPAN
    half_rows = SPAN
    key_matrix = key_up_weight.astype(jnp.float32).reshape(LATENT_WIDTH, LOCAL_HEAD_COUNT, HEAD_WIDTH)
    value_matrix = value_up_weight.astype(jnp.float32).reshape(LATENT_WIDTH, LOCAL_HEAD_COUNT, HEAD_WIDTH)
    latent_rows_full = latent.astype(jnp.float32).reshape(N_CTX, count_rows, LATENT_WIDTH)
    rot_all = k_rope.astype(jnp.float32).reshape(N_CTX, count_rows, ROTARY_WIDTH)
    ranks = jnp.arange(N_CTX, dtype=jnp.int32)
    inputs_all = (ranks, q_nope.reshape(N_CTX, count_rows, LOCAL_HEAD_COUNT, HEAD_WIDTH),
                  q_rope.reshape(N_CTX, count_rows, LOCAL_HEAD_COUNT, ROTARY_WIDTH),
                  d_out.reshape(N_CTX, count_rows, LOCAL_HEAD_COUNT, HEAD_WIDTH),
                  out_heads.reshape(N_CTX, count_rows, LOCAL_HEAD_COUNT, HEAD_WIDTH),
                  lse_rest.reshape(N_CTX, count_rows, LOCAL_HEAD_COUNT))
    positions = jnp.arange(half_rows, dtype=jnp.int32)
    causal = positions[None, :] <= positions[:, None]
    own_mask = jnp.concatenate([jnp.concatenate([causal, jnp.zeros_like(causal)], axis=1),
                                jnp.concatenate([jnp.ones_like(causal), causal], axis=1)], axis=0)

    def paired_rows(values, wrapped):
        return jnp.stack([jnp.where(wrapped, values[half_rows:], values[:half_rows]), values[half_rows:]])

    def paired_keys(values, wrapped):
        return jnp.stack([values[:half_rows], jnp.where(wrapped, values[half_rows:], values[:half_rows])])

    def paired_stats(first_part, second_part, wrapped):
        return jnp.stack([jnp.where(wrapped, second_part, first_part), second_part])

    def device_step(grads, inputs):
        latent_grad_sum, grad_rot = grads
        rank, nope_blk, rot_blk, dout_blk, out_blk, rest_blk = inputs
        q_abs = rounded(jnp.einsum("qhd,lhd->qhl", nope_blk.astype(jnp.float32), key_matrix, precision=highest))
        do_lat = rounded(jnp.einsum("qhd,lhd->qhl", dout_blk.astype(jnp.float32), value_matrix, precision=highest))
        q_rot = rot_blk.astype(jnp.float32)
        deltas = jnp.transpose(jnp.sum(dout_blk.astype(jnp.float32) * out_blk.astype(jnp.float32), axis=2))
        outside = jnp.transpose(rest_blk.astype(jnp.float32))
        own_lat = lax.dynamic_index_in_dim(latent_rows_full, rank, 0, keepdims=False)
        own_rot = lax.dynamic_index_in_dim(rot_all, rank, 0, keepdims=False)
        score_own = jnp.where(own_mask[None], scores_of(q_abs, q_rot, own_lat, own_rot, softmax_scale), -jnp.inf)
        own_max = jnp.max(score_own, axis=2)
        first_max = own_max[:, :half_rows]
        second_max = own_max[:, half_rows:]
        items = []
        for distance in range(1, HOPS):
            source = ((rank - distance) % N_CTX).astype(jnp.int32)
            key_lat = lax.dynamic_index_in_dim(latent_rows_full, source, 0, keepdims=False)
            key_rot = lax.dynamic_index_in_dim(rot_all, source, 0, keepdims=False)
            wrapped = rank < distance
            pair_q = (paired_rows(q_abs, wrapped), paired_rows(q_rot, wrapped), paired_rows(do_lat, wrapped))
            pair_lat = paired_keys(key_lat, wrapped)
            pair_rot = paired_keys(key_rot, wrapped)
            pair_scores = scores_of(pair_q[0], pair_q[1], pair_lat, pair_rot, softmax_scale)
            pair_max = jnp.max(pair_scores, axis=3)
            first_max = jnp.maximum(first_max, jnp.where(wrapped, -jnp.inf, pair_max[0]))
            second_max = jnp.maximum(second_max, jnp.maximum(pair_max[1], jnp.where(wrapped, pair_max[0], -jnp.inf)))
            items.append((source, wrapped, pair_q, pair_lat, pair_rot, pair_scores))
        row_max = jnp.concatenate([first_max, second_max], axis=1)
        own_total = jnp.sum(jnp.exp(score_own - row_max[..., None]), axis=2)
        first_total = own_total[:, :half_rows]
        second_total = own_total[:, half_rows:]
        for source, wrapped, pair_q, pair_lat, pair_rot, pair_scores in items:
            pair_rows_max = paired_stats(first_max, second_max, wrapped)
            pair_total = jnp.sum(jnp.exp(pair_scores - pair_rows_max[..., None]), axis=3)
            first_total = first_total + jnp.where(wrapped, 0.0, pair_total[0])
            second_total = second_total + pair_total[1] + jnp.where(wrapped, pair_total[0], 0.0)
        window_lse = row_max + jnp.log(jnp.concatenate([first_total, second_total], axis=1))
        larger = jnp.maximum(window_lse, outside)
        row_lse = larger + jnp.log(jnp.exp(window_lse - larger) + jnp.exp(outside - larger))
        dq_abs, dq_rot, dkey_lat, dkey_rot = backward_terms(score_own, row_lse, deltas, q_abs, q_rot, do_lat,
                                                            own_lat, own_rot, softmax_scale)
        latent_grad_sum = latent_grad_sum.at[rank].add(dkey_lat)
        grad_rot = grad_rot.at[rank].add(dkey_rot)
        for source, wrapped, pair_q, pair_lat, pair_rot, pair_scores in items:
            pair_lse = paired_stats(row_lse[:, :half_rows], row_lse[:, half_rows:], wrapped)
            pair_delta = paired_stats(deltas[:, :half_rows], deltas[:, half_rows:], wrapped)
            pq_abs, pq_rot, pk_lat, pk_rot = backward_terms(pair_scores, pair_lse, pair_delta, pair_q[0], pair_q[1],
                                                            pair_q[2], pair_lat, pair_rot, softmax_scale)
            dq_abs = dq_abs + jnp.concatenate([jnp.where(wrapped, 0.0, pq_abs[0]),
                                               pq_abs[1] + jnp.where(wrapped, pq_abs[0], 0.0)], axis=0)
            dq_rot = dq_rot + jnp.concatenate([jnp.where(wrapped, 0.0, pq_rot[0]),
                                               pq_rot[1] + jnp.where(wrapped, pq_rot[0], 0.0)], axis=0)
            lat_term = jnp.concatenate([pk_lat[0] + jnp.where(wrapped, 0.0, pk_lat[1]),
                                        jnp.where(wrapped, pk_lat[1], 0.0)], axis=0)
            rot_term = jnp.concatenate([pk_rot[0] + jnp.where(wrapped, 0.0, pk_rot[1]),
                                        jnp.where(wrapped, pk_rot[1], 0.0)], axis=0)
            latent_grad_sum = latent_grad_sum.at[source].add(lat_term)
            grad_rot = grad_rot.at[source].add(rot_term)
        dq_nope = jnp.einsum("qhl,lhd->qhd", rounded(dq_abs), key_matrix, precision=highest).astype(jnp.bfloat16)
        outputs = (dq_nope.reshape(count_rows, LOCAL_HEAD_COUNT * HEAD_WIDTH),
                   dq_rot.astype(jnp.bfloat16).reshape(count_rows, LOCAL_HEAD_COUNT * ROTARY_WIDTH))
        return (latent_grad_sum, grad_rot), outputs

    start_index = (jnp.zeros((N_CTX, count_rows, LATENT_WIDTH), jnp.float32), jnp.zeros((N_CTX, count_rows, ROTARY_WIDTH), jnp.float32))
    (latent_grad_sum, grad_rot), (dq_nope, dq_rope) = lax.scan(device_step, start_index, inputs_all)
    d_q_nope = dq_nope.reshape(TOKEN_COUNT, LOCAL_HEAD_COUNT * HEAD_WIDTH)
    d_q_rope = dq_rope.reshape(TOKEN_COUNT, LOCAL_HEAD_COUNT * ROTARY_WIDTH)
    latent_gradient = latent_grad_sum.reshape(TOKEN_COUNT, LATENT_WIDTH)
    d_k_rope = grad_rot.reshape(TOKEN_COUNT, ROTARY_WIDTH)
    return d_q_nope, d_q_rope, latent_gradient, d_k_rope
```

```python
import functools

import jax
import jax.numpy as jnp
from jax import lax
from jax.experimental import pallas as pl
from jax.experimental.pallas import tpu as pltpu
from jax.sharding import PartitionSpec as P

HEAD_WIDTH = 128
HOPS = 3
GROUP = 4
MIB = 1 << 20

NT = (((1,), (1,)), ((), ()))
TN = (((0,), (0,)), ((), ()))


def dot(a, b, dims=(((1,), (0,)), ((), ()))):
    return lax.dot_general(a, b, dims, preferred_element_type=jnp.float32)


def passed_along(block, axis, distance):
    count = lax.axis_size(axis)
    return lax.ppermute(block, axis, [((i - distance) % count, i) for i in range(count)])


def params(limit_mib, **extra):
    return pltpu.CompilerParams(vmem_limit_bytes=limit_mib * MIB, **extra)


def cost(flops, moved):
    return pl.CostEstimate(flops=int(flops), bytes_accessed=int(moved), transcendentals=0)


def pack_kernel(lat_ref, rot_ref, out_ref):
    width = lat_ref.shape[1]
    rot = jnp.transpose(rot_ref[...].astype(jnp.float32)).astype(out_ref.dtype)
    out_ref[:, :width] = lat_ref[...]
    out_ref[:, width:] = jnp.concatenate([rot, rot], axis=1)


def project_kernel(nope_ref, rope_ref, dout_ref, saved_ref, wk_ref, wv_ref, qx_ref, do_ref, delta_ref):
    rows = nope_ref.shape[0]
    width = wk_ref.shape[0]
    lanes = lax.broadcasted_iota(jnp.int32, (rows, HEAD_WIDTH), 1)
    ones = jnp.ones((8, HEAD_WIDTH), jnp.bfloat16)
    for g in range(GROUP):
        cols = slice(g * HEAD_WIDTH, (g + 1) * HEAD_WIDTH)
        d_out = dout_ref[:, cols]
        qx_ref[g, :, :width] = dot(nope_ref[:, cols], wk_ref[:, cols], NT).astype(jnp.bfloat16)
        do_ref[g] = dot(d_out, wv_ref[:, cols], NT).astype(jnp.bfloat16)
        prod = d_out.astype(jnp.float32) * saved_ref[:, cols].astype(jnp.float32)
        high = prod.astype(jnp.bfloat16)
        low = (prod - high.astype(jnp.float32)).astype(jnp.bfloat16)
        delta_ref[g] = (dot(ones, high, NT) + dot(ones, low, NT))[0:1]
        pair = rope_ref[:, (g // 2) * HEAD_WIDTH : (g // 2 + 1) * HEAD_WIDTH]
        mine = (lanes < HEAD_WIDTH // 2) if g % 2 == 0 else (lanes >= HEAD_WIDTH // 2)
        qx_ref[g, :, width:] = jnp.where(mine, pair, jnp.zeros_like(pair))


def scores_kernel(
    scale, qx_ref, do_ref, delta_ref, rest_ref, own_ref, near_ref, far_ref,
    ds_ref, pt_ref, c1_ref, c2_ref, keys_ref, bias_ref,
):
    rank = lax.axis_index("ctx")
    heads, rows, wide = qx_ref.shape
    width = do_ref.shape[2]
    half = rows // 2
    base = 2 * rows
    full = 3 * rows
    keys_ref[:half] = near_ref[:half]
    keys_ref[half:rows] = far_ref[:half]
    keys_ref[rows:base] = own_ref[...]
    keys_ref[base : base + half] = near_ref[half:]
    keys_ref[base + half :] = far_ref[half:]
    row = lax.broadcasted_iota(jnp.int32, (rows, rows), 0)
    col = lax.broadcasted_iota(jnp.int32, (rows, rows), 1)
    late = col >= half
    wrapped = jnp.where(row < half, rank, rank - 1) < 1
    off = jnp.float32(-jnp.inf)
    bias_ref[:rows] = jnp.where(jnp.logical_or(late, jnp.logical_not(wrapped)), 0.0, off)
    bias_ref[rows:base] = jnp.where(row <= col, 0.0, off)
    bias_ref[base:] = jnp.where(jnp.logical_and(late, wrapped), 0.0, off)

    def run(count):
        def body(p, carry):
            q = qx_ref[pl.ds(2 * p, 2)].reshape(2 * rows, wide)
            d = do_ref[pl.ds(2 * p, 2)].reshape(2 * rows, width)
            bias = bias_ref[:count]
            rest = jnp.concatenate([rest_ref[pl.ds(2 * p, 1)], rest_ref[pl.ds(2 * p + 1, 1)]], axis=1)
            delta = jnp.concatenate([delta_ref[2 * p], delta_ref[2 * p + 1]], axis=1)
            s = dot(keys_ref[:count], q, NT) * scale + jnp.concatenate([bias, bias], axis=1)
            top = jnp.maximum(jnp.max(s, axis=0, keepdims=True), rest)
            e = jnp.exp(s - top)
            total = jnp.sum(e, axis=0, keepdims=True) + jnp.exp(rest - top)
            inverse = 1.0 / total
            dp = dot(keys_ref[:count, :width], d, NT)
            prob = e * inverse
            cols = pl.ds(pl.multiple_of(p * 2 * rows, 2 * rows), 2 * rows)
            pt_ref[:count, cols] = prob.astype(jnp.bfloat16)
            ds_ref[:count, cols] = (prob * (dp - delta) * scale).astype(jnp.bfloat16)
            return carry

        lax.fori_loop(0, heads // 2, body, 0)

    def key_terms(first):
        q = qx_ref[...].reshape(heads * rows, wide)
        d = do_ref[...].reshape(heads * rows, width)
        picked = pl.ds(first, rows)
        lat = dot(ds_ref[picked], q[:, :width]) + dot(pt_ref[picked], d)
        rot = dot(ds_ref[picked], q[:, width:])
        for ref, part in ((c1_ref, slice(0, half)), (c2_ref, slice(half, rows))):
            place = slice(0, half) if first == 0 else slice(half, rows)
            ref[place, :width] = lat[part].astype(jnp.bfloat16)
            ref[place, width:] = rot[part].astype(jnp.bfloat16)

    @pl.when(rank >= HOPS - 1)
    def _():
        run(base)
        c1_ref[half:] = jnp.zeros_like(c1_ref[half:])
        c2_ref[half:] = jnp.zeros_like(c2_ref[half:])

    @pl.when(rank < HOPS - 1)
    def _():
        run(full)
        key_terms(base)

    key_terms(0)


def query_kernel(
    qx_ref, do_ref, ds_ref, pt_ref, own_ref, near_ref, far_ref, wk_ref,
    dnope_ref, drope_ref, grad_ref, keys_ref, dq_ref,
):
    rank = lax.axis_index("ctx")
    step = pl.program_id(0)
    rows, wide = own_ref.shape
    width = do_ref.shape[2]
    half = rows // 2
    base = 2 * rows

    @pl.when(step == 0)
    def _():
        keys_ref[:half] = near_ref[:half]
        keys_ref[half:rows] = far_ref[:half]
        keys_ref[rows:base] = own_ref[...]
        keys_ref[base : base + half] = near_ref[half:]
        keys_ref[base + half :] = far_ref[half:]
        grad_ref[...] = jnp.zeros_like(grad_ref)

    q = qx_ref[...].reshape(GROUP * rows, wide)
    d = do_ref[...].reshape(GROUP * rows, width)
    own = slice(rows, base)
    grad_ref[:, :width] += dot(ds_ref[own], q[:, :width]) + dot(pt_ref[own], d)
    grad_ref[:, width:] += dot(ds_ref[own], q[:, width:])
    dq_ref[...] = dot(ds_ref[:base], keys_ref[:base], TN)

    @pl.when(rank < HOPS - 1)
    def _():
        dq_ref[...] += dot(ds_ref[base:], keys_ref[base:], TN)

    lanes = lax.broadcasted_iota(jnp.int32, (rows, HEAD_WIDTH), 1)
    for g in range(GROUP):
        cols = slice(g * HEAD_WIDTH, (g + 1) * HEAD_WIDTH)
        mine = slice(g * rows, (g + 1) * rows)
        dnope_ref[:, cols] = dot(
            dq_ref[mine, :width].astype(jnp.bfloat16), wk_ref[:, cols]
        ).astype(jnp.bfloat16)
        if g % 2 == 1:
            before = slice((g - 1) * rows, g * rows)
            pair = jnp.where(lanes < HEAD_WIDTH // 2, dq_ref[before, width:], dq_ref[mine, width:])
            drope_ref[:, (g // 2) * HEAD_WIDTH : (g // 2 + 1) * HEAD_WIDTH] = pair.astype(jnp.bfloat16)


def sum_kernel(own_ref, a_ref, b_ref, out_ref):
    out_ref[...] = own_ref[...] + (a_ref[...].astype(jnp.float32) + b_ref[...].astype(jnp.float32))


def finish_kernel(mine_ref, other_ref, lat_ref, rot_ref):
    width = lat_ref.shape[1]
    narrow = rot_ref.shape[0]
    total = mine_ref[...] + other_ref[...]
    lat_ref[...] = total[:, :width]
    rot_ref[...] = jnp.transpose(total[:, width : width + narrow] + total[:, width + narrow :])


VMEM = pl.BlockSpec(memory_space=pltpu.VMEM)


def per_device(
    q_nope, q_rope, latent, k_rope, d_out, out_heads, lse_rest, key_up_weight, value_up_weight
):
    rows, width = latent.shape
    narrow = k_rope.shape[1]
    wide = width + 2 * narrow
    heads = key_up_weight.shape[1] // HEAD_WIDTH
    scale = (HEAD_WIDTH + narrow) ** (-0.5)
    bf16, f32 = jnp.bfloat16, jnp.float32
    steps = heads // GROUP

    own = pl.pallas_call(
        pack_kernel,
        out_shape=jax.ShapeDtypeStruct((rows, wide), bf16),
        in_specs=[VMEM, VMEM],
        out_specs=VMEM,
        compiler_params=params(4),
        name="pack",
    )(latent, jnp.transpose(k_rope))
    near = passed_along(own, "ctx", 1)
    far = passed_along(own, "ctx", 2)

    columns = pl.BlockSpec((rows, GROUP * HEAD_WIDTH), lambda i: (0, i))
    rotary = pl.BlockSpec((rows, GROUP * narrow), lambda i: (0, i))
    weights = pl.BlockSpec((width, GROUP * HEAD_WIDTH), lambda i: (0, i))
    q_block = pl.BlockSpec((GROUP, rows, wide), lambda i: (i, 0, 0))
    d_block = pl.BlockSpec((GROUP, rows, width), lambda i: (i, 0, 0))
    qx, do_lat, deltas = pl.pallas_call(
        project_kernel,
        grid=(steps,),
        out_shape=(
            pltpu.VMEM((heads, rows, wide), bf16),
            pltpu.VMEM((heads, rows, width), bf16),
            pltpu.VMEM((heads, 1, rows), f32),
        ),
        in_specs=[columns, rotary, columns, columns, weights, weights],
        out_specs=[q_block, d_block, pl.BlockSpec((GROUP, 1, rows), lambda i: (i, 0, 0))],
        compiler_params=params(16),
        cost_estimate=cost(4 * rows * heads * HEAD_WIDTH * width, 12 * MIB),
        name="project",
    )(q_nope, q_rope, d_out, out_heads, key_up_weight, value_up_weight)

    total = heads * rows
    d_s, p_t, c_near, c_far = pl.pallas_call(
        functools.partial(scores_kernel, scale),
        out_shape=(
            pltpu.VMEM((3 * rows, total), bf16),
            pltpu.VMEM((3 * rows, total), bf16),
            jax.ShapeDtypeStruct((rows, wide), bf16),
            jax.ShapeDtypeStruct((rows, wide), bf16),
        ),
        in_specs=[VMEM] * 7,
        out_specs=[VMEM] * 4,
        scratch_shapes=[pltpu.VMEM((3 * rows, wide), bf16), pltpu.VMEM((3 * rows, rows), f32)],
        compiler_params=params(24),
        cost_estimate=cost(8 * total * rows * width, 16 * MIB),
        name="scores",
    )(qx, do_lat, deltas, jnp.transpose(lse_rest), own, near, far)
    from_near = passed_along(c_near, "ctx", -1)
    from_far = passed_along(c_far, "ctx", -2)

    whole = pl.BlockSpec((rows, wide), lambda i: (0, 0))
    across = pl.BlockSpec((3 * rows, GROUP * rows), lambda i: (0, i))
    d_q_nope, d_q_rope, grad = pl.pallas_call(
        query_kernel,
        grid=(steps,),
        out_shape=(
            jax.ShapeDtypeStruct((rows, heads * HEAD_WIDTH), bf16),
            jax.ShapeDtypeStruct((rows, heads * narrow), bf16),
            jax.ShapeDtypeStruct((rows, wide), f32),
        ),
        in_specs=[q_block, d_block, across, across, whole, whole, whole, weights],
        out_specs=[columns, rotary, whole],
        scratch_shapes=[
            pltpu.VMEM((3 * rows, wide), bf16),
            pltpu.VMEM((GROUP * rows, wide), f32),
        ],
        compiler_params=params(16),
        cost_estimate=cost(10 * total * rows * width, 16 * MIB),
        name="query",
    )(qx, do_lat, d_s, p_t, own, near, far, key_up_weight)

    partial = pl.pallas_call(
        sum_kernel,
        out_shape=jax.ShapeDtypeStruct((rows, wide), f32),
        in_specs=[VMEM] * 3,
        out_specs=VMEM,
        compiler_params=params(4),
        name="gather",
    )(grad, from_near, from_far)

    sharers = lax.axis_size("head")
    distance = 1
    while 2 * distance < sharers:
        partial = partial + lax.ppermute(
            partial, "head", [(i, i ^ distance) for i in range(sharers)]
        )
        distance *= 2
    other = lax.ppermute(partial, "head", [(i, i ^ distance) for i in range(sharers)])
    latent_gradient, d_k_rope = pl.pallas_call(
        finish_kernel,
        out_shape=(
            jax.ShapeDtypeStruct((rows, width), f32),
            jax.ShapeDtypeStruct((narrow, rows), f32),
        ),
        in_specs=[VMEM] * 2,
        out_specs=[VMEM] * 2,
        compiler_params=params(4),
        name="finish",
    )(partial, other)
    return d_q_nope, d_q_rope, latent_gradient, jnp.transpose(d_k_rope)


def solution(mesh):
    placed = (
        P("ctx", "head"),
        P("ctx", "head"),
        P("ctx", None),
        P("ctx", None),
        P("ctx", "head"),
        P("ctx", "head"),
        P("ctx", "head"),
        P(None, "head"),
        P(None, "head"),
    )
    return jax.shard_map(
        per_device,
        mesh=mesh,
        in_specs=placed,
        out_specs=(P("ctx", "head"), P("ctx", "head"), P("ctx", None), P("ctx", None)),
        check_vma=False,
    )
```

```python
import functools

import jax
import jax.numpy as jnp
from jax import lax
from jax.experimental import pallas as pl
from jax.experimental.pallas import tpu as pltpu
from jax.sharding import PartitionSpec as P

HEAD_WIDTH = 128
HOPS = 3
GROUP = 4
MIB = 1 << 20

NT = (((1,), (1,)), ((), ()))
TN = (((0,), (0,)), ((), ()))


def dot(a, b, dims=(((1,), (0,)), ((), ()))):
    return lax.dot_general(a, b, dims, preferred_element_type=jnp.float32)


def passed_along(block, axis, distance):
    count = lax.axis_size(axis)
    return lax.ppermute(block, axis, [((i - distance) % count, i) for i in range(count)])


def params(limit_mib, **extra):
    return pltpu.CompilerParams(vmem_limit_bytes=limit_mib * MIB, **extra)


def cost(flops, moved):
    return pl.CostEstimate(flops=int(flops), bytes_accessed=int(moved), transcendentals=0)


def pack_kernel(lat_ref, rot_ref, out_ref):
    width = lat_ref.shape[1]
    rot = jnp.transpose(rot_ref[...].astype(jnp.float32)).astype(out_ref.dtype)
    out_ref[:, :width] = lat_ref[...]
    out_ref[:, width:] = jnp.concatenate([rot, rot], axis=1)


def project_kernel(nope_ref, rope_ref, dout_ref, saved_ref, wk_ref, wv_ref, qx_ref, do_ref, delta_ref):
    rows = nope_ref.shape[0]
    width = wk_ref.shape[0]
    lanes = lax.broadcasted_iota(jnp.int32, (rows, HEAD_WIDTH), 1)
    ones = jnp.ones((8, HEAD_WIDTH), jnp.bfloat16)
    for g in range(GROUP):
        cols = slice(g * HEAD_WIDTH, (g + 1) * HEAD_WIDTH)
        d_out = dout_ref[:, cols]
        qx_ref[g, :, :width] = dot(nope_ref[:, cols], wk_ref[:, cols], NT).astype(jnp.bfloat16)
        do_ref[g] = dot(d_out, wv_ref[:, cols], NT).astype(jnp.bfloat16)
        prod = d_out.astype(jnp.float32) * saved_ref[:, cols].astype(jnp.float32)
        high = prod.astype(jnp.bfloat16)
        low = (prod - high.astype(jnp.float32)).astype(jnp.bfloat16)
        delta_ref[g] = (dot(ones, high, NT) + dot(ones, low, NT))[0:1]
        pair = rope_ref[:, (g // 2) * HEAD_WIDTH : (g // 2 + 1) * HEAD_WIDTH]
        mine = (lanes < HEAD_WIDTH // 2) if g % 2 == 0 else (lanes >= HEAD_WIDTH // 2)
        qx_ref[g, :, width:] = jnp.where(mine, pair, jnp.zeros_like(pair))


def place_keys(keys_ref, own_ref, near_ref, far_ref):
    rows = own_ref.shape[0]
    half = rows // 2
    keys_ref[:rows] = own_ref[...]
    keys_ref[rows : rows + half] = near_ref[:half]
    keys_ref[rows + half : 2 * rows] = far_ref[:half]
    keys_ref[2 * rows : 2 * rows + half] = near_ref[half:]
    keys_ref[2 * rows + half :] = far_ref[half:]


def scores_kernel(
    scale, qx_ref, do_ref, delta_ref, rest_ref, own_ref, near_ref, far_ref,
    ds_ref, pt_ref, c1_ref, c2_ref, keys_ref, bias_ref,
):
    rank = lax.axis_index("ctx")
    heads, rows, wide = qx_ref.shape
    width = do_ref.shape[2]
    half = rows // 2
    base = 2 * rows
    full = 3 * rows
    place_keys(keys_ref, own_ref, near_ref, far_ref)
    row = lax.broadcasted_iota(jnp.int32, (rows, rows), 0)
    col = lax.broadcasted_iota(jnp.int32, (rows, rows), 1)
    late = col >= half
    wrapped = jnp.where(row < half, rank, rank - 1) < 1
    off = jnp.float32(-jnp.inf)
    bias_ref[:rows] = jnp.where(row <= col, 0.0, off)
    bias_ref[rows:base] = jnp.where(jnp.logical_or(late, jnp.logical_not(wrapped)), 0.0, off)
    bias_ref[base:] = jnp.where(jnp.logical_and(late, wrapped), 0.0, off)

    def run(count):
        def body(p, carry):
            q = qx_ref[pl.ds(2 * p, 2)].reshape(2 * rows, wide)
            d = do_ref[pl.ds(2 * p, 2)].reshape(2 * rows, width)
            bias = bias_ref[:count]
            rest = jnp.concatenate([rest_ref[pl.ds(2 * p, 1)], rest_ref[pl.ds(2 * p + 1, 1)]], axis=1)
            delta = jnp.concatenate([delta_ref[2 * p], delta_ref[2 * p + 1]], axis=1)
            s = dot(keys_ref[:count], q, NT) * scale + jnp.concatenate([bias, bias], axis=1)
            top = jnp.maximum(jnp.max(s, axis=0, keepdims=True), rest)
            e = jnp.exp(s - top)
            total = jnp.sum(e, axis=0, keepdims=True) + jnp.exp(rest - top)
            inverse = 1.0 / total
            dp = dot(keys_ref[:count, :width], d, NT)
            prob = e * inverse
            cols = pl.ds(pl.multiple_of(p * 2 * rows, 2 * rows), 2 * rows)
            pt_ref[:count, cols] = prob.astype(jnp.bfloat16)
            ds_ref[:count, cols] = (prob * (dp - delta) * scale).astype(jnp.bfloat16)
            return carry

        lax.fori_loop(0, heads // 2, body, 0, unroll=2)

    def key_terms(count):
        q = qx_ref[...].reshape(heads * rows, wide)
        d = do_ref[...].reshape(heads * rows, width)
        picked = pl.ds(rows, count)
        lat = (dot(ds_ref[picked], q[:, :width]) + dot(pt_ref[picked], d)).astype(jnp.bfloat16)
        rot = dot(ds_ref[picked], q[:, width:]).astype(jnp.bfloat16)
        for at in range(0, count, rows):
            place = slice(at // 2, at // 2 + half)
            for ref, start in ((c1_ref, at), (c2_ref, at + half)):
                ref[place, :width] = lat[start : start + half]
                ref[place, width:] = rot[start : start + half]

    @pl.when(rank >= HOPS - 1)
    def _():
        run(base)
        key_terms(rows)
        c1_ref[half:] = jnp.zeros_like(c1_ref[half:])
        c2_ref[half:] = jnp.zeros_like(c2_ref[half:])

    @pl.when(rank < HOPS - 1)
    def _():
        run(full)
        key_terms(base)


def query_kernel(
    qx_ref, do_ref, ds_ref, pt_ref, own_ref, near_ref, far_ref, wk_ref,
    dnope_ref, drope_ref, grad_ref, keys_ref, dq_ref,
):
    rank = lax.axis_index("ctx")
    step = pl.program_id(0)
    rows, wide = own_ref.shape
    width = do_ref.shape[2]
    half = rows // 2
    base = 2 * rows

    @pl.when(step == 0)
    def _():
        place_keys(keys_ref, own_ref, near_ref, far_ref)
        grad_ref[...] = jnp.zeros_like(grad_ref)

    q = qx_ref[...].reshape(GROUP * rows, wide)
    d = do_ref[...].reshape(GROUP * rows, width)
    own = slice(0, rows)
    grad_ref[:, :width] += dot(ds_ref[own], q[:, :width]) + dot(pt_ref[own], d)
    grad_ref[:, width:] += dot(ds_ref[own], q[:, width:])
    dq_ref[...] = dot(ds_ref[:base], keys_ref[:base], TN)

    @pl.when(rank < HOPS - 1)
    def _():
        for g in range(GROUP):
            late = slice(g * rows + half, (g + 1) * rows)
            more = jnp.transpose(ds_ref[base:, g * rows : (g + 1) * rows])[half:]
            dq_ref[late] += dot(more, keys_ref[base:])

    lanes = lax.broadcasted_iota(jnp.int32, (rows, HEAD_WIDTH), 1)
    for g in range(GROUP):
        cols = slice(g * HEAD_WIDTH, (g + 1) * HEAD_WIDTH)
        mine = slice(g * rows, (g + 1) * rows)
        dnope_ref[:, cols] = dot(
            dq_ref[mine, :width].astype(jnp.bfloat16), wk_ref[:, cols]
        ).astype(jnp.bfloat16)
        if g % 2 == 1:
            before = slice((g - 1) * rows, g * rows)
            pair = jnp.where(lanes < HEAD_WIDTH // 2, dq_ref[before, width:], dq_ref[mine, width:])
            drope_ref[:, (g // 2) * HEAD_WIDTH : (g // 2 + 1) * HEAD_WIDTH] = pair.astype(jnp.bfloat16)


def sum_kernel(own_ref, a_ref, b_ref, out_ref):
    out_ref[...] = own_ref[...] + (a_ref[...].astype(jnp.float32) + b_ref[...].astype(jnp.float32))


def finish_kernel(mine_ref, other_ref, lat_ref, rot_ref):
    width = lat_ref.shape[1]
    narrow = rot_ref.shape[0]
    total = mine_ref[...] + other_ref[...]
    lat_ref[...] = total[:, :width]
    rot_ref[...] = jnp.transpose(total[:, width : width + narrow] + total[:, width + narrow :])


VMEM = pl.BlockSpec(memory_space=pltpu.VMEM)


def per_device(
    q_nope, q_rope, latent, k_rope, d_out, out_heads, lse_rest, key_up_weight, value_up_weight
):
    rows, width = latent.shape
    narrow = k_rope.shape[1]
    wide = width + 2 * narrow
    heads = key_up_weight.shape[1] // HEAD_WIDTH
    scale = (HEAD_WIDTH + narrow) ** (-0.5)
    bf16, f32 = jnp.bfloat16, jnp.float32
    steps = heads // GROUP

    q_nope, q_rope, latent, d_out, out_heads, key_up_weight, value_up_weight = (
        pltpu.with_memory_space_constraint(array, pltpu.HBM)
        for array in (q_nope, q_rope, latent, d_out, out_heads, key_up_weight, value_up_weight)
    )
    own = pl.pallas_call(
        pack_kernel,
        out_shape=jax.ShapeDtypeStruct((rows, wide), bf16),
        in_specs=[VMEM, VMEM],
        out_specs=VMEM,
        compiler_params=params(4),
        name="pack",
    )(latent, pltpu.with_memory_space_constraint(jnp.transpose(k_rope), pltpu.HBM))
    near = passed_along(own, "ctx", 1)
    far = passed_along(own, "ctx", 2)

    columns = pl.BlockSpec((rows, GROUP * HEAD_WIDTH), lambda i: (0, i))
    rotary = pl.BlockSpec((rows, GROUP * narrow), lambda i: (0, i))
    weights = pl.BlockSpec((width, GROUP * HEAD_WIDTH), lambda i: (0, i))
    q_block = pl.BlockSpec((GROUP, rows, wide), lambda i: (i, 0, 0))
    d_block = pl.BlockSpec((GROUP, rows, width), lambda i: (i, 0, 0))
    qx, do_lat, deltas = pl.pallas_call(
        project_kernel,
        grid=(steps,),
        out_shape=(
            pltpu.VMEM((heads, rows, wide), bf16),
            pltpu.VMEM((heads, rows, width), bf16),
            pltpu.VMEM((heads, 1, rows), f32),
        ),
        in_specs=[columns, rotary, columns, columns, weights, weights],
        out_specs=[q_block, d_block, pl.BlockSpec((GROUP, 1, rows), lambda i: (i, 0, 0))],
        compiler_params=params(16),
        cost_estimate=cost(4 * rows * heads * HEAD_WIDTH * width, 12 * MIB),
        name="project",
    )(q_nope, q_rope, d_out, out_heads, key_up_weight, value_up_weight)

    total = heads * rows
    d_s, p_t, c_near, c_far = pl.pallas_call(
        functools.partial(scores_kernel, scale),
        out_shape=(
            pltpu.VMEM((3 * rows, total), bf16),
            pltpu.VMEM((3 * rows, total), bf16),
            jax.ShapeDtypeStruct((rows, wide), bf16),
            jax.ShapeDtypeStruct((rows, wide), bf16),
        ),
        in_specs=[VMEM] * 7,
        out_specs=[VMEM] * 4,
        scratch_shapes=[pltpu.VMEM((3 * rows, wide), bf16), pltpu.VMEM((3 * rows, rows), f32)],
        compiler_params=params(24),
        cost_estimate=cost(8 * total * rows * width, 16 * MIB),
        name="scores",
    )(qx, do_lat, deltas, jnp.transpose(lse_rest), own, near, far)
    from_near = passed_along(c_near, "ctx", -1)
    from_far = passed_along(c_far, "ctx", -2)

    whole = pl.BlockSpec((rows, wide), lambda i: (0, 0))
    across = pl.BlockSpec((3 * rows, GROUP * rows), lambda i: (0, i))
    d_q_nope, d_q_rope, grad = pl.pallas_call(
        query_kernel,
        grid=(steps,),
        out_shape=(
            jax.ShapeDtypeStruct((rows, heads * HEAD_WIDTH), bf16),
            jax.ShapeDtypeStruct((rows, heads * narrow), bf16),
            jax.ShapeDtypeStruct((rows, wide), f32),
        ),
        in_specs=[q_block, d_block, across, across, whole, whole, whole, weights],
        out_specs=[columns, rotary, whole],
        scratch_shapes=[
            pltpu.VMEM((3 * rows, wide), bf16),
            pltpu.VMEM((GROUP * rows, wide), f32),
        ],
        compiler_params=params(16),
        cost_estimate=cost(10 * total * rows * width, 16 * MIB),
        name="query",
    )(qx, do_lat, d_s, p_t, own, near, far, key_up_weight)

    partial = pl.pallas_call(
        sum_kernel,
        out_shape=jax.ShapeDtypeStruct((rows, wide), f32),
        in_specs=[VMEM] * 3,
        out_specs=VMEM,
        compiler_params=params(4),
        name="gather",
    )(grad, from_near, from_far)

    sharers = lax.axis_size("head")
    distance = 1
    while 2 * distance < sharers:
        partial = partial + lax.ppermute(
            partial, "head", [(i, i ^ distance) for i in range(sharers)]
        )
        distance *= 2
    other = lax.ppermute(partial, "head", [(i, i ^ distance) for i in range(sharers)])
    latent_gradient, d_k_rope = pl.pallas_call(
        finish_kernel,
        out_shape=(
            jax.ShapeDtypeStruct((rows, width), f32),
            jax.ShapeDtypeStruct((narrow, rows), f32),
        ),
        in_specs=[VMEM] * 2,
        out_specs=[VMEM] * 2,
        compiler_params=params(4),
        name="finish",
    )(partial, other)
    return d_q_nope, d_q_rope, latent_gradient, jnp.transpose(d_k_rope)


def solution(mesh):
    placed = (
        P("ctx", "head"),
        P("ctx", "head"),
        P("ctx", None),
        P("ctx", None),
        P("ctx", "head"),
        P("ctx", "head"),
        P("ctx", "head"),
        P(None, "head"),
        P(None, "head"),
    )
    return jax.shard_map(
        per_device,
        mesh=mesh,
        in_specs=placed,
        out_specs=(P("ctx", "head"), P("ctx", "head"), P("ctx", None), P("ctx", None)),
        check_vma=False,
    )
```

```python
import functools

import jax
import jax.numpy as jnp
from jax import lax
from jax.experimental import pallas as pl
from jax.experimental.pallas import tpu as pltpu
from jax.sharding import PartitionSpec as P

HEAD_WIDTH = 128
HOPS = 3
GROUP = 4
MIB = 1 << 20

NT = (((1,), (1,)), ((), ()))
TN = (((0,), (0,)), ((), ()))


def dot(a, b, dims=(((1,), (0,)), ((), ()))):
    return lax.dot_general(a, b, dims, preferred_element_type=jnp.float32)


def passed_along(block, axis, distance):
    count = lax.axis_size(axis)
    return lax.ppermute(block, axis, [((i - distance) % count, i) for i in range(count)])


def params(limit_mib):
    return pltpu.CompilerParams(vmem_limit_bytes=limit_mib * MIB)


def cost(flops, moved):
    return pl.CostEstimate(flops=int(flops), bytes_accessed=int(moved), transcendentals=0)


def pack_kernel(lat_ref, rot_ref, out_ref):
    width = lat_ref.shape[1]
    rot = jnp.transpose(rot_ref[...].astype(jnp.float32)).astype(out_ref.dtype)
    out_ref[:, :width] = lat_ref[...]
    out_ref[:, width:] = jnp.concatenate([rot, rot], axis=1)


def project_kernel(
    nope_hbm, rope_hbm, dout_hbm, saved_hbm, wk_hbm, wv_hbm, rest_ref,
    qx_ref, do_ref, stats_ref, columns_ref, flat_ref,
):
    rows = nope_hbm.shape[0]
    width, total = wk_hbm.shape
    heads = total // HEAD_WIDTH
    half = rows // 2
    lanes = lax.broadcasted_iota(jnp.int32, (rows, HEAD_WIDTH), 1)
    columns_ref[...] = jnp.zeros_like(columns_ref)

    def body(nope, rope, dout, saved, wk, wv):
        quad = pl.program_id(0)
        found = columns_ref[...]
        for g in range(GROUP):
            cols = slice(g * HEAD_WIDTH, (g + 1) * HEAD_WIDTH)
            place = slice(g * half, (g + 1) * half)
            d_out = dout[:, cols]
            q_abs = dot(nope[:, cols], wk[:, cols], NT).astype(jnp.bfloat16)
            d_lat = dot(d_out, wv[:, cols], NT).astype(jnp.bfloat16)
            pair = rope[:, (g // 2) * HEAD_WIDTH : (g // 2 + 1) * HEAD_WIDTH]
            mine = (lanes < HEAD_WIDTH // 2) if g % 2 == 0 else (lanes >= HEAD_WIDTH // 2)
            pair = jnp.where(mine, pair, jnp.zeros_like(pair))
            for late, part in ((0, slice(0, half)), (1, slice(half, rows))):
                qx_ref[late, quad, place, :width] = q_abs[part]
                qx_ref[late, quad, place, width:] = pair[part]
                do_ref[late, quad, place] = d_lat[part]
            prod = d_out.astype(jnp.float32) * saved[:, cols].astype(jnp.float32)
            delta = jnp.sum(prod, axis=1, keepdims=True)
            found = jnp.where(lanes == GROUP * quad + g, delta, found)
        columns_ref[...] = found

    wide_block = pl.BlockSpec((rows, GROUP * HEAD_WIDTH), lambda i: (0, i))
    rope_block = pl.BlockSpec((rows, GROUP * HEAD_WIDTH // 2), lambda i: (0, i))
    weight_block = pl.BlockSpec((width, GROUP * HEAD_WIDTH), lambda i: (0, i))
    pltpu.emit_pipeline(
        body,
        grid=(heads // GROUP,),
        in_specs=[wide_block, rope_block, wide_block, wide_block, weight_block, weight_block],
    )(nope_hbm, rope_hbm, dout_hbm, saved_hbm, wk_hbm, wv_hbm)

    flat_ref[0, :heads] = rest_ref[...]
    flat_ref[1] = jnp.transpose(columns_ref[...])
    low = lax.broadcasted_iota(jnp.int32, (heads // 2, rows), 1) < half
    for kind in range(2):
        even = flat_ref[kind, pl.ds(0, heads // 2, 2), :]
        odd = flat_ref[kind, pl.ds(1, heads // 2, 2), :]
        stats_ref[2 * kind] = jnp.where(low, even, pltpu.roll(odd, half, 1))
        stats_ref[2 * kind + 1] = jnp.where(low, pltpu.roll(even, half, 1), odd)


def place_keys(keys_ref, own_ref, near_ref, far_ref):
    rows = own_ref.shape[0]
    half = rows // 2
    parts = (
        (own_ref, half), (own_ref, 0), (near_ref, 0), (far_ref, 0), (near_ref, half), (far_ref, half),
    )
    for at, (ref, start) in enumerate(parts):
        keys_ref[at * half : (at + 1) * half] = ref[start : start + half]


def scores_kernel(
    scale, qx_ref, do_ref, stats_ref, own_ref, near_ref, far_ref,
    dsl_ref, dse_ref, ptl_ref, pte_ref, c1_ref, c2_ref, keys_ref, bias_ref,
):
    rank = lax.axis_index("ctx")
    quads, span, wide = qx_ref.shape[1:]
    width = do_ref.shape[3]
    rows = own_ref.shape[0]
    half = rows // 2
    place_keys(keys_ref, own_ref, near_ref, far_ref)
    off = jnp.float32(-jnp.inf)
    row = lax.broadcasted_iota(jnp.int32, (half, rows), 0)
    col = lax.broadcasted_iota(jnp.int32, (half, rows), 1) % half
    causal = jnp.where(row <= col, 0.0, off)
    open_ = jnp.zeros((half, rows), jnp.float32)
    bias_ref[1, :half] = causal
    bias_ref[1, half:rows] = open_
    bias_ref[0, half:rows] = causal
    for d in range(1, HOPS):
        first = slice(rows + (d - 1) * half, rows + d * half)
        second = slice(2 * rows + (d - 1) * half, 2 * rows + d * half)
        bias_ref[0, first] = jnp.where(rank < d, off, open_)
        bias_ref[1, first] = open_
        bias_ref[1, second] = jnp.where(rank < d, open_, off)

    def part(late, quad, count, ds_ref, pt_ref):
        start = half * (1 - late)
        seen = slice(start, start + count)
        q = qx_ref[late, quad]
        d = do_ref[late, quad]
        bias = bias_ref[late, seen]

        def lane_row(kind):
            pieces = [stats_ref[2 * kind + late, pl.ds(2 * quad + i, 1)] for i in range(2)]
            return jnp.concatenate(pieces, axis=1)

        rest = lane_row(0)
        delta = lane_row(1)
        s = dot(keys_ref[seen], q, NT) * scale + jnp.concatenate([bias, bias], axis=1)
        dp = dot(keys_ref[seen, :width], d, NT)
        top = jnp.maximum(jnp.max(s, axis=0, keepdims=True), rest)
        e = jnp.exp(s - top)
        inverse = 1.0 / (jnp.sum(e, axis=0, keepdims=True) + jnp.exp(rest - top))
        prob = e * inverse
        cols = pl.ds(pl.multiple_of(quad * span, span), span)
        pt_ref[:count, cols] = prob.astype(jnp.bfloat16)
        ds_ref[:count, cols] = (prob * (dp - delta) * scale).astype(jnp.bfloat16)

    def run(late_count, early_count):
        def body(quad, carry):
            part(1, quad, late_count, dsl_ref, ptl_ref)
            part(0, quad, early_count, dse_ref, pte_ref)
            return carry

        lax.fori_loop(0, quads, body, 0, unroll=UNROLL)

    def terms(late, picked, ds_ref, pt_ref):
        q = qx_ref[late].reshape(quads * span, wide)
        d = do_ref[late].reshape(quads * span, width)
        lat = dot(ds_ref[picked], q[:, :width]) + dot(pt_ref[picked], d)
        return lat, dot(ds_ref[picked], q[:, width:])

    def put(at, lat, rot):
        for i, ref in ((0, c1_ref), (1, c2_ref)):
            ref[at : at + half, :width] = lat[i * half : (i + 1) * half].astype(jnp.bfloat16)
            ref[at : at + half, width:] = rot[i * half : (i + 1) * half].astype(jnp.bfloat16)

    @pl.when(rank >= HOPS - 1)
    def _():
        run(2 * rows, rows + half)
        late = terms(1, pl.ds(rows, rows), dsl_ref, ptl_ref)
        early = terms(0, pl.ds(half, rows), dse_ref, pte_ref)
        put(0, late[0] + early[0], late[1] + early[1])
        for ref in (c1_ref, c2_ref):
            ref[half:] = jnp.zeros_like(ref[half:])

    @pl.when(jnp.logical_and(rank > 0, rank < HOPS - 1))
    def _():
        run(3 * rows, rows + half)
        late = terms(1, pl.ds(rows, 2 * rows), dsl_ref, ptl_ref)
        early = terms(0, pl.ds(half, rows), dse_ref, pte_ref)
        put(0, late[0][:rows] + early[0], late[1][:rows] + early[1])
        put(half, late[0][rows:], late[1][rows:])

    @pl.when(rank == 0)
    def _():
        dse_ref[half:] = jnp.zeros_like(dse_ref[half:])
        run(3 * rows, half)
        late = terms(1, pl.ds(rows, 2 * rows), dsl_ref, ptl_ref)
        put(0, late[0][:rows], late[1][:rows])
        put(half, late[0][rows:], late[1][rows:])


def query_kernel(
    qx_ref, do_ref, dsl_ref, dse_ref, ptl_ref, pte_ref, own_ref, near_ref, far_ref, wk_ref,
    dnope_hbm, drope_hbm, grad_ref, keys_ref, dq_ref,
):
    rank = lax.axis_index("ctx")
    quads, span, wide = qx_ref.shape[1:]
    width = do_ref.shape[3]
    rows = own_ref.shape[0]
    half = rows // 2
    lanes = lax.broadcasted_iota(jnp.int32, (rows, HEAD_WIDTH), 1)
    place_keys(keys_ref, own_ref, near_ref, far_ref)

    def terms(late, count, ds_ref, pt_ref):
        q = qx_ref[late].reshape(quads * span, wide)
        d = do_ref[late].reshape(quads * span, width)
        lat = dot(ds_ref[:count], q[:, :width]) + dot(pt_ref[:count], d)
        return lat, dot(ds_ref[:count], q[:, width:])

    late_terms = terms(1, rows, dsl_ref, ptl_ref)
    early_terms = terms(0, half, dse_ref, pte_ref)
    for place, late, early in zip((slice(0, width), slice(width, wide)), late_terms, early_terms):
        grad_ref[:half, place] = late[half:] + early
        grad_ref[half:, place] = late[:half]

    def body(dnope, drope):
        quad = pl.program_id(0)
        cols = pl.ds(pl.multiple_of(quad * span, span), span)
        dq_ref[1] = dot(dsl_ref[: 2 * rows, cols], keys_ref[: 2 * rows], TN)
        dq_ref[0] = dot(dse_ref[:, cols], keys_ref[half : 2 * rows], TN)

        @pl.when(rank < HOPS - 1)
        def _():
            dq_ref[1] += dot(dsl_ref[2 * rows :, cols], keys_ref[2 * rows :], TN)

        def head(g, place):
            mine = slice(g * half, (g + 1) * half)
            return jnp.concatenate([dq_ref[0, mine, place], dq_ref[1, mine, place]], axis=0)

        for g in range(GROUP):
            out = slice(g * HEAD_WIDTH, (g + 1) * HEAD_WIDTH)
            taken = pl.ds(pl.multiple_of((quad * GROUP + g) * HEAD_WIDTH, HEAD_WIDTH), HEAD_WIDTH)
            dq_abs = head(g, slice(0, width)).astype(jnp.bfloat16)
            dnope[:, out] = dot(dq_abs, wk_ref[:, taken]).astype(jnp.bfloat16)
            if g % 2 == 1:
                both = slice(width, wide)
                pair = jnp.where(lanes < HEAD_WIDTH // 2, head(g - 1, both), head(g, both))
                drope[:, (g // 2) * HEAD_WIDTH : (g // 2 + 1) * HEAD_WIDTH] = pair.astype(jnp.bfloat16)

    pltpu.emit_pipeline(
        body,
        grid=(quads,),
        out_specs=[
            pl.BlockSpec((rows, GROUP * HEAD_WIDTH), lambda i: (0, i)),
            pl.BlockSpec((rows, GROUP * HEAD_WIDTH // 2), lambda i: (0, i)),
        ],
    )(dnope_hbm, drope_hbm)


def sum_kernel(own_ref, a_ref, b_ref, out_ref):
    out_ref[...] = own_ref[...] + (a_ref[...].astype(jnp.float32) + b_ref[...].astype(jnp.float32))


def finish_kernel(mine_ref, other_ref, lat_ref, rot_ref):
    width = lat_ref.shape[1]
    narrow = rot_ref.shape[0]
    total = mine_ref[...] + other_ref[...]
    lat_ref[...] = total[:, :width]
    rot_ref[...] = jnp.transpose(total[:, width : width + narrow] + total[:, width + narrow :])


UNROLL = 2
VMEM = pl.BlockSpec(memory_space=pltpu.VMEM)
HBM = pl.BlockSpec(memory_space=pltpu.HBM)


def in_hbm(*arrays):
    return [pltpu.with_memory_space_constraint(array, pltpu.HBM) for array in arrays]


def per_device(
    q_nope, q_rope, latent, k_rope, d_out, out_heads, lse_rest, key_up_weight, value_up_weight
):
    rows, width = latent.shape
    narrow = k_rope.shape[1]
    wide = width + 2 * narrow
    half = rows // 2
    heads = key_up_weight.shape[1] // HEAD_WIDTH
    quads, span = heads // GROUP, GROUP * half
    scale = (HEAD_WIDTH + narrow) ** (-0.5)
    bf16, f32 = jnp.bfloat16, jnp.float32
    total = heads * rows

    own = pl.pallas_call(
        pack_kernel,
        out_shape=jax.ShapeDtypeStruct((rows, wide), bf16),
        in_specs=[VMEM, VMEM],
        out_specs=VMEM,
        compiler_params=params(4),
        name="pack",
    )(*in_hbm(latent, jnp.transpose(k_rope)))
    near = passed_along(own, "ctx", 1)
    far = passed_along(own, "ctx", 2)

    qx, do_lat, stats = pl.pallas_call(
        project_kernel,
        out_shape=(
            pltpu.VMEM((2, quads, span, wide), bf16),
            pltpu.VMEM((2, quads, span, width), bf16),
            pltpu.VMEM((4, heads // 2, rows), f32),
        ),
        in_specs=[HBM] * 6 + [VMEM],
        out_specs=[VMEM] * 3,
        scratch_shapes=[
            pltpu.VMEM((rows, HEAD_WIDTH), f32),
            pltpu.VMEM((2, HEAD_WIDTH, rows), f32),
        ],
        compiler_params=params(16),
        cost_estimate=cost(4 * total * HEAD_WIDTH * width, 12 * MIB),
        name="project",
    )(
        *in_hbm(q_nope, q_rope, d_out, out_heads, key_up_weight, value_up_weight),
        jnp.transpose(lse_rest),
    )

    late = pltpu.VMEM((3 * rows, quads * span), bf16)
    early = pltpu.VMEM((rows + half, quads * span), bf16)
    *terms, c_near, c_far = pl.pallas_call(
        functools.partial(scores_kernel, scale),
        out_shape=(late, early, late, early) + (jax.ShapeDtypeStruct((rows, wide), bf16),) * 2,
        in_specs=[VMEM] * 6,
        out_specs=[VMEM] * 6,
        scratch_shapes=[
            pltpu.VMEM((3 * rows, wide), bf16),
            pltpu.VMEM((2, 3 * rows, rows), f32),
        ],
        compiler_params=params(24),
        cost_estimate=cost(8 * total * rows * width, 16 * MIB),
        name="scores",
    )(qx, do_lat, stats, own, near, far)
    from_near = passed_along(c_near, "ctx", -1)
    from_far = passed_along(c_far, "ctx", -2)

    d_q_nope, d_q_rope, grad = pl.pallas_call(
        query_kernel,
        out_shape=(
            jax.ShapeDtypeStruct((rows, heads * HEAD_WIDTH), bf16),
            jax.ShapeDtypeStruct((rows, heads * narrow), bf16),
            jax.ShapeDtypeStruct((rows, wide), f32),
        ),
        in_specs=[VMEM] * 10,
        out_specs=[HBM, HBM, VMEM],
        scratch_shapes=[
            pltpu.VMEM((3 * rows, wide), bf16),
            pltpu.VMEM((2, span, wide), f32),
        ],
        compiler_params=params(16),
        cost_estimate=cost(10 * total * rows * width, 16 * MIB),
        name="query",
    )(qx, do_lat, *terms, own, near, far, key_up_weight)

    partial = pl.pallas_call(
        sum_kernel,
        out_shape=jax.ShapeDtypeStruct((rows, wide), f32),
        in_specs=[VMEM] * 3,
        out_specs=VMEM,
        compiler_params=params(4),
        name="gather",
    )(grad, from_near, from_far)

    sharers = lax.axis_size("head")
    distance = 1
    while 2 * distance < sharers:
        partial = partial + lax.ppermute(
            partial, "head", [(i, i ^ distance) for i in range(sharers)]
        )
        distance *= 2
    other = lax.ppermute(partial, "head", [(i, i ^ distance) for i in range(sharers)])
    latent_gradient, d_k_rope = pl.pallas_call(
        finish_kernel,
        out_shape=(
            jax.ShapeDtypeStruct((rows, width), f32),
            jax.ShapeDtypeStruct((narrow, rows), f32),
        ),
        in_specs=[VMEM] * 2,
        out_specs=[VMEM] * 2,
        compiler_params=params(4),
        name="finish",
    )(partial, other)
    return d_q_nope, d_q_rope, latent_gradient, jnp.transpose(d_k_rope)


def solution(mesh):
    placed = (
        P("ctx", "head"),
        P("ctx", "head"),
        P("ctx", None),
        P("ctx", None),
        P("ctx", "head"),
        P("ctx", "head"),
        P("ctx", "head"),
        P(None, "head"),
        P(None, "head"),
    )
    return jax.shard_map(
        per_device,
        mesh=mesh,
        in_specs=placed,
        out_specs=(P("ctx", "head"), P("ctx", "head"), P("ctx", None), P("ctx", None)),
        check_vma=False,
    )
```

```python
import functools

import jax
import jax.numpy as jnp
from jax import lax
from jax.experimental import pallas as pl
from jax.experimental.pallas import tpu as pltpu
from jax.sharding import PartitionSpec as P

HEAD_WIDTH = 128
HOPS = 3
GROUP = 4
SLOTS = 4
MIB = 1 << 20

NT = (((1,), (1,)), ((), ()))
TN = (((0,), (0,)), ((), ()))


def dot(a, b, dims=(((1,), (0,)), ((), ()))):
    return lax.dot_general(a, b, dims, preferred_element_type=jnp.float32)


def passed_along(block, axis, distance):
    count = lax.axis_size(axis)
    return lax.ppermute(block, axis, [((i - distance) % count, i) for i in range(count)])


def params(limit_mib):
    return pltpu.CompilerParams(vmem_limit_bytes=limit_mib * MIB)


def cost(flops, moved):
    return pl.CostEstimate(flops=int(flops), bytes_accessed=int(moved), transcendentals=0)


def pack_kernel(lat_ref, rot_ref, out_ref):
    width = lat_ref.shape[1]
    rot = jnp.transpose(rot_ref[...].astype(jnp.float32)).astype(out_ref.dtype)
    out_ref[:, :width] = lat_ref[...]
    out_ref[:, width:] = jnp.concatenate([rot, rot], axis=1)


def project_kernel(
    nope_hbm, rope_hbm, dout_hbm, saved_hbm, wk_hbm, wv_hbm, rest_hbm,
    qx_ref, do_ref, stats_ref,
    nope, rope, dout, saved, wk, wv, flat_ref, sems, rest_sem,
):
    rows = nope.shape[0]
    width, total = wk.shape
    heads = total // HEAD_WIDTH
    quads = heads // GROUP
    half = rows // 2
    lanes = lax.broadcasted_iota(jnp.int32, (rows, HEAD_WIDTH), 1)
    arrays = (
        (wk_hbm, wk), (nope_hbm, nope), (wv_hbm, wv), (dout_hbm, dout), (saved_hbm, saved), (rope_hbm, rope),
    )

    def copies(quad):
        for i, (source, target) in enumerate(arrays):
            size = source.shape[1] // quads
            cols = slice(quad * size, (quad + 1) * size)
            yield pltpu.make_async_copy(source.at[:, cols], target.at[:, cols], sems.at[quad, i])

    for quad in range(quads):
        for copy in copies(quad):
            copy.start()
    rest_copy = pltpu.make_async_copy(rest_hbm, flat_ref.at[0, pl.ds(0, heads)], rest_sem)
    rest_copy.start()
    found = jnp.zeros((rows, HEAD_WIDTH), jnp.float32)
    for quad in range(quads):
        for copy in copies(quad):
            copy.wait()
        for g in range(GROUP):
            at = quad * GROUP + g
            cols = slice(at * HEAD_WIDTH, (at + 1) * HEAD_WIDTH)
            place = slice(g * half, (g + 1) * half)
            d_out = dout[:, cols]
            q_abs = dot(nope[:, cols], wk[:, cols], NT).astype(jnp.bfloat16)
            d_lat = dot(d_out, wv[:, cols], NT).astype(jnp.bfloat16)
            pair = rope[:, (at // 2) * HEAD_WIDTH : (at // 2 + 1) * HEAD_WIDTH]
            mine = (lanes < HEAD_WIDTH // 2) if g % 2 == 0 else (lanes >= HEAD_WIDTH // 2)
            pair = jnp.where(mine, pair, jnp.zeros_like(pair))
            for late, part in ((0, slice(0, half)), (1, slice(half, rows))):
                qx_ref[late, quad, place, :width] = q_abs[part]
                qx_ref[late, quad, place, width:] = pair[part]
                do_ref[late, quad, place] = d_lat[part]
            prod = d_out.astype(jnp.float32) * saved[:, cols].astype(jnp.float32)
            delta = jnp.sum(prod, axis=1, keepdims=True)
            found = jnp.where(lanes == at, delta, found)
    rest_copy.wait()
    flat_ref[1] = jnp.transpose(found)
    low = lax.broadcasted_iota(jnp.int32, (heads // 2, rows), 1) < half
    for kind in range(2):
        even = flat_ref[kind, pl.ds(0, heads // 2, 2), :]
        odd = flat_ref[kind, pl.ds(1, heads // 2, 2), :]
        stats_ref[2 * kind] = jnp.where(low, even, pltpu.roll(odd, half, 1))
        stats_ref[2 * kind + 1] = jnp.where(low, pltpu.roll(even, half, 1), odd)


def place_keys(keys_ref, own_ref, near_ref, far_ref):
    rows = own_ref.shape[0]
    half = rows // 2
    parts = (
        (own_ref, half), (own_ref, 0), (near_ref, 0), (far_ref, 0), (near_ref, half), (far_ref, half),
    )
    for at, (ref, start) in enumerate(parts):
        keys_ref[at * half : (at + 1) * half] = ref[start : start + half]


def scores_kernel(
    scale, qx_ref, do_ref, stats_ref, own_ref, near_ref, far_ref,
    dsl_ref, dse_ref, ptl_ref, pte_ref, c1_ref, c2_ref, keys_ref, bias_ref, s_ref, p_ref,
):
    rank = lax.axis_index("ctx")
    quads, span, wide = qx_ref.shape[1:]
    width = do_ref.shape[3]
    rows = own_ref.shape[0]
    half = rows // 2
    place_keys(keys_ref, own_ref, near_ref, far_ref)
    off = jnp.float32(-jnp.inf)
    row = lax.broadcasted_iota(jnp.int32, (half, rows), 0)
    col = lax.broadcasted_iota(jnp.int32, (half, rows), 1) % half
    causal = jnp.where(row <= col, 0.0, off)
    open_ = jnp.zeros((half, rows), jnp.float32)
    bias_ref[1, :half] = causal
    bias_ref[1, half:rows] = open_
    bias_ref[0, half:rows] = causal
    for d in range(1, HOPS):
        first = slice(rows + (d - 1) * half, rows + d * half)
        second = slice(2 * rows + (d - 1) * half, 2 * rows + d * half)
        bias_ref[0, first] = jnp.where(rank < d, off, open_)
        bias_ref[1, first] = open_
        bias_ref[1, second] = jnp.where(rank < d, open_, off)

    def multiply(slot, late, quad, count):
        seen = slice(half * (1 - late), half * (1 - late) + count)
        s_ref[slot, :count] = dot(keys_ref[seen], qx_ref[late, quad], NT)
        p_ref[slot, :count] = dot(keys_ref[seen, :width], do_ref[late, quad], NT)

    def weigh(slot, late, quad, count, ds_ref, pt_ref):
        seen = slice(half * (1 - late), half * (1 - late) + count)
        bias = bias_ref[late, seen]

        def lane_row(kind):
            pieces = [stats_ref[2 * kind + late, slice(2 * quad + i, 2 * quad + i + 1)] for i in range(2)]
            return jnp.concatenate(pieces, axis=1)

        rest = lane_row(0)
        delta = lane_row(1)
        s = s_ref[slot, :count] * scale + jnp.concatenate([bias, bias], axis=1)
        top = jnp.maximum(jnp.max(s, axis=0, keepdims=True), rest)
        e = jnp.exp(s - top)
        inverse = 1.0 / (jnp.sum(e, axis=0, keepdims=True) + jnp.exp(rest - top))
        prob = e * inverse
        cols = slice(quad * span, (quad + 1) * span)
        pt_ref[:count, cols] = prob.astype(jnp.bfloat16)
        ds_ref[:count, cols] = (prob * (p_ref[slot, :count] - delta) * scale).astype(jnp.bfloat16)

    def run(late_count, early_count):
        items = []
        for quad in range(quads):
            items.append((1, quad, late_count, dsl_ref, ptl_ref))
            items.append((0, quad, early_count, dse_ref, pte_ref))
        multiply(0, *items[0][:3])
        for i, item in enumerate(items):
            if i + 1 < len(items):
                multiply((i + 1) % SLOTS, *items[i + 1][:3])
            weigh(i % SLOTS, *item)

    def terms(late, picked, ds_ref, pt_ref):
        q = qx_ref[late].reshape(quads * span, wide)
        d = do_ref[late].reshape(quads * span, width)
        lat = dot(ds_ref[picked], q[:, :width]) + dot(pt_ref[picked], d)
        return lat, dot(ds_ref[picked], q[:, width:])

    def put(at, lat, rot):
        for i, ref in ((0, c1_ref), (1, c2_ref)):
            ref[at : at + half, :width] = lat[i * half : (i + 1) * half].astype(jnp.bfloat16)
            ref[at : at + half, width:] = rot[i * half : (i + 1) * half].astype(jnp.bfloat16)

    @pl.when(rank >= HOPS - 1)
    def _():
        run(2 * rows, rows + half)
        late = terms(1, pl.ds(rows, rows), dsl_ref, ptl_ref)
        early = terms(0, pl.ds(half, rows), dse_ref, pte_ref)
        put(0, late[0] + early[0], late[1] + early[1])
        for ref in (c1_ref, c2_ref):
            ref[half:] = jnp.zeros_like(ref[half:])

    @pl.when(jnp.logical_and(rank > 0, rank < HOPS - 1))
    def _():
        run(3 * rows, rows + half)
        late = terms(1, pl.ds(rows, 2 * rows), dsl_ref, ptl_ref)
        early = terms(0, pl.ds(half, rows), dse_ref, pte_ref)
        put(0, late[0][:rows] + early[0], late[1][:rows] + early[1])
        put(half, late[0][rows:], late[1][rows:])

    @pl.when(rank == 0)
    def _():
        dse_ref[half:] = jnp.zeros_like(dse_ref[half:])
        run(3 * rows, half)
        late = terms(1, pl.ds(rows, 2 * rows), dsl_ref, ptl_ref)
        put(0, late[0][:rows], late[1][:rows])
        put(half, late[0][rows:], late[1][rows:])


def query_kernel(
    qx_ref, do_ref, dsl_ref, dse_ref, ptl_ref, pte_ref, own_ref, near_ref, far_ref, wk_ref,
    dnope_hbm, drope_hbm, grad_ref, keys_ref, dq_ref, dnope, drope, sems,
):
    rank = lax.axis_index("ctx")
    quads, span, wide = qx_ref.shape[1:]
    width = do_ref.shape[3]
    rows = own_ref.shape[0]
    half = rows // 2
    lanes = lax.broadcasted_iota(jnp.int32, (rows, HEAD_WIDTH), 1)
    place_keys(keys_ref, own_ref, near_ref, far_ref)

    def copies(quad):
        for i, (source, target) in enumerate(((dnope, dnope_hbm), (drope, drope_hbm))):
            size = source.shape[1] // quads
            cols = slice(quad * size, (quad + 1) * size)
            yield pltpu.make_async_copy(source.at[:, cols], target.at[:, cols], sems.at[quad, i])

    def meet(quad, late_count):
        cols = slice(quad * span, (quad + 1) * span)
        slot = quad % 2
        late = dot(dsl_ref[:late_count, cols], keys_ref[:late_count], TN)
        early = dot(dse_ref[:, cols], keys_ref[half : 2 * rows], TN)
        dq_ref[slot, 1] = late.astype(jnp.bfloat16)
        dq_ref[slot, 0] = early.astype(jnp.bfloat16)

    def leave(quad):
        slot = quad % 2

        def head(g, place):
            mine = slice(g * half, (g + 1) * half)
            return jnp.concatenate([dq_ref[slot, 0, mine, place], dq_ref[slot, 1, mine, place]], axis=0)

        for g in range(GROUP):
            at = quad * GROUP + g
            out = slice(at * HEAD_WIDTH, (at + 1) * HEAD_WIDTH)
            dnope[:, out] = dot(head(g, slice(0, width)), wk_ref[:, out]).astype(jnp.bfloat16)
            if g % 2 == 1:
                both = slice(width, wide)
                pair = jnp.where(lanes < HEAD_WIDTH // 2, head(g - 1, both), head(g, both))
                drope[:, (at // 2) * HEAD_WIDTH : (at // 2 + 1) * HEAD_WIDTH] = pair
        for copy in copies(quad):
            copy.start()

    def run(late_count):
        meet(0, late_count)
        for quad in range(quads):
            if quad + 1 < quads:
                meet(quad + 1, late_count)
            leave(quad)

    @pl.when(rank >= HOPS - 1)
    def _():
        run(2 * rows)

    @pl.when(rank < HOPS - 1)
    def _():
        run(3 * rows)

    def terms(late, count, ds_ref, pt_ref):
        q = qx_ref[late].reshape(quads * span, wide)
        d = do_ref[late].reshape(quads * span, width)
        lat = dot(ds_ref[:count], q[:, :width]) + dot(pt_ref[:count], d)
        return lat, dot(ds_ref[:count], q[:, width:])

    late_terms = terms(1, rows, dsl_ref, ptl_ref)
    early_terms = terms(0, half, dse_ref, pte_ref)
    for place, late, early in zip((slice(0, width), slice(width, wide)), late_terms, early_terms):
        grad_ref[:half, place] = late[half:] + early
        grad_ref[half:, place] = late[:half]
    for quad in range(quads):
        for copy in copies(quad):
            copy.wait()


def sum_kernel(own_ref, a_ref, b_ref, out_ref):
    out_ref[...] = own_ref[...] + (a_ref[...].astype(jnp.float32) + b_ref[...].astype(jnp.float32))


def finish_kernel(mine_ref, other_ref, lat_ref, rot_ref):
    width = lat_ref.shape[1]
    narrow = rot_ref.shape[0]
    total = mine_ref[...] + other_ref[...]
    lat_ref[...] = total[:, :width]
    rot_ref[...] = jnp.transpose(total[:, width : width + narrow] + total[:, width + narrow :])


VMEM = pl.BlockSpec(memory_space=pltpu.VMEM)
HBM = pl.BlockSpec(memory_space=pltpu.HBM)


def in_hbm(*arrays):
    return [pltpu.with_memory_space_constraint(array, pltpu.HBM) for array in arrays]


def per_device(
    q_nope, q_rope, latent, k_rope, d_out, out_heads, lse_rest, key_up_weight, value_up_weight
):
    rows, width = latent.shape
    narrow = k_rope.shape[1]
    wide = width + 2 * narrow
    half = rows // 2
    heads = key_up_weight.shape[1] // HEAD_WIDTH
    quads, span = heads // GROUP, GROUP * half
    scale = (HEAD_WIDTH + narrow) ** (-0.5)
    bf16, f32 = jnp.bfloat16, jnp.float32
    total = heads * rows

    own = pl.pallas_call(
        pack_kernel,
        out_shape=jax.ShapeDtypeStruct((rows, wide), bf16),
        in_specs=[VMEM, VMEM],
        out_specs=VMEM,
        compiler_params=params(4),
        name="pack",
    )(*in_hbm(latent, jnp.transpose(k_rope)))
    near = passed_along(own, "ctx", 1)
    far = passed_along(own, "ctx", 2)

    qx, do_lat, stats = pl.pallas_call(
        project_kernel,
        out_shape=(
            pltpu.VMEM((2, quads, span, wide), bf16),
            pltpu.VMEM((2, quads, span, width), bf16),
            pltpu.VMEM((4, heads // 2, rows), f32),
        ),
        in_specs=[HBM] * 7,
        out_specs=[VMEM] * 3,
        scratch_shapes=[
            pltpu.VMEM(q_nope.shape, bf16),
            pltpu.VMEM(q_rope.shape, bf16),
            pltpu.VMEM(d_out.shape, bf16),
            pltpu.VMEM(out_heads.shape, bf16),
            pltpu.VMEM(key_up_weight.shape, bf16),
            pltpu.VMEM(value_up_weight.shape, bf16),
            pltpu.VMEM((2, HEAD_WIDTH, rows), f32),
            pltpu.SemaphoreType.DMA((quads, 6)),
            pltpu.SemaphoreType.DMA,
        ],
        compiler_params=params(20),
        cost_estimate=cost(4 * total * HEAD_WIDTH * width, 12 * MIB),
        name="project",
    )(
        *in_hbm(
            q_nope, q_rope, d_out, out_heads, key_up_weight, value_up_weight, jnp.transpose(lse_rest)
        )
    )

    late = pltpu.VMEM((3 * rows, quads * span), bf16)
    early = pltpu.VMEM((rows + half, quads * span), bf16)
    *terms, c_near, c_far = pl.pallas_call(
        functools.partial(scores_kernel, scale),
        out_shape=(late, early, late, early) + (jax.ShapeDtypeStruct((rows, wide), bf16),) * 2,
        in_specs=[VMEM] * 6,
        out_specs=[VMEM] * 6,
        scratch_shapes=[
            pltpu.VMEM((3 * rows, wide), bf16),
            pltpu.VMEM((2, 3 * rows, rows), f32),
            pltpu.VMEM((SLOTS, 3 * rows, span), f32),
            pltpu.VMEM((SLOTS, 3 * rows, span), f32),
        ],
        compiler_params=params(24),
        cost_estimate=cost(8 * total * rows * width, 16 * MIB),
        name="scores",
    )(qx, do_lat, stats, own, near, far)
    from_near = passed_along(c_near, "ctx", -1)
    from_far = passed_along(c_far, "ctx", -2)

    d_q_nope, d_q_rope, grad = pl.pallas_call(
        query_kernel,
        out_shape=(
            jax.ShapeDtypeStruct((rows, heads * HEAD_WIDTH), bf16),
            jax.ShapeDtypeStruct((rows, heads * narrow), bf16),
            jax.ShapeDtypeStruct((rows, wide), f32),
        ),
        in_specs=[VMEM] * 10,
        out_specs=[HBM, HBM, VMEM],
        scratch_shapes=[
            pltpu.VMEM((3 * rows, wide), bf16),
            pltpu.VMEM((2, 2, span, wide), bf16),
            pltpu.VMEM((rows, heads * HEAD_WIDTH), bf16),
            pltpu.VMEM((rows, heads * narrow), bf16),
            pltpu.SemaphoreType.DMA((quads, 2)),
        ],
        compiler_params=params(16),
        cost_estimate=cost(10 * total * rows * width, 16 * MIB),
        name="query",
    )(qx, do_lat, *terms, own, near, far, key_up_weight)

    partial = pl.pallas_call(
        sum_kernel,
        out_shape=jax.ShapeDtypeStruct((rows, wide), f32),
        in_specs=[VMEM] * 3,
        out_specs=VMEM,
        compiler_params=params(4),
        name="gather",
    )(grad, from_near, from_far)

    sharers = lax.axis_size("head")
    distance = 1
    while 2 * distance < sharers:
        partial = partial + lax.ppermute(
            partial, "head", [(i, i ^ distance) for i in range(sharers)]
        )
        distance *= 2
    other = lax.ppermute(partial, "head", [(i, i ^ distance) for i in range(sharers)])
    latent_gradient, d_k_rope = pl.pallas_call(
        finish_kernel,
        out_shape=(
            jax.ShapeDtypeStruct((rows, width), f32),
            jax.ShapeDtypeStruct((narrow, rows), f32),
        ),
        in_specs=[VMEM] * 2,
        out_specs=[VMEM] * 2,
        compiler_params=params(4),
        name="finish",
    )(partial, other)
    return d_q_nope, d_q_rope, latent_gradient, jnp.transpose(d_k_rope)


def solution(mesh):
    placed = (
        P("ctx", "head"),
        P("ctx", "head"),
        P("ctx", None),
        P("ctx", None),
        P("ctx", "head"),
        P("ctx", "head"),
        P("ctx", "head"),
        P(None, "head"),
        P(None, "head"),
    )
    return jax.shard_map(
        per_device,
        mesh=mesh,
        in_specs=placed,
        out_specs=(P("ctx", "head"), P("ctx", "head"), P("ctx", None), P("ctx", None)),
        check_vma=False,
    )
```

```python
import functools

import jax
import jax.numpy as jnp
from jax import lax
from jax.experimental import pallas as pl
from jax.experimental.pallas import tpu as pltpu
from jax.sharding import PartitionSpec as P

HEAD_WIDTH = 128
HOPS = 3
GROUP = 4
SLOTS = 4
MIB = 1 << 20

NT = (((1,), (1,)), ((), ()))
TN = (((0,), (0,)), ((), ()))


def dot(a, b, dims=(((1,), (0,)), ((), ()))):
    return lax.dot_general(a, b, dims, preferred_element_type=jnp.float32)


def between_groups(block, direction):
    groups, sharers = lax.axis_size("ctx"), lax.axis_size("head")
    route = []
    for group in range(groups):
        for head in range(sharers):
            to = (group + direction * (1 + head % 2)) % groups
            route.append((group * sharers + head, to * sharers + head))
    return lax.ppermute(block, ("ctx", "head"), route)


def with_partner(block, bit=1):
    return lax.ppermute(block, "head", [(i, i ^ bit) for i in range(lax.axis_size("head"))])


def params(limit_mib):
    return pltpu.CompilerParams(vmem_limit_bytes=limit_mib * MIB)


def cost(flops, moved):
    return pl.CostEstimate(flops=int(flops), bytes_accessed=int(moved), transcendentals=0)


def pack_kernel(lat_ref, rot_ref, out_ref):
    width = lat_ref.shape[1]
    rot = jnp.transpose(rot_ref[...].astype(jnp.float32)).astype(out_ref.dtype)
    out_ref[:, :width] = lat_ref[...]
    out_ref[:, width:] = jnp.concatenate([rot, rot], axis=1)


def project_kernel(
    scale, nope_hbm, rope_hbm, dout_hbm, saved_hbm, wk_hbm, wv_hbm, rest_hbm, own_ref,
    qx_ref, do_ref, stats_ref, sl_ref, se_ref, pl_ref, pe_ref,
    nope, rope, dout, saved, wk, wv, flat_ref, sems, rest_sem,
):
    rows = nope.shape[0]
    width, total = wk.shape
    heads = total // HEAD_WIDTH
    quads = heads // GROUP
    half = rows // 2
    lanes = lax.broadcasted_iota(jnp.int32, (rows, HEAD_WIDTH), 1)
    arrays = (
        (wk_hbm, wk), (nope_hbm, nope), (wv_hbm, wv), (dout_hbm, dout), (saved_hbm, saved), (rope_hbm, rope),
    )

    def copies(quad):
        for i, (source, target) in enumerate(arrays):
            size = source.shape[1] // quads
            cols = slice(quad * size, (quad + 1) * size)
            yield pltpu.make_async_copy(source.at[:, cols], target.at[:, cols], sems.at[quad, i])

    for quad in range(quads):
        for copy in copies(quad):
            copy.start()
    rest_copy = pltpu.make_async_copy(rest_hbm, flat_ref.at[0, pl.ds(0, heads)], rest_sem)
    rest_copy.start()
    found = jnp.zeros((rows, HEAD_WIDTH), jnp.float32)
    span = GROUP * half
    key = lax.broadcasted_iota(jnp.int32, (half, span), 0)
    causal = key <= lax.broadcasted_iota(jnp.int32, (half, span), 1) % half

    def meet_own(quad):
        s = dot(own_ref[...], qx_ref[1, quad], NT) * scale
        sl_ref[quad, :half] = s[:half]
        sl_ref[quad, half:] = jnp.where(causal, s[half:], -jnp.inf)
        pl_ref[quad] = dot(own_ref[:, :width], do_ref[1, quad], NT)
        s = dot(own_ref[:half], qx_ref[0, quad], NT) * scale
        se_ref[quad] = jnp.where(causal, s, -jnp.inf)
        pe_ref[quad] = dot(own_ref[:half, :width], do_ref[0, quad], NT)

    for quad in range(quads):
        for copy in copies(quad):
            copy.wait()
        for g in range(GROUP):
            at = quad * GROUP + g
            cols = slice(at * HEAD_WIDTH, (at + 1) * HEAD_WIDTH)
            place = slice(g * half, (g + 1) * half)
            d_out = dout[:, cols]
            q_abs = dot(nope[:, cols], wk[:, cols], NT).astype(jnp.bfloat16)
            d_lat = dot(d_out, wv[:, cols], NT).astype(jnp.bfloat16)
            pair = rope[:, (at // 2) * HEAD_WIDTH : (at // 2 + 1) * HEAD_WIDTH]
            mine = (lanes < HEAD_WIDTH // 2) if g % 2 == 0 else (lanes >= HEAD_WIDTH // 2)
            pair = jnp.where(mine, pair, jnp.zeros_like(pair))
            for late, part in ((0, slice(0, half)), (1, slice(half, rows))):
                qx_ref[late, quad, place, :width] = q_abs[part]
                qx_ref[late, quad, place, width:] = pair[part]
                do_ref[late, quad, place] = d_lat[part]
            prod = d_out.astype(jnp.float32) * saved[:, cols].astype(jnp.float32)
            delta = jnp.sum(prod, axis=1, keepdims=True)
            found = jnp.where(lanes == at, delta, found)
        if quad:
            meet_own(quad - 1)
    meet_own(quads - 1)
    rest_copy.wait()
    flat_ref[1] = jnp.transpose(found)
    low = lax.broadcasted_iota(jnp.int32, (heads // 2, rows), 1) < half
    for kind in range(2):
        even = flat_ref[kind, pl.ds(0, heads // 2, 2), :]
        odd = flat_ref[kind, pl.ds(1, heads // 2, 2), :]
        stats_ref[2 * kind] = jnp.where(low, even, pltpu.roll(odd, half, 1))
        stats_ref[2 * kind + 1] = jnp.where(low, pltpu.roll(even, half, 1), odd)


def place_keys(keys_ref, mine_ref, other_ref):
    half = mine_ref.shape[0] // 2
    even = lax.axis_index("head") % 2 == 0

    @pl.when(even)
    def _():
        for at, ref in ((0, mine_ref), (1, other_ref)):
            keys_ref[at * half : (at + 1) * half] = ref[:half]
            keys_ref[(at + 2) * half : (at + 3) * half] = ref[half:]

    @pl.when(jnp.logical_not(even))
    def _():
        for at, ref in ((0, other_ref), (1, mine_ref)):
            keys_ref[at * half : (at + 1) * half] = ref[:half]
            keys_ref[(at + 2) * half : (at + 3) * half] = ref[half:]


def scores_kernel(
    scale, qx_ref, do_ref, stats_ref, sl_ref, se_ref, pl_ref, pe_ref, mine_ref, other_ref,
    dsl_ref, dse_ref, ptl_ref, pte_ref, keep_ref, give_ref, keys_ref, bias_ref, s_ref, p_ref,
):
    rank = lax.axis_index("ctx")
    even = lax.axis_index("head") % 2 == 0
    quads, span, wide = qx_ref.shape[1:]
    width = do_ref.shape[3]
    rows = mine_ref.shape[0]
    half = rows // 2
    place_keys(keys_ref, mine_ref, other_ref)
    off = jnp.float32(-jnp.inf)
    open_ = jnp.zeros((half, rows), jnp.float32)
    for d in range(1, HOPS):
        place = slice((d - 1) * half, d * half)
        bias_ref[0, place] = jnp.where(rank < d, off, open_)
        bias_ref[1, place] = jnp.where(rank < d, open_, off)

    def multiply(slot, late, quad, count):
        if count:
            s_ref[slot, :count] = dot(keys_ref[:count], qx_ref[late, quad], NT)
            p_ref[slot, :count] = dot(keys_ref[:count, :width], do_ref[late, quad], NT)

    def weigh(slot, late, quad, count):
        own_s, own_p, ds_ref, pt_ref = (
            (sl_ref, pl_ref, dsl_ref, ptl_ref) if late else (se_ref, pe_ref, dse_ref, pte_ref)
        )
        for i in range(span // rows):
            lanes = slice(i * rows, (i + 1) * rows)
            row = slice((span // rows) * quad + i, (span // rows) * quad + i + 1)
            rest = stats_ref[late, row]
            delta = stats_ref[2 + late, row]
            parts = [(own_s[quad, :, lanes], own_p[quad, :, lanes])]
            if count:
                s = s_ref[slot, :rows, lanes] * scale
                parts.append((s if late else s + bias_ref[0], p_ref[slot, :rows, lanes]))
            if count > rows:
                s = s_ref[slot, rows:, lanes] * scale
                parts.append((s + bias_ref[1], p_ref[slot, rows:, lanes]))
            top = rest
            for s, _ in parts:
                top = jnp.maximum(top, jnp.max(s, axis=0, keepdims=True))
            exps = [jnp.exp(s - top) for s, _ in parts]
            mass = jnp.exp(rest - top)
            for e in exps:
                mass = mass + jnp.sum(e, axis=0, keepdims=True)
            inverse = 1.0 / mass
            cols = slice(quad * span + i * rows, quad * span + (i + 1) * rows)
            at = 0
            for e, (_, p) in zip(exps, parts):
                prob = e * inverse
                place = slice(at, at + e.shape[0])
                pt_ref[place, cols] = prob.astype(jnp.bfloat16)
                ds_ref[place, cols] = (prob * (p - delta) * scale).astype(jnp.bfloat16)
                at += e.shape[0]

    def run(late_count, early_count):
        items = []
        for quad in range(quads):
            items.append((1, quad, late_count))
            items.append((0, quad, early_count))
        multiply(0, *items[0])
        for i, item in enumerate(items):
            if i + 1 < len(items):
                multiply((i + 1) % SLOTS, *items[i + 1])
            weigh(i % SLOTS, *item)

    def terms(late, picked, ds_ref, pt_ref):
        q = qx_ref[late].reshape(quads * span, wide)
        d = do_ref[late].reshape(quads * span, width)
        lat = dot(ds_ref[picked], q[:, :width]) + dot(pt_ref[picked], d)
        return lat, dot(ds_ref[picked], q[:, width:])

    def put(at, lat, rot):
        near, far = slice(0, half), slice(half, rows)
        place = slice(at, at + half)

        @pl.when(even)
        def _():
            keep_ref[place, :width], keep_ref[place, width:] = lat[near], rot[near]
            give_ref[place, :width] = lat[far].astype(jnp.bfloat16)
            give_ref[place, width:] = rot[far].astype(jnp.bfloat16)

        @pl.when(jnp.logical_not(even))
        def _():
            keep_ref[place, :width], keep_ref[place, width:] = lat[far], rot[far]
            give_ref[place, :width] = lat[near].astype(jnp.bfloat16)
            give_ref[place, width:] = rot[near].astype(jnp.bfloat16)

    @pl.when(rank >= HOPS - 1)
    def _():
        run(rows, rows)
        late = terms(1, pl.ds(rows, rows), dsl_ref, ptl_ref)
        early = terms(0, pl.ds(half, rows), dse_ref, pte_ref)
        put(0, late[0] + early[0], late[1] + early[1])
        for ref in (keep_ref, give_ref):
            ref[half:] = jnp.zeros_like(ref[half:])

    @pl.when(jnp.logical_and(rank > 0, rank < HOPS - 1))
    def _():
        run(2 * rows, rows)
        late = terms(1, pl.ds(rows, 2 * rows), dsl_ref, ptl_ref)
        early = terms(0, pl.ds(half, rows), dse_ref, pte_ref)
        put(0, late[0][:rows] + early[0], late[1][:rows] + early[1])
        put(half, late[0][rows:], late[1][rows:])

    @pl.when(rank == 0)
    def _():
        dse_ref[half:] = jnp.zeros_like(dse_ref[half:])
        run(2 * rows, 0)
        late = terms(1, pl.ds(rows, 2 * rows), dsl_ref, ptl_ref)
        put(0, late[0][:rows], late[1][:rows])
        put(half, late[0][rows:], late[1][rows:])


def own_kernel(qx_ref, do_ref, dsl_ref, dse_ref, ptl_ref, pte_ref, grad_ref):
    quads, span, wide = qx_ref.shape[1:]
    width = do_ref.shape[3]
    rows = grad_ref.shape[0]
    half = rows // 2

    def terms(late, count, ds_ref, pt_ref):
        q = qx_ref[late].reshape(quads * span, wide)
        d = do_ref[late].reshape(quads * span, width)
        lat = dot(ds_ref[:count], q[:, :width]) + dot(pt_ref[:count], d)
        return lat, dot(ds_ref[:count], q[:, width:])

    late_terms = terms(1, rows, dsl_ref, ptl_ref)
    early_terms = terms(0, half, dse_ref, pte_ref)
    for place, late, early in zip((slice(0, width), slice(width, wide)), late_terms, early_terms):
        grad_ref[:half, place] = late[:half] + early
        grad_ref[half:, place] = late[half:]


def query_kernel(
    dsl_ref, dse_ref, own_ref, mine_ref, other_ref, wk_ref,
    dnope_hbm, drope_hbm, keys_ref, first_ref, dq_ref, dnope, drope, sems,
):
    rank = lax.axis_index("ctx")
    rows, wide = own_ref.shape
    width = wk_ref.shape[0]
    half = rows // 2
    span = GROUP * half
    quads = dsl_ref.shape[1] // span
    lanes = lax.broadcasted_iota(jnp.int32, (rows, HEAD_WIDTH), 1)
    place_keys(keys_ref.at[pl.ds(rows, 2 * rows)], mine_ref, other_ref)
    keys_ref[:rows] = own_ref[...]
    first_ref[:half] = own_ref[:half]
    first_ref[half:] = keys_ref[rows : 2 * rows]

    def copies(quad):
        for i, (source, target) in enumerate(((dnope, dnope_hbm), (drope, drope_hbm))):
            size = source.shape[1] // quads
            cols = slice(quad * size, (quad + 1) * size)
            yield pltpu.make_async_copy(source.at[:, cols], target.at[:, cols], sems.at[quad, i])

    def meet(quad, late_count):
        cols = slice(quad * span, (quad + 1) * span)
        slot = quad % 2
        late = dot(dsl_ref[:late_count, cols], keys_ref[:late_count], TN)
        early = dot(dse_ref[:, cols], first_ref[...], TN)
        dq_ref[slot, 1] = late.astype(jnp.bfloat16)
        dq_ref[slot, 0] = early.astype(jnp.bfloat16)

    def leave(quad):
        slot = quad % 2

        def head(g, place):
            mine = slice(g * half, (g + 1) * half)
            return jnp.concatenate([dq_ref[slot, 0, mine, place], dq_ref[slot, 1, mine, place]], axis=0)

        for g in range(GROUP):
            at = quad * GROUP + g
            out = slice(at * HEAD_WIDTH, (at + 1) * HEAD_WIDTH)
            dnope[:, out] = dot(head(g, slice(0, width)), wk_ref[:, out]).astype(jnp.bfloat16)
            if g % 2 == 1:
                both = slice(width, wide)
                pair = jnp.where(lanes < HEAD_WIDTH // 2, head(g - 1, both), head(g, both))
                drope[:, (at // 2) * HEAD_WIDTH : (at // 2 + 1) * HEAD_WIDTH] = pair
        for copy in copies(quad):
            copy.start()

    def run(late_count):
        meet(0, late_count)
        for quad in range(quads):
            if quad + 1 < quads:
                meet(quad + 1, late_count)
            leave(quad)

    @pl.when(rank >= HOPS - 1)
    def _():
        run(2 * rows)

    @pl.when(rank < HOPS - 1)
    def _():
        run(3 * rows)

    for quad in range(quads):
        for copy in copies(quad):
            copy.wait()


def pair_kernel(keep_ref, got_ref, out_ref):
    out_ref[...] = (keep_ref[...] + got_ref[...].astype(jnp.float32)).astype(out_ref.dtype)


def sum_kernel(own_ref, got_ref, out_ref):
    out_ref[...] = own_ref[...] + got_ref[...].astype(jnp.float32)


def finish_kernel(mine_ref, other_ref, lat_ref, rot_ref):
    width = lat_ref.shape[1]
    narrow = rot_ref.shape[0]
    total = mine_ref[...] + other_ref[...]
    lat_ref[...] = total[:, :width]
    rot_ref[...] = jnp.transpose(total[:, width : width + narrow] + total[:, width + narrow :])


VMEM = pl.BlockSpec(memory_space=pltpu.VMEM)
HBM = pl.BlockSpec(memory_space=pltpu.HBM)


def in_hbm(*arrays):
    return [pltpu.with_memory_space_constraint(array, pltpu.HBM) for array in arrays]


def per_device(
    q_nope, q_rope, latent, k_rope, d_out, out_heads, lse_rest, key_up_weight, value_up_weight
):
    rows, width = latent.shape
    narrow = k_rope.shape[1]
    wide = width + 2 * narrow
    half = rows // 2
    heads = key_up_weight.shape[1] // HEAD_WIDTH
    quads, span = heads // GROUP, GROUP * half
    scale = (HEAD_WIDTH + narrow) ** (-0.5)
    bf16, f32 = jnp.bfloat16, jnp.float32
    total = heads * rows

    own = pl.pallas_call(
        pack_kernel,
        out_shape=jax.ShapeDtypeStruct((rows, wide), bf16),
        in_specs=[VMEM, VMEM],
        out_specs=VMEM,
        compiler_params=params(4),
        name="pack",
    )(*in_hbm(latent, jnp.transpose(k_rope)))
    mine = between_groups(own, 1)

    late_own = pltpu.VMEM((quads, rows, span), f32)
    early_own = pltpu.VMEM((quads, half, span), f32)
    qx, do_lat, stats, *met = pl.pallas_call(
        functools.partial(project_kernel, scale),
        out_shape=(
            pltpu.VMEM((2, quads, span, wide), bf16),
            pltpu.VMEM((2, quads, span, width), bf16),
            pltpu.VMEM((4, heads // 2, rows), f32),
            late_own, early_own, late_own, early_own,
        ),
        in_specs=[HBM] * 7 + [VMEM],
        out_specs=[VMEM] * 7,
        scratch_shapes=[
            pltpu.VMEM(q_nope.shape, bf16),
            pltpu.VMEM(q_rope.shape, bf16),
            pltpu.VMEM(d_out.shape, bf16),
            pltpu.VMEM(out_heads.shape, bf16),
            pltpu.VMEM(key_up_weight.shape, bf16),
            pltpu.VMEM(value_up_weight.shape, bf16),
            pltpu.VMEM((2, HEAD_WIDTH, rows), f32),
            pltpu.SemaphoreType.DMA((quads, 6)),
            pltpu.SemaphoreType.DMA,
        ],
        compiler_params=params(20),
        cost_estimate=cost(4 * total * HEAD_WIDTH * width, 12 * MIB),
        name="project",
    )(
        *in_hbm(
            q_nope, q_rope, d_out, out_heads, key_up_weight, value_up_weight, jnp.transpose(lse_rest)
        ),
        own,
    )
    mine, stats = lax.optimization_barrier((mine, stats))
    other = with_partner(mine)

    late = pltpu.VMEM((3 * rows, quads * span), bf16)
    early = pltpu.VMEM((rows + half, quads * span), bf16)
    *terms, keep, give = pl.pallas_call(
        functools.partial(scores_kernel, scale),
        out_shape=(
            late, early, late, early,
            jax.ShapeDtypeStruct((rows, wide), f32),
            jax.ShapeDtypeStruct((rows, wide), bf16),
        ),
        in_specs=[VMEM] * 9,
        out_specs=[VMEM] * 6,
        scratch_shapes=[
            pltpu.VMEM((2 * rows, wide), bf16),
            pltpu.VMEM((2, rows, rows), f32),
            pltpu.VMEM((SLOTS, 2 * rows, span), f32),
            pltpu.VMEM((SLOTS, 2 * rows, span), f32),
        ],
        compiler_params=params(20),
        cost_estimate=cost(8 * total * rows * width, 16 * MIB),
        name="scores",
    )(qx, do_lat, stats, *met, mine, other)
    got = with_partner(give)
    grad = pl.pallas_call(
        own_kernel,
        out_shape=jax.ShapeDtypeStruct((rows, wide), f32),
        in_specs=[VMEM] * 6,
        out_specs=VMEM,
        compiler_params=params(8),
        cost_estimate=cost(4 * total * rows * width, 16 * MIB),
        name="own",
    )(qx, do_lat, *terms)
    got, grad = lax.optimization_barrier((got, grad))
    summed = pl.pallas_call(
        pair_kernel,
        out_shape=jax.ShapeDtypeStruct((rows, wide), bf16),
        in_specs=[VMEM] * 2,
        out_specs=VMEM,
        compiler_params=params(4),
        name="pair",
    )(keep, got)
    arrived = between_groups(summed, -1)

    d_q_nope, d_q_rope = pl.pallas_call(
        query_kernel,
        out_shape=(
            jax.ShapeDtypeStruct((rows, heads * HEAD_WIDTH), bf16),
            jax.ShapeDtypeStruct((rows, heads * narrow), bf16),
        ),
        in_specs=[VMEM] * 6,
        out_specs=[HBM, HBM],
        scratch_shapes=[
            pltpu.VMEM((3 * rows, wide), bf16),
            pltpu.VMEM((rows + half, wide), bf16),
            pltpu.VMEM((2, 2, span, wide), bf16),
            pltpu.VMEM((rows, heads * HEAD_WIDTH), bf16),
            pltpu.VMEM((rows, heads * narrow), bf16),
            pltpu.SemaphoreType.DMA((quads, 2)),
        ],
        compiler_params=params(16),
        cost_estimate=cost(6 * total * rows * width, 16 * MIB),
        name="query",
    )(terms[0], terms[1], own, mine, other, key_up_weight)

    arrived, d_q_nope = lax.optimization_barrier((arrived, d_q_nope))
    partial = pl.pallas_call(
        sum_kernel,
        out_shape=jax.ShapeDtypeStruct((rows, wide), f32),
        in_specs=[VMEM] * 2,
        out_specs=VMEM,
        compiler_params=params(4),
        name="gather",
    )(grad, arrived)

    sharers = lax.axis_size("head")
    bit = 1
    while 2 * bit < sharers:
        partial = partial + with_partner(partial, bit)
        bit *= 2
    counterpart = with_partner(partial, bit)
    latent_gradient, d_k_rope = pl.pallas_call(
        finish_kernel,
        out_shape=(
            jax.ShapeDtypeStruct((rows, width), f32),
            jax.ShapeDtypeStruct((narrow, rows), f32),
        ),
        in_specs=[VMEM] * 2,
        out_specs=[VMEM] * 2,
        compiler_params=params(4),
        name="finish",
    )(partial, counterpart)
    return d_q_nope, d_q_rope, latent_gradient, jnp.transpose(d_k_rope)


def solution(mesh):
    placed = (
        P("ctx", "head"),
        P("ctx", "head"),
        P("ctx", None),
        P("ctx", None),
        P("ctx", "head"),
        P("ctx", "head"),
        P("ctx", "head"),
        P(None, "head"),
        P(None, "head"),
    )
    return jax.shard_map(
        per_device,
        mesh=mesh,
        in_specs=placed,
        out_specs=(P("ctx", "head"), P("ctx", "head"), P("ctx", None), P("ctx", None)),
        check_vma=False,
    )
```

```python
import functools

import jax
import jax.numpy as jnp
from jax import lax
from jax.experimental import pallas as pl
from jax.experimental.pallas import tpu as pltpu
from jax.sharding import PartitionSpec as P

HEAD_WIDTH = 128
HOPS = 3
GROUP = 4
SLOTS = 4
MIB = 1 << 20

NT = (((1,), (1,)), ((), ()))
TN = (((0,), (0,)), ((), ()))


def dot(a, b, dims=(((1,), (0,)), ((), ()))):
    return lax.dot_general(a, b, dims, preferred_element_type=jnp.float32)


def to_later_groups(block):
    groups, sharers = lax.axis_size("ctx"), lax.axis_size("head")
    route = []
    for group in range(groups):
        for head in range(sharers):
            to = (group + 1 + head % 2) % groups
            route.append((group * sharers + head, to * sharers + head))
    return lax.ppermute(block, ("ctx", "head"), route)


def to_earlier_groups(block):
    groups, sharers = lax.axis_size("ctx"), lax.axis_size("head")
    route = []
    for group in range(groups):
        for head in range(sharers):
            to = group - 1 - head % 2
            if to >= 0:
                route.append((group * sharers + head, to * sharers + head))
    return lax.ppermute(block, ("ctx", "head"), route)


def round_the_end(block, distance):
    groups = lax.axis_size("ctx")
    return lax.ppermute(block, "ctx", [(i, (i - distance) % groups) for i in range(distance)])


def with_partner(block, bit=1):
    return lax.ppermute(block, "head", [(i, i ^ bit) for i in range(lax.axis_size("head"))])


def params(limit_mib):
    return pltpu.CompilerParams(vmem_limit_bytes=limit_mib * MIB)


def cost(flops, moved):
    return pl.CostEstimate(flops=int(flops), bytes_accessed=int(moved), transcendentals=0)


def pack_kernel(lat_ref, rot_ref, out_ref):
    width = lat_ref.shape[1]
    rot = jnp.transpose(rot_ref[...].astype(jnp.float32)).astype(out_ref.dtype)
    out_ref[:, :width] = lat_ref[...]
    out_ref[:, width:] = jnp.concatenate([rot, rot], axis=1)


def project_kernel(
    scale, nope_hbm, rope_hbm, dout_hbm, saved_hbm, wk_hbm, wv_hbm, rest_hbm, own_ref,
    qx_ref, do_ref, stats_ref, sl_ref, se_ref, pl_ref, pe_ref,
    nope, rope, dout, saved, wk, wv, flat_ref, sems, rest_sem,
):
    rows = nope.shape[0]
    width, total = wk.shape
    heads = total // HEAD_WIDTH
    quads = heads // GROUP
    half = rows // 2
    lanes = lax.broadcasted_iota(jnp.int32, (rows, HEAD_WIDTH), 1)
    arrays = (
        (wk_hbm, wk), (nope_hbm, nope), (wv_hbm, wv), (dout_hbm, dout), (saved_hbm, saved), (rope_hbm, rope),
    )

    def copies(quad):
        for i, (source, target) in enumerate(arrays):
            size = source.shape[1] // quads
            cols = slice(quad * size, (quad + 1) * size)
            yield pltpu.make_async_copy(source.at[:, cols], target.at[:, cols], sems.at[quad, i])

    for quad in range(quads):
        for copy in copies(quad):
            copy.start()
    rest_copy = pltpu.make_async_copy(rest_hbm, flat_ref.at[0, pl.ds(0, heads)], rest_sem)
    rest_copy.start()
    found = jnp.zeros((rows, HEAD_WIDTH), jnp.float32)
    span = GROUP * half
    key = lax.broadcasted_iota(jnp.int32, (half, span), 0)
    causal = key <= lax.broadcasted_iota(jnp.int32, (half, span), 1) % half

    def meet_own(quad):
        s = dot(own_ref[...], qx_ref[1, quad], NT) * scale
        sl_ref[quad, :half] = s[:half]
        sl_ref[quad, half:] = jnp.where(causal, s[half:], -jnp.inf)
        pl_ref[quad] = dot(own_ref[:, :width], do_ref[1, quad], NT)
        s = dot(own_ref[:half], qx_ref[0, quad], NT) * scale
        se_ref[quad] = jnp.where(causal, s, -jnp.inf)
        pe_ref[quad] = dot(own_ref[:half, :width], do_ref[0, quad], NT)

    for quad in range(quads):
        for copy in copies(quad):
            copy.wait()
        for g in range(GROUP):
            at = quad * GROUP + g
            cols = slice(at * HEAD_WIDTH, (at + 1) * HEAD_WIDTH)
            place = slice(g * half, (g + 1) * half)
            d_out = dout[:, cols]
            q_abs = dot(nope[:, cols], wk[:, cols], NT).astype(jnp.bfloat16)
            d_lat = dot(d_out, wv[:, cols], NT).astype(jnp.bfloat16)
            pair = rope[:, (at // 2) * HEAD_WIDTH : (at // 2 + 1) * HEAD_WIDTH]
            mine = (lanes < HEAD_WIDTH // 2) if g % 2 == 0 else (lanes >= HEAD_WIDTH // 2)
            pair = jnp.where(mine, pair, jnp.zeros_like(pair))
            for late, part in ((0, slice(0, half)), (1, slice(half, rows))):
                qx_ref[late, quad, place, :width] = q_abs[part]
                qx_ref[late, quad, place, width:] = pair[part]
                do_ref[late, quad, place] = d_lat[part]
            prod = d_out.astype(jnp.float32) * saved[:, cols].astype(jnp.float32)
            delta = jnp.sum(prod, axis=1, keepdims=True)
            found = jnp.where(lanes == at, delta, found)

    @pl.when(lax.axis_index("ctx") < HOPS - 1)
    def _():
        for quad in range(quads):
            meet_own(quad)

    rest_copy.wait()
    flat_ref[1] = jnp.transpose(found)
    low = lax.broadcasted_iota(jnp.int32, (heads // 2, rows), 1) < half
    for kind in range(2):
        even = flat_ref[kind, pl.ds(0, heads // 2, 2), :]
        odd = flat_ref[kind, pl.ds(1, heads // 2, 2), :]
        stats_ref[2 * kind] = jnp.where(low, even, pltpu.roll(odd, half, 1))
        stats_ref[2 * kind + 1] = jnp.where(low, pltpu.roll(even, half, 1), odd)


def place_keys(keys_ref, mine_ref, other_ref):
    half = mine_ref.shape[0] // 2
    even = lax.axis_index("head") % 2 == 0

    def place(near, far):
        for at, (ref, start) in enumerate(((near, 0), (far, 0), (far, half), (near, half))):
            keys_ref[at * half : (at + 1) * half] = ref[start : start + half]

    @pl.when(even)
    def _():
        place(mine_ref, other_ref)

    @pl.when(jnp.logical_not(even))
    def _():
        place(other_ref, mine_ref)


def weigh_quad(scale, rest_of, delta_of, parts, span, lane_tile, start, ds_ref, pt_ref):
    for i in range(span // lane_tile):
        lanes = slice(i * lane_tile, (i + 1) * lane_tile)
        rest, delta = rest_of(i), delta_of(i)
        met = [part(lanes) for part in parts]
        top = rest
        for s, _ in met:
            top = jnp.maximum(top, jnp.max(s, axis=0, keepdims=True))
        exps = [jnp.exp(s - top) for s, _ in met]
        mass = jnp.exp(rest - top)
        for e in exps:
            mass = mass + jnp.sum(e, axis=0, keepdims=True)
        inverse = 1.0 / mass
        cols = slice(start + i * lane_tile, start + (i + 1) * lane_tile)
        at = 0
        for e, (_, p) in zip(exps, met):
            prob = e * inverse
            place = slice(at, at + e.shape[0])
            pt_ref[place, cols] = prob.astype(jnp.bfloat16)
            ds_ref[place, cols] = (prob * (p - delta) * scale).astype(jnp.bfloat16)
            at += e.shape[0]


def key_terms(qx_ref, do_ref, late, picked, ds_ref, pt_ref):
    quads, span, wide = qx_ref.shape[1:]
    width = do_ref.shape[3]
    q = qx_ref[late].reshape(quads * span, wide)
    d = do_ref[late].reshape(quads * span, width)
    lat = dot(ds_ref[picked], q[:, :width]) + dot(pt_ref[picked], d)
    return lat, dot(ds_ref[picked], q[:, width:])


def put(ref, place, terms, picked):
    width = terms[0].shape[1]
    ref[place, :width] = terms[0][picked].astype(ref.dtype)
    ref[place, width:] = terms[1][picked].astype(ref.dtype)


def wrapped_kernel(
    scale, qx_ref, do_ref, stats_ref, sl_ref, se_ref, pl_ref, pe_ref, mine_ref, other_ref,
    dsl_ref, dse_ref, ptl_ref, pte_ref, near_ref, far_ref, keys_ref, s_ref, p_ref,
):
    rank = lax.axis_index("ctx")
    quads, span, _ = qx_ref.shape[1:]
    width = do_ref.shape[3]
    rows = mine_ref.shape[0]
    half = rows // 2

    def multiply(slot, late, quad, count):
        if count:
            s_ref[slot, :count] = dot(keys_ref[:count], qx_ref[late, quad], NT)
            p_ref[slot, :count] = dot(keys_ref[:count, :width], do_ref[late, quad], NT)

    def weigh(slot, late, quad, count):
        own_s, own_p, ds_ref, pt_ref = (
            (sl_ref, pl_ref, dsl_ref, ptl_ref) if late else (se_ref, pe_ref, dse_ref, pte_ref)
        )
        tiles = span // rows
        parts = [lambda lanes: (own_s[quad, :, lanes], own_p[quad, :, lanes])]
        if count:
            parts.append(lambda lanes: (s_ref[slot, :count, lanes] * scale, p_ref[slot, :count, lanes]))
        weigh_quad(
            scale,
            lambda i: stats_ref[late, tiles * quad + i : tiles * quad + i + 1],
            lambda i: stats_ref[2 + late, tiles * quad + i : tiles * quad + i + 1],
            parts, span, rows, quad * span, ds_ref, pt_ref,
        )

    def run(late_count, early_count):
        items = []
        for quad in range(quads):
            items.append((1, quad, late_count))
            items.append((0, quad, early_count))
        multiply(0, *items[0])
        for i, item in enumerate(items):
            if i + 1 < len(items):
                multiply((i + 1) % SLOTS, *items[i + 1])
            weigh(i % SLOTS, *item)

    first, second = slice(0, half), slice(half, rows)

    @pl.when(rank < HOPS - 1)
    def _():
        place_keys(keys_ref, mine_ref, other_ref)

    @pl.when(rank == 0)
    def _():
        dse_ref[half:] = jnp.zeros_like(dse_ref[half:])
        run(2 * rows, 0)
        late = key_terms(qx_ref, do_ref, 1, pl.ds(rows, 2 * rows), dsl_ref, ptl_ref)
        put(near_ref, first, late, slice(0, half))
        put(far_ref, first, late, slice(half, rows))
        put(far_ref, second, late, slice(rows, rows + half))
        put(near_ref, second, late, slice(rows + half, 2 * rows))

    @pl.when(rank == 1)
    def _():
        dse_ref[rows:] = jnp.zeros_like(dse_ref[rows:])
        dsl_ref[2 * rows + half :] = jnp.zeros_like(dsl_ref[2 * rows + half :])
        run(rows + half, half)
        late = key_terms(qx_ref, do_ref, 1, pl.ds(rows, rows + half), dsl_ref, ptl_ref)
        early = key_terms(qx_ref, do_ref, 0, pl.ds(half, half), dse_ref, pte_ref)
        put(near_ref, first, (late[0][:half] + early[0], late[1][:half] + early[1]), slice(0, half))
        put(far_ref, first, late, slice(half, rows))
        put(far_ref, second, late, slice(rows, rows + half))
        near_ref[half:] = jnp.zeros_like(near_ref[half:])


def scores_kernel(
    scale, qx_ref, do_ref, stats_ref, own_ref, mine_ref, other_ref, wrapped_ref,
    dsl_ref, dse_ref, ptl_ref, pte_ref, keep_ref, give_ref, keys_ref, first_ref, away_ref, s_ref, p_ref,
):
    rank = lax.axis_index("ctx")
    even = lax.axis_index("head") % 2 == 0
    quads, span, _ = qx_ref.shape[1:]
    width = do_ref.shape[3]
    rows = own_ref.shape[0]
    half = rows // 2

    def multiply(slot, late, quad):
        keys = keys_ref if late else first_ref
        count = keys.shape[0]
        s_ref[slot, :count] = dot(keys[...], qx_ref[late, quad], NT)
        p_ref[slot, :count] = dot(keys[:, :width], do_ref[late, quad], NT)

    key = lax.broadcasted_iota(jnp.int32, (half, rows), 0)
    causal = key <= lax.broadcasted_iota(jnp.int32, (half, rows), 1) % half

    def weigh(slot, late, quad):
        ds_ref, pt_ref = (dsl_ref, ptl_ref) if late else (dse_ref, pte_ref)
        tiles = span // rows
        diagonal = half if late else 0

        def plain(start, stop):
            return lambda lanes: (s_ref[slot, start:stop, lanes] * scale, p_ref[slot, start:stop, lanes])

        def masked(lanes):
            s, p = plain(diagonal, diagonal + half)(lanes)
            return jnp.where(causal, s, -jnp.inf), p

        parts = [plain(0, half)] if late else []
        parts += [masked, plain(diagonal + half, diagonal + half + rows)]
        weigh_quad(
            scale,
            lambda i: stats_ref[late, tiles * quad + i : tiles * quad + i + 1],
            lambda i: stats_ref[2 + late, tiles * quad + i : tiles * quad + i + 1],
            parts, span, rows, quad * span, ds_ref, pt_ref,
        )

    def share(terms, near, far):
        everything = slice(0, half)

        @pl.when(even)
        def _():
            put(keep_ref, everything, terms, near)
            put(give_ref, everything, terms, far)

        @pl.when(jnp.logical_not(even))
        def _():
            put(keep_ref, everything, terms, far)
            put(give_ref, everything, terms, near)

    @pl.when(rank >= HOPS - 1)
    def _():
        place_keys(away_ref, mine_ref, other_ref)
        keys_ref[:rows] = own_ref[...]
        keys_ref[rows:] = away_ref[:rows]
        first_ref[:half] = own_ref[:half]
        first_ref[half:] = away_ref[:rows]
        items = []
        for quad in range(quads):
            items += [(1, quad), (0, quad)]
        multiply(0, *items[0])
        for i, item in enumerate(items):
            if i + 1 < len(items):
                multiply((i + 1) % SLOTS, *items[i + 1])
            weigh(i % SLOTS, *item)
        late = key_terms(qx_ref, do_ref, 1, pl.ds(rows, rows), dsl_ref, ptl_ref)
        early = key_terms(qx_ref, do_ref, 0, pl.ds(half, rows), dse_ref, pte_ref)
        share((late[0] + early[0], late[1] + early[1]), slice(0, half), slice(half, rows))

    @pl.when(rank < HOPS - 1)
    def _():
        for ref, is_near in ((keep_ref, even), (give_ref, jnp.logical_not(even))):
            sent = jnp.logical_and(is_near, rank == 1)
            near = wrapped_ref[:half].astype(jnp.float32)
            ref[...] = jnp.where(sent, near, 0.0).astype(ref.dtype)


def own_kernel(qx_ref, do_ref, wdl, wde, wpl, wpe, ndl, nde, npl, npe, grad_ref):
    rank = lax.axis_index("ctx")
    rows = grad_ref.shape[0]
    half = rows // 2

    def run(dsl_ref, dse_ref, ptl_ref, pte_ref):
        late = key_terms(qx_ref, do_ref, 1, pl.ds(0, rows), dsl_ref, ptl_ref)
        early = key_terms(qx_ref, do_ref, 0, pl.ds(0, half), dse_ref, pte_ref)
        both = (late[0][:half] + early[0], late[1][:half] + early[1])
        put(grad_ref, slice(0, half), both, slice(0, half))
        put(grad_ref, slice(half, rows), late, slice(half, rows))

    @pl.when(rank < HOPS - 1)
    def _():
        run(wdl, wde, wpl, wpe)

    @pl.when(rank >= HOPS - 1)
    def _():
        run(ndl, nde, npl, npe)


def query_kernel(
    chosen, wdl, wde, ndl, nde, own_ref, mine_ref, other_ref, wk_ref, *rest,
):
    dnope_hbm, drope_hbm, keys_ref, first_ref, dq_ref, dnope, drope, sems = rest[-8:]
    rank = lax.axis_index("ctx")
    rows, wide = own_ref.shape
    width = wk_ref.shape[0]
    half = rows // 2
    span = GROUP * half
    quads = wdl.shape[1] // span
    lanes = lax.broadcasted_iota(jnp.int32, (rows, HEAD_WIDTH), 1)
    place_keys(keys_ref.at[pl.ds(rows, 2 * rows)], mine_ref, other_ref)
    keys_ref[:rows] = own_ref[...]
    first_ref[:half] = own_ref[:half]
    first_ref[half:] = keys_ref[rows : 2 * rows]

    def copies(quad):
        for i, (source, target) in enumerate(((dnope, dnope_hbm), (drope, drope_hbm))):
            size = source.shape[1] // quads
            cols = slice(quad * size, (quad + 1) * size)
            yield pltpu.make_async_copy(source.at[:, cols], target.at[:, cols], sems.at[quad, i])

    def meet(quad, late_count, dsl_ref, dse_ref):
        cols = slice(quad * span, (quad + 1) * span)
        slot = quad % 2
        late = dot(dsl_ref[:late_count, cols], keys_ref[:late_count], TN)
        early = dot(dse_ref[:, cols], first_ref[...], TN)
        dq_ref[slot, 1] = late.astype(jnp.bfloat16)
        dq_ref[slot, 0] = early.astype(jnp.bfloat16)

    def leave(quad):
        slot = quad % 2

        def head(g, place):
            mine = slice(g * half, (g + 1) * half)
            return jnp.concatenate([dq_ref[slot, 0, mine, place], dq_ref[slot, 1, mine, place]], axis=0)

        for g in range(GROUP):
            at = quad * GROUP + g
            out = slice(at * HEAD_WIDTH, (at + 1) * HEAD_WIDTH)
            dnope[:, out] = dot(head(g, slice(0, width)), wk_ref[:, out]).astype(jnp.bfloat16)
            if g % 2 == 1:
                both = slice(width, wide)
                pair = jnp.where(lanes < HEAD_WIDTH // 2, head(g - 1, both), head(g, both))
                drope[:, (at // 2) * HEAD_WIDTH : (at // 2 + 1) * HEAD_WIDTH] = pair
        for copy in copies(quad):
            copy.start()

    def run(*given):
        meet(chosen[0], *given)
        for quad in chosen:
            if quad + 1 in chosen:
                meet(quad + 1, *given)
            leave(quad)

    @pl.when(rank >= HOPS - 1)
    def _():
        run(2 * rows, ndl, nde)

    @pl.when(rank < HOPS - 1)
    def _():
        run(3 * rows, wdl, wde)

    for quad in chosen:
        for copy in copies(quad):
            copy.wait()


def pair_kernel(keep_ref, got_ref, out_ref):
    out_ref[...] = (keep_ref[...] + got_ref[...].astype(jnp.float32)).astype(out_ref.dtype)


def sum_kernel(own_ref, got_ref, near_ref, far_ref, out_ref):
    half = got_ref.shape[0]
    out_ref[...] = own_ref[...] + (near_ref[...].astype(jnp.float32) + far_ref[...].astype(jnp.float32))
    out_ref[:half] += got_ref[...].astype(jnp.float32)


def finish_kernel(mine_ref, other_ref, lat_ref, rot_ref):
    width = lat_ref.shape[1]
    narrow = rot_ref.shape[0]
    total = mine_ref[...] + other_ref[...]
    lat_ref[...] = total[:, :width]
    rot_ref[...] = jnp.transpose(total[:, width : width + narrow] + total[:, width + narrow :])


VMEM = pl.BlockSpec(memory_space=pltpu.VMEM)
HBM = pl.BlockSpec(memory_space=pltpu.HBM)


def in_hbm(*arrays):
    return [pltpu.with_memory_space_constraint(array, pltpu.HBM) for array in arrays]


def per_device(
    q_nope, q_rope, latent, k_rope, d_out, out_heads, lse_rest, key_up_weight, value_up_weight
):
    rows, width = latent.shape
    narrow = k_rope.shape[1]
    wide = width + 2 * narrow
    half = rows // 2
    heads = key_up_weight.shape[1] // HEAD_WIDTH
    quads, span = heads // GROUP, GROUP * half
    scale = (HEAD_WIDTH + narrow) ** (-0.5)
    bf16, f32 = jnp.bfloat16, jnp.float32
    total = heads * rows

    own = pl.pallas_call(
        pack_kernel,
        out_shape=jax.ShapeDtypeStruct((rows, wide), bf16),
        in_specs=[VMEM, VMEM],
        out_specs=VMEM,
        compiler_params=params(4),
        name="pack",
    )(*in_hbm(latent, jnp.transpose(k_rope)))
    mine = to_later_groups(own)

    late_own = pltpu.VMEM((quads, rows, span), f32)
    early_own = pltpu.VMEM((quads, half, span), f32)
    qx, do_lat, stats, *met = pl.pallas_call(
        functools.partial(project_kernel, scale),
        out_shape=(
            pltpu.VMEM((2, quads, span, wide), bf16),
            pltpu.VMEM((2, quads, span, width), bf16),
            pltpu.VMEM((4, heads // 2, rows), f32),
            late_own, early_own, late_own, early_own,
        ),
        in_specs=[HBM] * 7 + [VMEM],
        out_specs=[VMEM] * 7,
        scratch_shapes=[
            pltpu.VMEM(q_nope.shape, bf16),
            pltpu.VMEM(q_rope.shape, bf16),
            pltpu.VMEM(d_out.shape, bf16),
            pltpu.VMEM(out_heads.shape, bf16),
            pltpu.VMEM(key_up_weight.shape, bf16),
            pltpu.VMEM(value_up_weight.shape, bf16),
            pltpu.VMEM((2, HEAD_WIDTH, rows), f32),
            pltpu.SemaphoreType.DMA((quads, 6)),
            pltpu.SemaphoreType.DMA,
        ],
        compiler_params=params(20),
        cost_estimate=cost(4 * total * HEAD_WIDTH * width, 12 * MIB),
        name="project",
    )(
        *in_hbm(
            q_nope, q_rope, d_out, out_heads, key_up_weight, value_up_weight, jnp.transpose(lse_rest)
        ),
        own,
    )
    mine, stats = lax.optimization_barrier((mine, stats))
    other = with_partner(mine)

    def pair_of(late_count, early_count):
        return (
            pltpu.VMEM((late_count, quads * span), bf16),
            pltpu.VMEM((early_count, quads * span), bf16),
        ) * 2

    slots = pltpu.VMEM((SLOTS, 2 * rows, span), f32)
    block = jax.ShapeDtypeStruct((rows, wide), bf16)
    *wrapped, to_near, to_far = pl.pallas_call(
        functools.partial(wrapped_kernel, scale),
        out_shape=pair_of(3 * rows, rows + half) + (block, block),
        in_specs=[VMEM] * 9,
        out_specs=[VMEM] * 6,
        scratch_shapes=[pltpu.VMEM((2 * rows, wide), bf16), slots, slots],
        compiler_params=params(16),
        cost_estimate=cost(MIB, MIB),
        name="wrapped",
    )(qx, do_lat, stats, *met, mine, other)
    end_near = round_the_end(to_near, 1)
    end_far = round_the_end(to_far, 2)

    *plain, keep, give = pl.pallas_call(
        functools.partial(scores_kernel, scale),
        out_shape=pair_of(2 * rows, rows + half)
        + (jax.ShapeDtypeStruct((half, wide), f32), jax.ShapeDtypeStruct((half, wide), bf16)),
        in_specs=[VMEM] * 7,
        out_specs=[VMEM] * 6,
        scratch_shapes=[
            pltpu.VMEM((2 * rows, wide), bf16),
            pltpu.VMEM((rows + half, wide), bf16),
            pltpu.VMEM((2 * rows, wide), bf16),
            slots,
            slots,
        ],
        compiler_params=params(16),
        cost_estimate=cost(8 * total * rows * width, 16 * MIB),
        name="scores",
    )(qx, do_lat, stats, own, mine, other, to_near)
    got = with_partner(give)
    grad = pl.pallas_call(
        own_kernel,
        out_shape=jax.ShapeDtypeStruct((rows, wide), f32),
        in_specs=[VMEM] * 10,
        out_specs=VMEM,
        compiler_params=params(8),
        cost_estimate=cost(4 * total * rows * width, 16 * MIB),
        name="own",
    )(qx, do_lat, *wrapped, *plain)
    got, grad = lax.optimization_barrier((got, grad))
    summed = pl.pallas_call(
        pair_kernel,
        out_shape=jax.ShapeDtypeStruct((half, wide), bf16),
        in_specs=[VMEM] * 2,
        out_specs=VMEM,
        compiler_params=params(4),
        name="pair",
    )(keep, got)
    arrived = to_earlier_groups(summed)

    def queries(name, chosen, *made):
        return pl.pallas_call(
            functools.partial(query_kernel, chosen),
            out_shape=(
                jax.ShapeDtypeStruct((rows, heads * HEAD_WIDTH), bf16),
                jax.ShapeDtypeStruct((rows, heads * narrow), bf16),
            ),
            in_specs=[VMEM] * 8 + [HBM] * len(made),
            out_specs=[HBM, HBM],
            input_output_aliases={8 + i: i for i in range(len(made))},
            scratch_shapes=[
                pltpu.VMEM((3 * rows, wide), bf16),
                pltpu.VMEM((rows + half, wide), bf16),
                pltpu.VMEM((2, 2, span, wide), bf16),
                pltpu.VMEM((rows, heads * HEAD_WIDTH), bf16),
                pltpu.VMEM((rows, heads * narrow), bf16),
                pltpu.SemaphoreType.DMA((quads, 2)),
            ],
            compiler_params=params(16),
            cost_estimate=cost(3 * total * rows * width, 8 * MIB),
            name=name,
        )(wrapped[0], wrapped[1], plain[0], plain[1], own, mine, other, key_up_weight, *made)

    cut = quads - (quads + 2) // 3
    d_q_nope, d_q_rope = queries("query", range(cut))
    arrived, d_q_nope = lax.optimization_barrier((arrived, d_q_nope))
    partial = pl.pallas_call(
        sum_kernel,
        out_shape=jax.ShapeDtypeStruct((rows, wide), f32),
        in_specs=[VMEM] * 4,
        out_specs=VMEM,
        compiler_params=params(4),
        name="gather",
    )(grad, arrived, end_near, end_far)

    sharers = lax.axis_size("head")
    bit = 1
    while 2 * bit < sharers:
        partial = partial + with_partner(partial, bit)
        bit *= 2
    counterpart = with_partner(partial, bit)
    d_q_nope, d_q_rope = queries("query_rest", range(cut, quads), d_q_nope, d_q_rope)
    counterpart, d_q_nope = lax.optimization_barrier((counterpart, d_q_nope))
    latent_gradient, d_k_rope = pl.pallas_call(
        finish_kernel,
        out_shape=(
            jax.ShapeDtypeStruct((rows, width), f32),
            jax.ShapeDtypeStruct((narrow, rows), f32),
        ),
        in_specs=[VMEM] * 2,
        out_specs=[VMEM] * 2,
        compiler_params=params(4),
        name="finish",
    )(partial, counterpart)
    return d_q_nope, d_q_rope, latent_gradient, jnp.transpose(d_k_rope)


def solution(mesh):
    placed = (
        P("ctx", "head"),
        P("ctx", "head"),
        P("ctx", None),
        P("ctx", None),
        P("ctx", "head"),
        P("ctx", "head"),
        P("ctx", "head"),
        P(None, "head"),
        P(None, "head"),
    )
    return jax.shard_map(
        per_device,
        mesh=mesh,
        in_specs=placed,
        out_specs=(P("ctx", "head"), P("ctx", "head"), P("ctx", None), P("ctx", None)),
        check_vma=False,
    )
```

```python
import functools

import jax
import jax.numpy as jnp
from jax import lax
from jax.experimental import pallas as pl
from jax.experimental.pallas import tpu as pltpu
from jax.sharding import PartitionSpec as P

HEAD_WIDTH = 128
HOPS = 3
GROUP = 4
SLOTS = 4
AHEAD = 2 * (HOPS - 1)
MIB = 1 << 20

NT = (((1,), (1,)), ((), ()))
TN = (((0,), (0,)), ((), ()))


def dot(a, b, dims=(((1,), (0,)), ((), ()))):
    return lax.dot_general(a, b, dims, preferred_element_type=jnp.float32)


def to_later_groups(block):
    groups, sharers = lax.axis_size("ctx"), lax.axis_size("head")
    route = []
    for group in range(groups):
        for head in range(sharers):
            to = (group + 1 + head % 2) % groups
            route.append((group * sharers + head, to * sharers + head))
    return lax.ppermute(block, ("ctx", "head"), route)


def to_earlier(block, distance):
    groups = lax.axis_size("ctx")
    return lax.ppermute(block, "ctx", [(i, (i - distance) % groups) for i in range(groups)])


def with_partner(block, bit=1):
    return lax.ppermute(block, "head", [(i, i ^ bit) for i in range(lax.axis_size("head"))])


def params(limit_mib):
    return pltpu.CompilerParams(vmem_limit_bytes=limit_mib * MIB)


def cost(flops, moved):
    return pl.CostEstimate(flops=int(flops), bytes_accessed=int(moved), transcendentals=0)


def pack_kernel(lat_ref, rot_ref, out_ref):
    width = lat_ref.shape[1]
    rot = jnp.transpose(rot_ref[...].astype(jnp.float32)).astype(out_ref.dtype)
    out_ref[:, :width] = lat_ref[...]
    out_ref[:, width:] = jnp.concatenate([rot, rot], axis=1)


def project_kernel(
    nope_hbm, rope_hbm, dout_hbm, saved_hbm, wk_hbm, wv_hbm, rest_hbm,
    qx_ref, do_ref, stats_ref,
    nope, rope, dout, saved, wk, wv, flat_ref, sems, rest_sem,
):
    rows = nope.shape[0]
    width, total = wk.shape
    heads = total // HEAD_WIDTH
    quads = heads // GROUP
    half = rows // 2
    lanes = lax.broadcasted_iota(jnp.int32, (rows, HEAD_WIDTH), 1)
    arrays = (
        (wk_hbm, wk), (nope_hbm, nope), (wv_hbm, wv), (dout_hbm, dout), (saved_hbm, saved), (rope_hbm, rope),
    )

    def copies(quad):
        for i, (source, target) in enumerate(arrays):
            size = source.shape[1] // quads
            cols = slice(quad * size, (quad + 1) * size)
            yield pltpu.make_async_copy(source.at[:, cols], target.at[:, cols], sems.at[quad, i])

    for quad in range(quads):
        for copy in copies(quad):
            copy.start()
    rest_copy = pltpu.make_async_copy(rest_hbm, flat_ref.at[0, pl.ds(0, heads)], rest_sem)
    rest_copy.start()
    found = jnp.zeros((rows, HEAD_WIDTH), jnp.float32)
    for quad in range(quads):
        for copy in copies(quad):
            copy.wait()
        for g in range(GROUP):
            at = quad * GROUP + g
            cols = slice(at * HEAD_WIDTH, (at + 1) * HEAD_WIDTH)
            place = slice(g * half, (g + 1) * half)
            d_out = dout[:, cols]
            q_abs = dot(nope[:, cols], wk[:, cols], NT).astype(jnp.bfloat16)
            d_lat = dot(d_out, wv[:, cols], NT).astype(jnp.bfloat16)
            pair = rope[:, (at // 2) * HEAD_WIDTH : (at // 2 + 1) * HEAD_WIDTH]
            mine = (lanes < HEAD_WIDTH // 2) if g % 2 == 0 else (lanes >= HEAD_WIDTH // 2)
            pair = jnp.where(mine, pair, jnp.zeros_like(pair))
            for late, part in ((0, slice(0, half)), (1, slice(half, rows))):
                qx_ref[late, quad, place, :width] = q_abs[part]
                qx_ref[late, quad, place, width:] = pair[part]
                do_ref[late, quad, place] = d_lat[part]
            prod = d_out.astype(jnp.float32) * saved[:, cols].astype(jnp.float32)
            delta = jnp.sum(prod, axis=1, keepdims=True)
            found = jnp.where(lanes == at, delta, found)
    rest_copy.wait()
    flat_ref[1] = jnp.transpose(found)
    low = lax.broadcasted_iota(jnp.int32, (heads // 2, rows), 1) < half
    for kind in range(2):
        even = flat_ref[kind, pl.ds(0, heads // 2, 2), :]
        odd = flat_ref[kind, pl.ds(1, heads // 2, 2), :]
        stats_ref[2 * kind] = jnp.where(low, even, pltpu.roll(odd, half, 1))
        stats_ref[2 * kind + 1] = jnp.where(low, pltpu.roll(even, half, 1), odd)


def place_keys(keys_ref, mine_ref, other_ref):
    half = mine_ref.shape[0] // 2
    even = lax.axis_index("head") % 2 == 0

    def place(near, far):
        for at, (ref, start) in enumerate(((near, 0), (far, 0), (far, half), (near, half))):
            keys_ref[at * half : (at + 1) * half] = ref[start : start + half]

    @pl.when(even)
    def _():
        place(mine_ref, other_ref)

    @pl.when(jnp.logical_not(even))
    def _():
        place(other_ref, mine_ref)


def weigh_quad(scale, rest_of, delta_of, parts, span, lane_tile, start, ds_ref, pt_ref):
    for i in range(span // lane_tile):
        lanes = slice(i * lane_tile, (i + 1) * lane_tile)
        rest, delta = rest_of(i), delta_of(i)
        met = [part(lanes) for part in parts]
        top = rest
        for s, _ in met:
            top = jnp.maximum(top, jnp.max(s, axis=0, keepdims=True))
        exps = [jnp.exp(s - top) for s, _ in met]
        mass = jnp.exp(rest - top)
        for e in exps:
            mass = mass + jnp.sum(e, axis=0, keepdims=True)
        inverse = 1.0 / mass
        cols = slice(start + i * lane_tile, start + (i + 1) * lane_tile)
        at = 0
        for e, (_, p) in zip(exps, met):
            prob = e * inverse
            place = slice(at, at + e.shape[0])
            pt_ref[place, cols] = prob.astype(jnp.bfloat16)
            ds_ref[place, cols] = (prob * (p - delta) * scale).astype(jnp.bfloat16)
            at += e.shape[0]


def key_terms(qx_ref, do_ref, late, picked, ds_ref, pt_ref):
    quads, span, wide = qx_ref.shape[1:]
    width = do_ref.shape[3]
    q = qx_ref[late].reshape(quads * span, wide)
    d = do_ref[late].reshape(quads * span, width)
    lat = dot(ds_ref[picked], q[:, :width]) + dot(pt_ref[picked], d)
    return lat, dot(ds_ref[picked], q[:, width:])


def put(ref, place, terms, picked):
    width = terms[0].shape[1]
    ref[place, :width] = terms[0][picked].astype(ref.dtype)
    ref[place, width:] = terms[1][picked].astype(ref.dtype)


def scores_kernel(
    scale, qx_ref, do_ref, stats_ref, own_ref, mine_ref, other_ref,
    dsl_ref, dse_ref, ptl_ref, pte_ref, near_ref, far_ref, keys_ref, first_ref, s_ref, p_ref,
):
    rank = lax.axis_index("ctx")
    quads, span, _ = qx_ref.shape[1:]
    width = do_ref.shape[3]
    rows = own_ref.shape[0]
    half = rows // 2
    place_keys(keys_ref.at[pl.ds(rows, 2 * rows)], mine_ref, other_ref)
    keys_ref[:rows] = own_ref[...]
    first_ref[:half] = own_ref[:half]
    first_ref[half:] = keys_ref[rows : 2 * rows]
    key = lax.broadcasted_iota(jnp.int32, (half, rows), 0)
    causal = key <= lax.broadcasted_iota(jnp.int32, (half, rows), 1) % half

    def multiply(slot, late, quad, count):
        keys = keys_ref if late else first_ref
        s_ref[slot, :count] = dot(keys[:count], qx_ref[late, quad], NT)
        p_ref[slot, :count] = dot(keys[:count, :width], do_ref[late, quad], NT)

    def weigh(slot, late, quad, count):
        ds_ref, pt_ref = (dsl_ref, ptl_ref) if late else (dse_ref, pte_ref)
        tiles = span // rows
        diagonal = half if late else 0

        def plain(start, stop):
            return lambda lanes: (s_ref[slot, start:stop, lanes] * scale, p_ref[slot, start:stop, lanes])

        def masked(lanes):
            s, p = plain(diagonal, diagonal + half)(lanes)
            return jnp.where(causal, s, -jnp.inf), p

        parts = [plain(0, half)] if late else []
        parts.append(masked)
        if count > diagonal + half:
            parts.append(plain(diagonal + half, count))
        weigh_quad(
            scale,
            lambda i: stats_ref[late, tiles * quad + i : tiles * quad + i + 1],
            lambda i: stats_ref[2 + late, tiles * quad + i : tiles * quad + i + 1],
            parts, span, rows, quad * span, ds_ref, pt_ref,
        )

    def run(late_count, early_count):
        items = []
        for quad in range(quads):
            items.append((1, quad, rows + late_count))
            items.append((0, quad, half + early_count))
        multiply(0, *items[0])
        for i, item in enumerate(items):
            if i + 1 < len(items):
                multiply((i + 1) % SLOTS, *items[i + 1])
            weigh(i % SLOTS, *item)

    first, second = slice(0, half), slice(half, rows)
    terms = functools.partial(key_terms, qx_ref, do_ref)

    @pl.when(rank >= HOPS - 1)
    def _():
        run(rows, rows)
        late = terms(1, pl.ds(rows, rows), dsl_ref, ptl_ref)
        early = terms(0, pl.ds(half, rows), dse_ref, pte_ref)
        both = (late[0] + early[0], late[1] + early[1])
        put(near_ref, first, both, first)
        put(far_ref, first, both, second)
        for ref in (near_ref, far_ref):
            ref[second] = jnp.zeros_like(ref[second])

    @pl.when(jnp.logical_and(rank >= HOPS - 1, rank < AHEAD))
    def _():
        dsl_ref[2 * rows :] = jnp.zeros_like(dsl_ref[2 * rows :])

    @pl.when(rank == 1)
    def _():
        dse_ref[rows:] = jnp.zeros_like(dse_ref[rows:])
        dsl_ref[2 * rows + half :] = jnp.zeros_like(dsl_ref[2 * rows + half :])
        run(rows + half, half)
        late = terms(1, pl.ds(rows, rows + half), dsl_ref, ptl_ref)
        early = terms(0, pl.ds(half, half), dse_ref, pte_ref)
        put(near_ref, first, (late[0][first] + early[0], late[1][first] + early[1]), first)
        put(far_ref, first, late, second)
        put(far_ref, second, late, slice(rows, rows + half))
        near_ref[second] = jnp.zeros_like(near_ref[second])

    @pl.when(rank == 0)
    def _():
        dse_ref[half:] = jnp.zeros_like(dse_ref[half:])
        run(2 * rows, 0)
        late = terms(1, pl.ds(rows, 2 * rows), dsl_ref, ptl_ref)
        put(near_ref, first, late, first)
        put(far_ref, first, late, second)
        put(far_ref, second, late, slice(rows, rows + half))
        put(near_ref, second, late, slice(rows + half, 2 * rows))


def query_kernel(
    early_kernel, qx_ref, do_ref, dsl_ref, dse_ref, ptl_ref, pte_ref, own_ref, mine_ref, other_ref, wk_ref,
    *rest,
):
    dnope_hbm, drope_hbm, grad_ref, keys_ref, first_ref, dq_ref, dnope, drope, sems = rest[-9:]
    rank = lax.axis_index("ctx")
    rows, wide = own_ref.shape
    width = wk_ref.shape[0]
    half = rows // 2
    span = GROUP * half
    quads = dsl_ref.shape[1] // span
    lanes = lax.broadcasted_iota(jnp.int32, (rows, HEAD_WIDTH), 1)
    some = range(quads // 4)

    def prepare():
        place_keys(keys_ref.at[pl.ds(rows, 2 * rows)], mine_ref, other_ref)
        keys_ref[:rows] = own_ref[...]
        first_ref[:half] = own_ref[:half]
        first_ref[half:] = keys_ref[rows : 2 * rows]

    def copies(quad):
        for i, (source, target) in enumerate(((dnope, dnope_hbm), (drope, drope_hbm))):
            size = source.shape[1] // quads
            cols = slice(quad * size, (quad + 1) * size)
            yield pltpu.make_async_copy(source.at[:, cols], target.at[:, cols], sems.at[quad, i])

    def meet(quad, late_count):
        cols = slice(quad * span, (quad + 1) * span)
        slot = quad % 2
        late = dot(dsl_ref[:late_count, cols], keys_ref[:late_count], TN)
        early = dot(dse_ref[:, cols], first_ref[...], TN)
        dq_ref[slot, 1] = late.astype(jnp.bfloat16)
        dq_ref[slot, 0] = early.astype(jnp.bfloat16)

    def leave(quad):
        slot = quad % 2

        def head(g, place):
            mine = slice(g * half, (g + 1) * half)
            return jnp.concatenate([dq_ref[slot, 0, mine, place], dq_ref[slot, 1, mine, place]], axis=0)

        for g in range(GROUP):
            at = quad * GROUP + g
            out = slice(at * HEAD_WIDTH, (at + 1) * HEAD_WIDTH)
            dnope[:, out] = dot(head(g, slice(0, width)), wk_ref[:, out]).astype(jnp.bfloat16)
            if g % 2 == 1:
                both = slice(width, wide)
                pair = jnp.where(lanes < HEAD_WIDTH // 2, head(g - 1, both), head(g, both))
                drope[:, (at // 2) * HEAD_WIDTH : (at // 2 + 1) * HEAD_WIDTH] = pair
        for copy in copies(quad):
            copy.start()

    def run(late_count, chosen):
        meet(chosen[0], late_count)
        for quad in chosen:
            if quad + 1 in chosen:
                meet(quad + 1, late_count)
            leave(quad)

    def finish(chosen):
        for quad in chosen:
            for copy in copies(quad):
                copy.wait()

    def own_terms():
        first, second = slice(0, half), slice(half, rows)
        late = key_terms(qx_ref, do_ref, 1, pl.ds(0, rows), dsl_ref, ptl_ref)
        early = key_terms(qx_ref, do_ref, 0, pl.ds(0, half), dse_ref, pte_ref)
        put(grad_ref, first, (late[0][first] + early[0], late[1][first] + early[1]), first)
        put(grad_ref, second, late, second)

    if early_kernel:

        @pl.when(rank < AHEAD)
        def _():
            prepare()

            @pl.when(rank == 0)
            def _():
                run(3 * rows, some)

            @pl.when(rank > 0)
            def _():
                run(3 * rows, range(quads))

            own_terms()
            finish(some)

            @pl.when(rank > 0)
            def _():
                finish(range(len(some), quads))

    else:

        @pl.when(rank == 0)
        def _():
            prepare()
            run(3 * rows, range(len(some), quads))

        @pl.when(rank < AHEAD)
        def _():
            grad_ref[...] = rest[2][...]

        @pl.when(rank == 0)
        def _():
            finish(range(len(some), quads))

        @pl.when(rank >= AHEAD)
        def _():
            prepare()
            run(2 * rows, range(quads))
            own_terms()
            finish(range(quads))


def sum_kernel(own_ref, near_ref, far_ref, out_ref):
    out_ref[...] = own_ref[...] + (near_ref[...].astype(jnp.float32) + far_ref[...].astype(jnp.float32))


def finish_kernel(mine_ref, other_ref, lat_ref, rot_ref):
    width = lat_ref.shape[1]
    narrow = rot_ref.shape[0]
    total = mine_ref[...] + other_ref[...]
    lat_ref[...] = total[:, :width]
    rot_ref[...] = jnp.transpose(total[:, width : width + narrow] + total[:, width + narrow :])


VMEM = pl.BlockSpec(memory_space=pltpu.VMEM)
HBM = pl.BlockSpec(memory_space=pltpu.HBM)


def in_hbm(*arrays):
    return [pltpu.with_memory_space_constraint(array, pltpu.HBM) for array in arrays]


def per_device(
    q_nope, q_rope, latent, k_rope, d_out, out_heads, lse_rest, key_up_weight, value_up_weight
):
    rows, width = latent.shape
    narrow = k_rope.shape[1]
    wide = width + 2 * narrow
    half = rows // 2
    heads = key_up_weight.shape[1] // HEAD_WIDTH
    quads, span = heads // GROUP, GROUP * half
    scale = (HEAD_WIDTH + narrow) ** (-0.5)
    bf16, f32 = jnp.bfloat16, jnp.float32
    total = heads * rows

    own = pl.pallas_call(
        pack_kernel,
        out_shape=jax.ShapeDtypeStruct((rows, wide), bf16),
        in_specs=[VMEM, VMEM],
        out_specs=VMEM,
        compiler_params=params(4),
        name="pack",
    )(*in_hbm(latent, jnp.transpose(k_rope)))
    mine = to_later_groups(own)

    qx, do_lat, stats = pl.pallas_call(
        project_kernel,
        out_shape=(
            pltpu.VMEM((2, quads, span, wide), bf16),
            pltpu.VMEM((2, quads, span, width), bf16),
            pltpu.VMEM((4, heads // 2, rows), f32),
        ),
        in_specs=[HBM] * 7,
        out_specs=[VMEM] * 3,
        scratch_shapes=[
            pltpu.VMEM(q_nope.shape, bf16),
            pltpu.VMEM(q_rope.shape, bf16),
            pltpu.VMEM(d_out.shape, bf16),
            pltpu.VMEM(out_heads.shape, bf16),
            pltpu.VMEM(key_up_weight.shape, bf16),
            pltpu.VMEM(value_up_weight.shape, bf16),
            pltpu.VMEM((2, HEAD_WIDTH, rows), f32),
            pltpu.SemaphoreType.DMA((quads, 6)),
            pltpu.SemaphoreType.DMA,
        ],
        compiler_params=params(20),
        cost_estimate=cost(4 * total * HEAD_WIDTH * width, 12 * MIB),
        name="project",
    )(
        *in_hbm(
            q_nope, q_rope, d_out, out_heads, key_up_weight, value_up_weight, jnp.transpose(lse_rest)
        )
    )
    mine, stats = lax.optimization_barrier((mine, stats))
    other = with_partner(mine)

    late = pltpu.VMEM((3 * rows, quads * span), bf16)
    early = pltpu.VMEM((rows + half, quads * span), bf16)
    slots = pltpu.VMEM((SLOTS, 3 * rows, span), f32)
    *terms, to_near, to_far = pl.pallas_call(
        functools.partial(scores_kernel, scale),
        out_shape=(late, early, late, early) + (jax.ShapeDtypeStruct((rows, wide), bf16),) * 2,
        in_specs=[VMEM] * 6,
        out_specs=[VMEM] * 6,
        scratch_shapes=[
            pltpu.VMEM((3 * rows, wide), bf16),
            pltpu.VMEM((rows + half, wide), bf16),
            slots,
            slots,
        ],
        compiler_params=params(16),
        cost_estimate=cost(8 * total * rows * width, 16 * MIB),
        name="scores",
    )(qx, do_lat, stats, own, mine, other)
    def queries(early_kernel, *made):
        return pl.pallas_call(
            functools.partial(query_kernel, early_kernel),
            out_shape=(
                jax.ShapeDtypeStruct((rows, heads * HEAD_WIDTH), bf16),
                jax.ShapeDtypeStruct((rows, heads * narrow), bf16),
                pltpu.VMEM((rows, wide), f32),
            ),
            in_specs=[VMEM] * 10 + ([HBM, HBM, VMEM] if made else []),
            out_specs=[HBM, HBM, VMEM],
            input_output_aliases={10: 0, 11: 1} if made else {},
            scratch_shapes=[
                pltpu.VMEM((3 * rows, wide), bf16),
                pltpu.VMEM((rows + half, wide), bf16),
                pltpu.VMEM((2, 2, span, wide), bf16),
                pltpu.VMEM((rows, heads * HEAD_WIDTH), bf16),
                pltpu.VMEM((rows, heads * narrow), bf16),
                pltpu.SemaphoreType.DMA((quads, 2)),
            ],
            compiler_params=params(16),
            cost_estimate=cost(MIB, MIB) if early_kernel else cost(10 * total * rows * width, 16 * MIB),
            name="query_early" if early_kernel else "query",
        )(qx, do_lat, *terms, own, mine, other, key_up_weight, *made)

    made = queries(True)
    to_near, to_far, grad = lax.optimization_barrier((to_near, to_far, made[2]))
    from_near = to_earlier(to_near, 1)
    from_far = to_earlier(to_far, 2)
    d_q_nope, d_q_rope, grad = queries(False, made[0], made[1], grad)

    partial = pl.pallas_call(
        sum_kernel,
        out_shape=jax.ShapeDtypeStruct((rows, wide), f32),
        in_specs=[VMEM] * 3,
        out_specs=VMEM,
        compiler_params=params(4),
        name="gather",
    )(grad, from_near, from_far)

    sharers = lax.axis_size("head")
    bit = 1
    while 2 * bit < sharers:
        partial = partial + with_partner(partial, bit)
        bit *= 2
    counterpart = with_partner(partial, bit)
    latent_gradient, d_k_rope = pl.pallas_call(
        finish_kernel,
        out_shape=(
            jax.ShapeDtypeStruct((rows, width), f32),
            jax.ShapeDtypeStruct((narrow, rows), f32),
        ),
        in_specs=[VMEM] * 2,
        out_specs=[VMEM] * 2,
        compiler_params=params(4),
        name="finish",
    )(partial, counterpart)
    return d_q_nope, d_q_rope, latent_gradient, jnp.transpose(d_k_rope)


def solution(mesh):
    placed = (
        P("ctx", "head"),
        P("ctx", "head"),
        P("ctx", None),
        P("ctx", None),
        P("ctx", "head"),
        P("ctx", "head"),
        P("ctx", "head"),
        P(None, "head"),
        P(None, "head"),
    )
    return jax.shard_map(
        per_device,
        mesh=mesh,
        in_specs=placed,
        out_specs=(P("ctx", "head"), P("ctx", "head"), P("ctx", None), P("ctx", None)),
        check_vma=False,
    )
```

```python
import functools

import jax
import jax.numpy as jnp
from jax import lax
from jax.experimental import pallas as pl
from jax.experimental.pallas import tpu as pltpu
from jax.sharding import PartitionSpec as P

HEAD_WIDTH = 128
HOPS = 3
GROUP = 4
SLOTS = 4
MIB = 1 << 20

NT = (((1,), (1,)), ((), ()))
TN = (((0,), (0,)), ((), ()))


def dot(a, b, dims=(((1,), (0,)), ((), ()))):
    return lax.dot_general(a, b, dims, preferred_element_type=jnp.float32)


def between_groups(block, direction):
    groups, sharers = lax.axis_size("ctx"), lax.axis_size("head")
    route = []
    for group in range(groups):
        for head in range(sharers):
            to = (group + direction * (1 + head % 2)) % groups
            route.append((group * sharers + head, to * sharers + head))
    return lax.ppermute(block, ("ctx", "head"), route)


def with_partner(block, bit=1):
    return lax.ppermute(block, "head", [(i, i ^ bit) for i in range(lax.axis_size("head"))])


def params(limit_mib):
    return pltpu.CompilerParams(vmem_limit_bytes=limit_mib * MIB)


def cost(flops, moved):
    return pl.CostEstimate(flops=int(flops), bytes_accessed=int(moved), transcendentals=0)


def pack_kernel(lat_ref, rot_ref, out_ref):
    width = lat_ref.shape[1]
    rot = jnp.transpose(rot_ref[...].astype(jnp.float32)).astype(out_ref.dtype)
    out_ref[:, :width] = lat_ref[...]
    out_ref[:, width:] = jnp.concatenate([rot, rot], axis=1)


def project_kernel(
    nope_hbm, rope_hbm, dout_hbm, saved_hbm, wk_hbm, wv_hbm, rest_hbm,
    qx_ref, do_ref, stats_ref,
    nope, rope, dout, saved, wk, wv, flat_ref, sems, rest_sem,
):
    rows = nope.shape[0]
    width, total = wk.shape
    heads = total // HEAD_WIDTH
    quads = heads // GROUP
    half = rows // 2
    lanes = lax.broadcasted_iota(jnp.int32, (rows, HEAD_WIDTH), 1)
    arrays = (
        (wk_hbm, wk), (nope_hbm, nope), (wv_hbm, wv), (dout_hbm, dout), (saved_hbm, saved), (rope_hbm, rope),
    )

    def copies(quad):
        for i, (source, target) in enumerate(arrays):
            size = source.shape[1] // quads
            cols = slice(quad * size, (quad + 1) * size)
            yield pltpu.make_async_copy(source.at[:, cols], target.at[:, cols], sems.at[quad, i])

    for quad in range(quads):
        for copy in copies(quad):
            copy.start()
    rest_copy = pltpu.make_async_copy(rest_hbm, flat_ref.at[0, pl.ds(0, heads)], rest_sem)
    rest_copy.start()
    found = jnp.zeros((rows, HEAD_WIDTH), jnp.float32)
    for quad in range(quads):
        for copy in copies(quad):
            copy.wait()
        for g in range(GROUP):
            at = quad * GROUP + g
            cols = slice(at * HEAD_WIDTH, (at + 1) * HEAD_WIDTH)
            place = slice(g * half, (g + 1) * half)
            d_out = dout[:, cols]
            q_abs = dot(nope[:, cols], wk[:, cols], NT).astype(jnp.bfloat16)
            d_lat = dot(d_out, wv[:, cols], NT).astype(jnp.bfloat16)
            pair = rope[:, (at // 2) * HEAD_WIDTH : (at // 2 + 1) * HEAD_WIDTH]
            mine = (lanes < HEAD_WIDTH // 2) if g % 2 == 0 else (lanes >= HEAD_WIDTH // 2)
            pair = jnp.where(mine, pair, jnp.zeros_like(pair))
            for late, part in ((0, slice(0, half)), (1, slice(half, rows))):
                qx_ref[late, quad, place, :width] = q_abs[part]
                qx_ref[late, quad, place, width:] = pair[part]
                do_ref[late, quad, place] = d_lat[part]
            prod = d_out.astype(jnp.float32) * saved[:, cols].astype(jnp.float32)
            delta = jnp.sum(prod, axis=1, keepdims=True)
            found = jnp.where(lanes == at, delta, found)
    rest_copy.wait()
    flat_ref[1] = jnp.transpose(found)
    low = lax.broadcasted_iota(jnp.int32, (heads // 2, rows), 1) < half
    for kind in range(2):
        even = flat_ref[kind, pl.ds(0, heads // 2, 2), :]
        odd = flat_ref[kind, pl.ds(1, heads // 2, 2), :]
        stats_ref[2 * kind] = jnp.where(low, even, pltpu.roll(odd, half, 1))
        stats_ref[2 * kind + 1] = jnp.where(low, pltpu.roll(even, half, 1), odd)


def place_keys(keys_ref, mine_ref, other_ref):
    half = mine_ref.shape[0] // 2
    even = lax.axis_index("head") % 2 == 0

    def place(near, far):
        for at, (ref, start) in enumerate(((near, 0), (far, 0), (far, half), (near, half))):
            keys_ref[at * half : (at + 1) * half] = ref[start : start + half]

    @pl.when(even)
    def _():
        place(mine_ref, other_ref)

    @pl.when(jnp.logical_not(even))
    def _():
        place(other_ref, mine_ref)


def weigh_quad(scale, rest_of, delta_of, parts, span, lane_tile, start, ds_ref, pt_ref):
    for i in range(span // lane_tile):
        lanes = slice(i * lane_tile, (i + 1) * lane_tile)
        rest, delta = rest_of(i), delta_of(i)
        met = [part(lanes) for part in parts]
        top = rest
        for s, _ in met:
            top = jnp.maximum(top, jnp.max(s, axis=0, keepdims=True))
        exps = [jnp.exp(s - top) for s, _ in met]
        mass = jnp.exp(rest - top)
        for e in exps:
            mass = mass + jnp.sum(e, axis=0, keepdims=True)
        inverse = 1.0 / mass
        cols = slice(start + i * lane_tile, start + (i + 1) * lane_tile)
        at = 0
        for e, (_, p) in zip(exps, met):
            prob = e * inverse
            place = slice(at, at + e.shape[0])
            pt_ref[place, cols] = prob.astype(jnp.bfloat16)
            ds_ref[place, cols] = (prob * (p - delta) * scale).astype(jnp.bfloat16)
            at += e.shape[0]


def key_terms(qx_ref, do_ref, late, picked, ds_ref, pt_ref):
    quads, span, wide = qx_ref.shape[1:]
    width = do_ref.shape[3]
    q = qx_ref[late].reshape(quads * span, wide)
    d = do_ref[late].reshape(quads * span, width)
    lat = dot(ds_ref[picked], q[:, :width]) + dot(pt_ref[picked], d)
    return lat, dot(ds_ref[picked], q[:, width:])


def put(ref, place, terms, picked):
    width = terms[0].shape[1]
    ref[place, :width] = terms[0][picked].astype(ref.dtype)
    ref[place, width:] = terms[1][picked].astype(ref.dtype)


def scores_kernel(
    scale, qx_ref, do_ref, stats_ref, own_ref, mine_ref, other_ref,
    dsl_ref, dse_ref, ptl_ref, pte_ref, keep_ref, give_ref, keys_ref, first_ref, s_ref, p_ref,
):
    rank = lax.axis_index("ctx")
    quads, span, _ = qx_ref.shape[1:]
    width = do_ref.shape[3]
    rows = own_ref.shape[0]
    half = rows // 2
    place_keys(keys_ref.at[pl.ds(rows, 2 * rows)], mine_ref, other_ref)
    keys_ref[:rows] = own_ref[...]
    first_ref[:half] = own_ref[:half]
    first_ref[half:] = keys_ref[rows : 2 * rows]
    key = lax.broadcasted_iota(jnp.int32, (half, rows), 0)
    causal = key <= lax.broadcasted_iota(jnp.int32, (half, rows), 1) % half

    def multiply(slot, late, quad, count):
        keys = keys_ref if late else first_ref
        s_ref[slot, :count] = dot(keys[:count], qx_ref[late, quad], NT)
        p_ref[slot, :count] = dot(keys[:count, :width], do_ref[late, quad], NT)

    def weigh(slot, late, quad, count):
        ds_ref, pt_ref = (dsl_ref, ptl_ref) if late else (dse_ref, pte_ref)
        tiles = span // rows
        diagonal = half if late else 0

        def plain(start, stop):
            return lambda lanes: (s_ref[slot, start:stop, lanes] * scale, p_ref[slot, start:stop, lanes])

        def masked(lanes):
            s, p = plain(diagonal, diagonal + half)(lanes)
            return jnp.where(causal, s, -jnp.inf), p

        parts = [plain(0, half)] if late else []
        parts.append(masked)
        if count > diagonal + half:
            parts.append(plain(diagonal + half, count))
        weigh_quad(
            scale,
            lambda i: stats_ref[late, tiles * quad + i : tiles * quad + i + 1],
            lambda i: stats_ref[2 + late, tiles * quad + i : tiles * quad + i + 1],
            parts, span, rows, quad * span, ds_ref, pt_ref,
        )

    def run(late_count, early_count):
        items = []
        for quad in range(quads):
            items.append((1, quad, rows + late_count))
            items.append((0, quad, half + early_count))
        multiply(0, *items[0])
        for i, item in enumerate(items):
            if i + 1 < len(items):
                multiply((i + 1) % SLOTS, *items[i + 1])
            weigh(i % SLOTS, *item)

    first, second = slice(0, half), slice(half, rows)
    terms = functools.partial(key_terms, qx_ref, do_ref)

    even = lax.axis_index("head") % 2 == 0

    def share(place, of, near, far):
        @pl.when(even)
        def _():
            put(keep_ref, place, of, near)
            put(give_ref, place, of, far)

        @pl.when(jnp.logical_not(even))
        def _():
            put(keep_ref, place, of, far)
            put(give_ref, place, of, near)

    @pl.when(rank >= HOPS - 1)
    def _():
        run(rows, rows)
        late = terms(1, pl.ds(rows, rows), dsl_ref, ptl_ref)
        early = terms(0, pl.ds(half, rows), dse_ref, pte_ref)
        share(first, (late[0] + early[0], late[1] + early[1]), first, second)
        for ref in (keep_ref, give_ref):
            ref[second] = jnp.zeros_like(ref[second])

    @pl.when(rank == 1)
    def _():
        dse_ref[rows:] = jnp.zeros_like(dse_ref[rows:])
        dsl_ref[2 * rows + half :] = jnp.zeros_like(dsl_ref[2 * rows + half :])
        run(rows + half, half)
        late = terms(1, pl.ds(rows, rows + half), dsl_ref, ptl_ref)
        early = terms(0, pl.ds(half, half), dse_ref, pte_ref)
        seconds = slice(rows, rows + half)
        both = tuple(
            jnp.concatenate([a[first] + b, a[second], a[seconds], jnp.zeros_like(b)], axis=0)
            for a, b in zip(late, early)
        )
        share(first, both, first, second)
        share(second, both, slice(rows + half, 2 * rows), seconds)

    @pl.when(rank == 0)
    def _():
        dse_ref[half:] = jnp.zeros_like(dse_ref[half:])
        run(2 * rows, 0)
        late = terms(1, pl.ds(rows, 2 * rows), dsl_ref, ptl_ref)
        share(first, late, first, second)
        share(second, late, slice(rows + half, 2 * rows), slice(rows, rows + half))


def own_kernel(qx_ref, do_ref, dsl_ref, dse_ref, ptl_ref, pte_ref, grad_ref):
    rows = grad_ref.shape[0]
    half = rows // 2
    first, second = slice(0, half), slice(half, rows)
    late = key_terms(qx_ref, do_ref, 1, pl.ds(0, rows), dsl_ref, ptl_ref)
    early = key_terms(qx_ref, do_ref, 0, pl.ds(0, half), dse_ref, pte_ref)
    put(grad_ref, first, (late[0][first] + early[0], late[1][first] + early[1]), first)
    put(grad_ref, second, late, second)


def pair_kernel(keep_ref, got_ref, out_ref):
    out_ref[...] = (keep_ref[...] + got_ref[...].astype(jnp.float32)).astype(out_ref.dtype)


def query_kernel(
    dsl_ref, dse_ref, own_ref, mine_ref, other_ref, wk_ref,
    dnope_hbm, drope_hbm, keys_ref, first_ref, dq_ref, dnope, drope, sems,
):
    rank = lax.axis_index("ctx")
    rows, wide = own_ref.shape
    width = wk_ref.shape[0]
    half = rows // 2
    span = GROUP * half
    quads = dsl_ref.shape[1] // span
    lanes = lax.broadcasted_iota(jnp.int32, (rows, HEAD_WIDTH), 1)
    place_keys(keys_ref.at[pl.ds(rows, 2 * rows)], mine_ref, other_ref)
    keys_ref[:rows] = own_ref[...]
    first_ref[:half] = own_ref[:half]
    first_ref[half:] = keys_ref[rows : 2 * rows]

    def copies(quad):
        for i, (source, target) in enumerate(((dnope, dnope_hbm), (drope, drope_hbm))):
            size = source.shape[1] // quads
            cols = slice(quad * size, (quad + 1) * size)
            yield pltpu.make_async_copy(source.at[:, cols], target.at[:, cols], sems.at[quad, i])

    def meet(quad, late_count):
        cols = slice(quad * span, (quad + 1) * span)
        slot = quad % 2
        late = dot(dsl_ref[:late_count, cols], keys_ref[:late_count], TN)
        early = dot(dse_ref[:, cols], first_ref[...], TN)
        dq_ref[slot, 1] = late.astype(jnp.bfloat16)
        dq_ref[slot, 0] = early.astype(jnp.bfloat16)

    def leave(quad):
        slot = quad % 2

        def head(g, place):
            mine = slice(g * half, (g + 1) * half)
            return jnp.concatenate([dq_ref[slot, 0, mine, place], dq_ref[slot, 1, mine, place]], axis=0)

        for g in range(GROUP):
            at = quad * GROUP + g
            out = slice(at * HEAD_WIDTH, (at + 1) * HEAD_WIDTH)
            dnope[:, out] = dot(head(g, slice(0, width)), wk_ref[:, out]).astype(jnp.bfloat16)
            if g % 2 == 1:
                both = slice(width, wide)
                pair = jnp.where(lanes < HEAD_WIDTH // 2, head(g - 1, both), head(g, both))
                drope[:, (at // 2) * HEAD_WIDTH : (at // 2 + 1) * HEAD_WIDTH] = pair
        for copy in copies(quad):
            copy.start()

    def run(late_count):
        meet(0, late_count)
        for quad in range(quads):
            if quad + 1 < quads:
                meet(quad + 1, late_count)
            leave(quad)

    @pl.when(rank >= HOPS - 1)
    def _():
        run(2 * rows)

    @pl.when(rank < HOPS - 1)
    def _():
        run(3 * rows)

    for quad in range(quads):
        for copy in copies(quad):
            copy.wait()


def sum_kernel(own_ref, got_ref, out_ref):
    out_ref[...] = own_ref[...] + got_ref[...].astype(jnp.float32)


def finish_kernel(mine_ref, other_ref, lat_ref, rot_ref):
    width = lat_ref.shape[1]
    narrow = rot_ref.shape[0]
    total = mine_ref[...] + other_ref[...]
    lat_ref[...] = total[:, :width]
    rot_ref[...] = jnp.transpose(total[:, width : width + narrow] + total[:, width + narrow :])


VMEM = pl.BlockSpec(memory_space=pltpu.VMEM)
HBM = pl.BlockSpec(memory_space=pltpu.HBM)


def in_hbm(*arrays):
    return [pltpu.with_memory_space_constraint(array, pltpu.HBM) for array in arrays]


def per_device(
    q_nope, q_rope, latent, k_rope, d_out, out_heads, lse_rest, key_up_weight, value_up_weight
):
    rows, width = latent.shape
    narrow = k_rope.shape[1]
    wide = width + 2 * narrow
    half = rows // 2
    heads = key_up_weight.shape[1] // HEAD_WIDTH
    quads, span = heads // GROUP, GROUP * half
    scale = (HEAD_WIDTH + narrow) ** (-0.5)
    bf16, f32 = jnp.bfloat16, jnp.float32
    total = heads * rows

    own = pl.pallas_call(
        pack_kernel,
        out_shape=jax.ShapeDtypeStruct((rows, wide), bf16),
        in_specs=[VMEM, VMEM],
        out_specs=VMEM,
        compiler_params=params(4),
        name="pack",
    )(*in_hbm(latent, jnp.transpose(k_rope)))
    mine = between_groups(own, 1)

    qx, do_lat, stats = pl.pallas_call(
        project_kernel,
        out_shape=(
            pltpu.VMEM((2, quads, span, wide), bf16),
            pltpu.VMEM((2, quads, span, width), bf16),
            pltpu.VMEM((4, heads // 2, rows), f32),
        ),
        in_specs=[HBM] * 7,
        out_specs=[VMEM] * 3,
        scratch_shapes=[
            pltpu.VMEM(q_nope.shape, bf16),
            pltpu.VMEM(q_rope.shape, bf16),
            pltpu.VMEM(d_out.shape, bf16),
            pltpu.VMEM(out_heads.shape, bf16),
            pltpu.VMEM(key_up_weight.shape, bf16),
            pltpu.VMEM(value_up_weight.shape, bf16),
            pltpu.VMEM((2, HEAD_WIDTH, rows), f32),
            pltpu.SemaphoreType.DMA((quads, 6)),
            pltpu.SemaphoreType.DMA,
        ],
        compiler_params=params(20),
        cost_estimate=cost(4 * total * HEAD_WIDTH * width, 12 * MIB),
        name="project",
    )(
        *in_hbm(
            q_nope, q_rope, d_out, out_heads, key_up_weight, value_up_weight, jnp.transpose(lse_rest)
        )
    )
    mine, stats = lax.optimization_barrier((mine, stats))
    other = with_partner(mine)

    late = pltpu.VMEM((3 * rows, quads * span), bf16)
    early = pltpu.VMEM((rows + half, quads * span), bf16)
    slots = pltpu.VMEM((SLOTS, 3 * rows, span), f32)
    *terms, keep, give = pl.pallas_call(
        functools.partial(scores_kernel, scale),
        out_shape=(
            late, early, late, early,
            jax.ShapeDtypeStruct((rows, wide), f32),
            jax.ShapeDtypeStruct((rows, wide), bf16),
        ),
        in_specs=[VMEM] * 6,
        out_specs=[VMEM] * 6,
        scratch_shapes=[
            pltpu.VMEM((3 * rows, wide), bf16),
            pltpu.VMEM((rows + half, wide), bf16),
            slots,
            slots,
        ],
        compiler_params=params(16),
        cost_estimate=cost(8 * total * rows * width, 16 * MIB),
        name="scores",
    )(qx, do_lat, stats, own, mine, other)
    got = with_partner(give)
    grad = pl.pallas_call(
        own_kernel,
        out_shape=jax.ShapeDtypeStruct((rows, wide), f32),
        in_specs=[VMEM] * 6,
        out_specs=VMEM,
        compiler_params=params(8),
        cost_estimate=cost(4 * total * rows * width, 16 * MIB),
        name="own",
    )(qx, do_lat, *terms)
    got, grad = lax.optimization_barrier((got, grad))
    summed = pl.pallas_call(
        pair_kernel,
        out_shape=jax.ShapeDtypeStruct((rows, wide), bf16),
        in_specs=[VMEM] * 2,
        out_specs=VMEM,
        compiler_params=params(4),
        name="pair",
    )(keep, got)
    arrived = between_groups(summed, -1)

    d_q_nope, d_q_rope = pl.pallas_call(
        query_kernel,
        out_shape=(
            jax.ShapeDtypeStruct((rows, heads * HEAD_WIDTH), bf16),
            jax.ShapeDtypeStruct((rows, heads * narrow), bf16),
        ),
        in_specs=[VMEM] * 6,
        out_specs=[HBM, HBM],
        scratch_shapes=[
            pltpu.VMEM((3 * rows, wide), bf16),
            pltpu.VMEM((rows + half, wide), bf16),
            pltpu.VMEM((2, 2, span, wide), bf16),
            pltpu.VMEM((rows, heads * HEAD_WIDTH), bf16),
            pltpu.VMEM((rows, heads * narrow), bf16),
            pltpu.SemaphoreType.DMA((quads, 2)),
        ],
        compiler_params=params(16),
        cost_estimate=cost(6 * total * rows * width, 16 * MIB),
        name="query",
    )(terms[0], terms[1], own, mine, other, key_up_weight)
    arrived, d_q_nope = lax.optimization_barrier((arrived, d_q_nope))

    partial = pl.pallas_call(
        sum_kernel,
        out_shape=jax.ShapeDtypeStruct((rows, wide), f32),
        in_specs=[VMEM] * 2,
        out_specs=VMEM,
        compiler_params=params(4),
        name="gather",
    )(grad, arrived)

    sharers = lax.axis_size("head")
    bit = 1
    while 2 * bit < sharers:
        partial = partial + with_partner(partial, bit)
        bit *= 2
    counterpart = with_partner(partial, bit)
    latent_gradient, d_k_rope = pl.pallas_call(
        finish_kernel,
        out_shape=(
            jax.ShapeDtypeStruct((rows, width), f32),
            jax.ShapeDtypeStruct((narrow, rows), f32),
        ),
        in_specs=[VMEM] * 2,
        out_specs=[VMEM] * 2,
        compiler_params=params(4),
        name="finish",
    )(partial, counterpart)
    return d_q_nope, d_q_rope, latent_gradient, jnp.transpose(d_k_rope)


def solution(mesh):
    placed = (
        P("ctx", "head"),
        P("ctx", "head"),
        P("ctx", None),
        P("ctx", None),
        P("ctx", "head"),
        P("ctx", "head"),
        P("ctx", "head"),
        P(None, "head"),
        P(None, "head"),
    )
    return jax.shard_map(
        per_device,
        mesh=mesh,
        in_specs=placed,
        out_specs=(P("ctx", "head"), P("ctx", "head"), P("ctx", None), P("ctx", None)),
        check_vma=False,
    )
```

```python
import functools

import jax
import jax.numpy as jnp
from jax import lax
from jax.experimental import pallas as pl
from jax.experimental.pallas import tpu as pltpu
from jax.sharding import PartitionSpec as P

HEAD_WIDTH = 128
HOPS = 3
GROUP = 4
SLOTS = 4
MIB = 1 << 20

NT = (((1,), (1,)), ((), ()))
TN = (((0,), (0,)), ((), ()))


def dot(a, b, dims=(((1,), (0,)), ((), ()))):
    return lax.dot_general(a, b, dims, preferred_element_type=jnp.float32)


def between_groups(block, direction):
    groups, sharers = lax.axis_size("ctx"), lax.axis_size("head")
    route = []
    for group in range(groups):
        for head in range(sharers):
            to = (group + direction * (1 + head % 2)) % groups
            route.append((group * sharers + head, to * sharers + head))
    return lax.ppermute(block, ("ctx", "head"), route)


def with_partner(block, bit=1):
    return lax.ppermute(block, "head", [(i, i ^ bit) for i in range(lax.axis_size("head"))])


def params(limit_mib):
    return pltpu.CompilerParams(vmem_limit_bytes=limit_mib * MIB)


def cost(flops, moved):
    return pl.CostEstimate(flops=int(flops), bytes_accessed=int(moved), transcendentals=0)


def pack_kernel(lat_ref, rot_ref, out_ref):
    width = lat_ref.shape[1]
    rot = jnp.transpose(rot_ref[...].astype(jnp.float32)).astype(out_ref.dtype)
    out_ref[:, :width] = lat_ref[...]
    out_ref[:, width:] = jnp.concatenate([rot, rot], axis=1)


def project_kernel(
    nope_hbm, rope_hbm, dout_hbm, saved_hbm, wk_hbm, wv_hbm, rest_hbm,
    qx_ref, do_ref, stats_ref,
    nope, rope, dout, saved, wk, wv, flat_ref, sems, rest_sem,
):
    rows = nope.shape[0]
    width, total = wk.shape
    heads = total // HEAD_WIDTH
    quads = heads // GROUP
    half = rows // 2
    lanes = lax.broadcasted_iota(jnp.int32, (rows, HEAD_WIDTH), 1)
    arrays = (
        (wk_hbm, wk), (nope_hbm, nope), (wv_hbm, wv), (dout_hbm, dout), (saved_hbm, saved), (rope_hbm, rope),
    )

    def copies(quad):
        for i, (source, target) in enumerate(arrays):
            size = source.shape[1] // quads
            cols = slice(quad * size, (quad + 1) * size)
            yield pltpu.make_async_copy(source.at[:, cols], target.at[:, cols], sems.at[quad, i])

    for quad in range(quads):
        for copy in copies(quad):
            copy.start()
    rest_copy = pltpu.make_async_copy(rest_hbm, flat_ref.at[0, pl.ds(0, heads)], rest_sem)
    rest_copy.start()
    found = jnp.zeros((rows, HEAD_WIDTH), jnp.float32)
    for quad in range(quads):
        due = range(quad, quad + 1) if quad < 2 else range(quad, min(quad + 2, quads)) if quad % 2 == 0 else ()
        for ready in due:
            for copy in copies(ready):
                copy.wait()
        for g in range(GROUP):
            at = quad * GROUP + g
            cols = slice(at * HEAD_WIDTH, (at + 1) * HEAD_WIDTH)
            place = slice(g * half, (g + 1) * half)
            d_out = dout[:, cols]
            q_abs = dot(nope[:, cols], wk[:, cols], NT).astype(jnp.bfloat16)
            d_lat = dot(d_out, wv[:, cols], NT).astype(jnp.bfloat16)
            pair = rope[:, (at // 2) * HEAD_WIDTH : (at // 2 + 1) * HEAD_WIDTH]
            mine = (lanes < HEAD_WIDTH // 2) if g % 2 == 0 else (lanes >= HEAD_WIDTH // 2)
            pair = jnp.where(mine, pair, jnp.zeros_like(pair))
            for late, part in ((0, slice(0, half)), (1, slice(half, rows))):
                qx_ref[late, quad, place, :width] = q_abs[part]
                qx_ref[late, quad, place, width:] = pair[part]
                do_ref[late, quad, place] = d_lat[part]
            prod = d_out.astype(jnp.float32) * saved[:, cols].astype(jnp.float32)
            delta = jnp.sum(prod, axis=1, keepdims=True)
            found = jnp.where(lanes == at, delta, found)
    rest_copy.wait()
    flat_ref[1] = jnp.transpose(found)
    low = lax.broadcasted_iota(jnp.int32, (heads // 2, rows), 1) < half
    for kind in range(2):
        even = flat_ref[kind, pl.ds(0, heads // 2, 2), :]
        odd = flat_ref[kind, pl.ds(1, heads // 2, 2), :]
        stats_ref[2 * kind] = jnp.where(low, even, pltpu.roll(odd, half, 1))
        stats_ref[2 * kind + 1] = jnp.where(low, pltpu.roll(even, half, 1), odd)


def place_keys(keys_ref, mine_ref, other_ref):
    half = mine_ref.shape[0] // 2
    even = lax.axis_index("head") % 2 == 0

    def place(near, far):
        for at, (ref, start) in enumerate(((near, 0), (far, 0), (far, half), (near, half))):
            keys_ref[at * half : (at + 1) * half] = ref[start : start + half]

    @pl.when(even)
    def _():
        place(mine_ref, other_ref)

    @pl.when(jnp.logical_not(even))
    def _():
        place(other_ref, mine_ref)


def weigh_quad(scale, rest_of, delta_of, parts, span, lane_tile, start, ds_ref, pt_ref):
    for i in range(span // lane_tile):
        lanes = slice(i * lane_tile, (i + 1) * lane_tile)
        rest, delta = rest_of(i), delta_of(i)
        met = [part(lanes) for part in parts]
        top = rest
        for s, _ in met:
            top = jnp.maximum(top, jnp.max(s, axis=0, keepdims=True))
        exps = [jnp.exp(s - top) for s, _ in met]
        mass = jnp.exp(rest - top)
        for e in exps:
            mass = mass + jnp.sum(e, axis=0, keepdims=True)
        inverse = 1.0 / mass
        cols = slice(start + i * lane_tile, start + (i + 1) * lane_tile)
        at = 0
        for e, (_, p) in zip(exps, met):
            prob = e * inverse
            place = slice(at, at + e.shape[0])
            pt_ref[place, cols] = prob.astype(jnp.bfloat16)
            ds_ref[place, cols] = (prob * (p - delta) * scale).astype(jnp.bfloat16)
            at += e.shape[0]


def key_terms(qx_ref, do_ref, late, picked, ds_ref, pt_ref):
    quads, span, wide = qx_ref.shape[1:]
    width = do_ref.shape[3]
    q = qx_ref[late].reshape(quads * span, wide)
    d = do_ref[late].reshape(quads * span, width)
    lat = dot(ds_ref[picked], q[:, :width]) + dot(pt_ref[picked], d)
    return lat, dot(ds_ref[picked], q[:, width:])


def put(ref, place, terms, picked):
    width = terms[0].shape[1]
    ref[place, :width] = terms[0][picked].astype(ref.dtype)
    ref[place, width:] = terms[1][picked].astype(ref.dtype)


def scores_kernel(
    scale, qx_ref, do_ref, stats_ref, own_ref, mine_ref, other_ref,
    dsl_ref, dse_ref, ptl_ref, pte_ref, keep_ref, give_ref, keys_ref, first_ref, s_ref, p_ref,
):
    rank = lax.axis_index("ctx")
    quads, span, _ = qx_ref.shape[1:]
    width = do_ref.shape[3]
    rows = own_ref.shape[0]
    half = rows // 2
    place_keys(keys_ref.at[pl.ds(rows, 2 * rows)], mine_ref, other_ref)
    keys_ref[:rows] = own_ref[...]
    first_ref[:half] = own_ref[:half]
    first_ref[half:] = keys_ref[rows : 2 * rows]
    key = lax.broadcasted_iota(jnp.int32, (half, rows), 0)
    causal = key <= lax.broadcasted_iota(jnp.int32, (half, rows), 1) % half

    def multiply(slot, late, quad, count):
        keys = keys_ref if late else first_ref
        s_ref[slot, :count] = dot(keys[:count], qx_ref[late, quad], NT)
        p_ref[slot, :count] = dot(keys[:count, :width], do_ref[late, quad], NT)

    def weigh(slot, late, quad, count):
        ds_ref, pt_ref = (dsl_ref, ptl_ref) if late else (dse_ref, pte_ref)
        tiles = span // rows
        diagonal = half if late else 0

        def plain(start, stop):
            return lambda lanes: (s_ref[slot, start:stop, lanes] * scale, p_ref[slot, start:stop, lanes])

        def masked(lanes):
            s, p = plain(diagonal, diagonal + half)(lanes)
            return jnp.where(causal, s, -jnp.inf), p

        parts = [plain(0, half)] if late else []
        parts.append(masked)
        if count > diagonal + half:
            parts.append(plain(diagonal + half, count))
        weigh_quad(
            scale,
            lambda i: stats_ref[late, tiles * quad + i : tiles * quad + i + 1],
            lambda i: stats_ref[2 + late, tiles * quad + i : tiles * quad + i + 1],
            parts, span, rows, quad * span, ds_ref, pt_ref,
        )

    def run(late_count, early_count):
        items = []
        for quad in range(quads):
            items.append((1, quad, rows + late_count))
            items.append((0, quad, half + early_count))
        multiply(0, *items[0])
        for i, item in enumerate(items):
            if i + 1 < len(items):
                multiply((i + 1) % SLOTS, *items[i + 1])
            weigh(i % SLOTS, *item)

    first, second = slice(0, half), slice(half, rows)
    terms = functools.partial(key_terms, qx_ref, do_ref)

    even = lax.axis_index("head") % 2 == 0

    def share(place, of, near, far):
        @pl.when(even)
        def _():
            put(keep_ref, place, of, near)
            put(give_ref, place, of, far)

        @pl.when(jnp.logical_not(even))
        def _():
            put(keep_ref, place, of, far)
            put(give_ref, place, of, near)

    @pl.when(rank >= HOPS - 1)
    def _():
        run(rows, rows)
        late = terms(1, pl.ds(rows, rows), dsl_ref, ptl_ref)
        early = terms(0, pl.ds(half, rows), dse_ref, pte_ref)
        share(first, (late[0] + early[0], late[1] + early[1]), first, second)
        for ref in (keep_ref, give_ref):
            ref[second] = jnp.zeros_like(ref[second])

    @pl.when(rank == 1)
    def _():
        dse_ref[rows:] = jnp.zeros_like(dse_ref[rows:])
        dsl_ref[2 * rows + half :] = jnp.zeros_like(dsl_ref[2 * rows + half :])
        run(rows + half, half)
        late = terms(1, pl.ds(rows, rows + half), dsl_ref, ptl_ref)
        early = terms(0, pl.ds(half, half), dse_ref, pte_ref)
        seconds = slice(rows, rows + half)
        both = tuple(
            jnp.concatenate([a[first] + b, a[second], a[seconds], jnp.zeros_like(b)], axis=0)
            for a, b in zip(late, early)
        )
        share(first, both, first, second)
        share(second, both, slice(rows + half, 2 * rows), seconds)

    @pl.when(rank == 0)
    def _():
        dse_ref[half:] = jnp.zeros_like(dse_ref[half:])
        run(2 * rows, 0)
        late = terms(1, pl.ds(rows, 2 * rows), dsl_ref, ptl_ref)
        share(first, late, first, second)
        share(second, late, slice(rows + half, 2 * rows), slice(rows, rows + half))


def own_kernel(qx_ref, do_ref, dsl_ref, dse_ref, ptl_ref, pte_ref, grad_ref):
    rows = grad_ref.shape[0]
    half = rows // 2
    first, second = slice(0, half), slice(half, rows)
    late = key_terms(qx_ref, do_ref, 1, pl.ds(0, rows), dsl_ref, ptl_ref)
    early = key_terms(qx_ref, do_ref, 0, pl.ds(0, half), dse_ref, pte_ref)
    put(grad_ref, first, (late[0][first] + early[0], late[1][first] + early[1]), first)
    put(grad_ref, second, late, second)


def pair_kernel(keep_ref, got_ref, out_ref):
    out_ref[...] = (keep_ref[...] + got_ref[...].astype(jnp.float32)).astype(out_ref.dtype)


def query_kernel(chosen, dsl_ref, dse_ref, own_ref, mine_ref, other_ref, wk_ref, *rest):
    last = len(rest) > 5
    if last:
        made_nope, made_rope, dnope_hbm, drope_hbm, keys_ref, first_ref, dq_ref, dnope, drope, sems = rest
    else:
        dnope, drope, keys_ref, first_ref, dq_ref = rest
    rank = lax.axis_index("ctx")
    rows, wide = own_ref.shape
    width = wk_ref.shape[0]
    half = rows // 2
    span = GROUP * half
    quads = dsl_ref.shape[1] // span
    lanes = lax.broadcasted_iota(jnp.int32, (rows, HEAD_WIDTH), 1)
    place_keys(keys_ref.at[pl.ds(rows, 2 * rows)], mine_ref, other_ref)
    keys_ref[:rows] = own_ref[...]
    first_ref[:half] = own_ref[:half]
    first_ref[half:] = keys_ref[rows : 2 * rows]

    def copies(quad):
        sources = (dnope, drope) if quad in chosen else (made_nope, made_rope)
        for i, (source, target) in enumerate(zip(sources, (dnope_hbm, drope_hbm))):
            size = source.shape[1] // quads
            cols = slice(quad * size, (quad + 1) * size)
            yield pltpu.make_async_copy(source.at[:, cols], target.at[:, cols], sems.at[quad, i])

    if last:
        for quad in range(chosen[0]):
            for copy in copies(quad):
                copy.start()

    def meet(quad, late_count):
        cols = slice(quad * span, (quad + 1) * span)
        slot = quad % 2
        late = dot(dsl_ref[:late_count, cols], keys_ref[:late_count], TN)
        early = dot(dse_ref[:, cols], first_ref[...], TN)
        dq_ref[slot, 1] = late.astype(jnp.bfloat16)
        dq_ref[slot, 0] = early.astype(jnp.bfloat16)

    def leave(quad):
        slot = quad % 2

        def head(g, place):
            mine = slice(g * half, (g + 1) * half)
            return jnp.concatenate([dq_ref[slot, 0, mine, place], dq_ref[slot, 1, mine, place]], axis=0)

        for g in range(GROUP):
            at = quad * GROUP + g
            out = slice(at * HEAD_WIDTH, (at + 1) * HEAD_WIDTH)
            dnope[:, out] = dot(head(g, slice(0, width)), wk_ref[:, out]).astype(jnp.bfloat16)
            if g % 2 == 1:
                both = slice(width, wide)
                pair = jnp.where(lanes < HEAD_WIDTH // 2, head(g - 1, both), head(g, both))
                drope[:, (at // 2) * HEAD_WIDTH : (at // 2 + 1) * HEAD_WIDTH] = pair
        if last:
            for copy in copies(quad):
                copy.start()

    def run(late_count):
        meet(chosen[0], late_count)
        for quad in chosen:
            if quad + 1 in chosen:
                meet(quad + 1, late_count)
            leave(quad)

    @pl.when(rank >= HOPS - 1)
    def _():
        run(2 * rows)

    @pl.when(rank < HOPS - 1)
    def _():
        run(3 * rows)

    if last:
        for quad in range(quads):
            for copy in copies(quad):
                copy.wait()


def finish_kernel(own_ref, other_ref, mine_ref, sent_ref, lat_ref, rot_ref):
    width = lat_ref.shape[1]
    narrow = rot_ref.shape[0]
    away = mine_ref[...].astype(jnp.float32) + sent_ref[...].astype(jnp.float32)
    total = (own_ref[...] + other_ref[...]) + away
    lat_ref[...] = total[:, :width]
    rot_ref[...] = jnp.transpose(total[:, width : width + narrow] + total[:, width + narrow :])


VMEM = pl.BlockSpec(memory_space=pltpu.VMEM)
HBM = pl.BlockSpec(memory_space=pltpu.HBM)


def in_hbm(*arrays):
    return [pltpu.with_memory_space_constraint(array, pltpu.HBM) for array in arrays]


def per_device(
    q_nope, q_rope, latent, k_rope, d_out, out_heads, lse_rest, key_up_weight, value_up_weight
):
    rows, width = latent.shape
    narrow = k_rope.shape[1]
    wide = width + 2 * narrow
    half = rows // 2
    heads = key_up_weight.shape[1] // HEAD_WIDTH
    quads, span = heads // GROUP, GROUP * half
    scale = (HEAD_WIDTH + narrow) ** (-0.5)
    bf16, f32 = jnp.bfloat16, jnp.float32
    total = heads * rows

    own = pl.pallas_call(
        pack_kernel,
        out_shape=jax.ShapeDtypeStruct((rows, wide), bf16),
        in_specs=[VMEM, VMEM],
        out_specs=VMEM,
        compiler_params=params(4),
        name="pack",
    )(*in_hbm(latent, jnp.transpose(k_rope)))
    mine = between_groups(own, 1)

    qx, do_lat, stats = pl.pallas_call(
        project_kernel,
        out_shape=(
            pltpu.VMEM((2, quads, span, wide), bf16),
            pltpu.VMEM((2, quads, span, width), bf16),
            pltpu.VMEM((4, heads // 2, rows), f32),
        ),
        in_specs=[HBM] * 7,
        out_specs=[VMEM] * 3,
        scratch_shapes=[
            pltpu.VMEM(q_nope.shape, bf16),
            pltpu.VMEM(q_rope.shape, bf16),
            pltpu.VMEM(d_out.shape, bf16),
            pltpu.VMEM(out_heads.shape, bf16),
            pltpu.VMEM(key_up_weight.shape, bf16),
            pltpu.VMEM(value_up_weight.shape, bf16),
            pltpu.VMEM((2, HEAD_WIDTH, rows), f32),
            pltpu.SemaphoreType.DMA((quads, 6)),
            pltpu.SemaphoreType.DMA,
        ],
        compiler_params=params(20),
        cost_estimate=cost(4 * total * HEAD_WIDTH * width, 12 * MIB),
        name="project",
    )(
        *in_hbm(
            q_nope, q_rope, d_out, out_heads, key_up_weight, value_up_weight, jnp.transpose(lse_rest)
        )
    )
    mine, stats = lax.optimization_barrier((mine, stats))
    other = with_partner(mine)

    late = pltpu.VMEM((3 * rows, quads * span), bf16)
    early = pltpu.VMEM((rows + half, quads * span), bf16)
    slots = pltpu.VMEM((SLOTS, 3 * rows, span), f32)
    *terms, keep, give = pl.pallas_call(
        functools.partial(scores_kernel, scale),
        out_shape=(
            late, early, late, early,
            jax.ShapeDtypeStruct((rows, wide), f32),
            jax.ShapeDtypeStruct((rows, wide), bf16),
        ),
        in_specs=[VMEM] * 6,
        out_specs=[VMEM] * 6,
        scratch_shapes=[
            pltpu.VMEM((3 * rows, wide), bf16),
            pltpu.VMEM((rows + half, wide), bf16),
            slots,
            slots,
        ],
        compiler_params=params(16),
        cost_estimate=cost(8 * total * rows * width, 16 * MIB),
        name="scores",
    )(qx, do_lat, stats, own, mine, other)
    got = with_partner(give)
    grad = pl.pallas_call(
        own_kernel,
        out_shape=jax.ShapeDtypeStruct((rows, wide), f32),
        in_specs=[VMEM] * 6,
        out_specs=VMEM,
        compiler_params=params(8),
        cost_estimate=cost(4 * total * rows * width, 16 * MIB),
        name="own",
    )(qx, do_lat, *terms)
    got, grad = lax.optimization_barrier((got, grad))
    summed = pl.pallas_call(
        pair_kernel,
        out_shape=jax.ShapeDtypeStruct((rows, wide), bf16),
        in_specs=[VMEM] * 2,
        out_specs=VMEM,
        compiler_params=params(4),
        name="pair",
    )(keep, got)
    arrived = between_groups(summed, -1)

    def queries(name, chosen, *made):
        shapes = (rows, heads * HEAD_WIDTH), (rows, heads * narrow)
        kind = functools.partial(jax.ShapeDtypeStruct, dtype=bf16) if made else functools.partial(pltpu.VMEM, dtype=bf16)
        own_copies = [pltpu.VMEM(shape, bf16) for shape in shapes] + [pltpu.SemaphoreType.DMA((quads, 2))]
        return pl.pallas_call(
            functools.partial(query_kernel, chosen),
            out_shape=tuple(kind(shape) for shape in shapes),
            in_specs=[VMEM] * (6 + len(made)),
            out_specs=[HBM if made else VMEM] * 2,
            scratch_shapes=[
                pltpu.VMEM((3 * rows, wide), bf16),
                pltpu.VMEM((rows + half, wide), bf16),
                pltpu.VMEM((2, 2, span, wide), bf16),
            ]
            + (own_copies if made else []),
            compiler_params=params(12),
            cost_estimate=cost(3 * total * rows * width, 8 * MIB),
            name=name,
        )(terms[0], terms[1], own, mine, other, key_up_weight, *made)

    sharers = lax.axis_size("head")
    bit = 1
    while 2 * bit < sharers:
        grad = grad + with_partner(grad, bit)
        bit *= 2
    grad_other = with_partner(grad, bit)
    cut = quads - (quads + 2) // 3
    made = queries("query", range(cut))
    arrived, *made = lax.optimization_barrier((arrived, *made))
    bit = 1
    while 2 * bit < sharers:
        arrived = (arrived.astype(f32) + with_partner(arrived, bit).astype(f32)).astype(bf16)
        bit *= 2
    arrived_other = with_partner(arrived, bit)
    d_q_nope, d_q_rope = queries("query_rest", range(cut, quads), *made)
    arrived_other, d_q_nope = lax.optimization_barrier((arrived_other, d_q_nope))
    latent_gradient, d_k_rope = pl.pallas_call(
        finish_kernel,
        out_shape=(
            jax.ShapeDtypeStruct((rows, width), f32),
            jax.ShapeDtypeStruct((narrow, rows), f32),
        ),
        in_specs=[VMEM] * 4,
        out_specs=[VMEM] * 2,
        compiler_params=params(4),
        name="finish",
    )(grad, grad_other, arrived, arrived_other)
    return d_q_nope, d_q_rope, latent_gradient, jnp.transpose(d_k_rope)


def solution(mesh):
    placed = (
        P("ctx", "head"),
        P("ctx", "head"),
        P("ctx", None),
        P("ctx", None),
        P("ctx", "head"),
        P("ctx", "head"),
        P("ctx", "head"),
        P(None, "head"),
        P(None, "head"),
    )
    return jax.shard_map(
        per_device,
        mesh=mesh,
        in_specs=placed,
        out_specs=(P("ctx", "head"), P("ctx", "head"), P("ctx", None), P("ctx", None)),
        check_vma=False,
    )
```

```python
import functools

import jax
import jax.numpy as jnp
from jax import lax
from jax.experimental import pallas as pl
from jax.experimental.pallas import tpu as pltpu
from jax.sharding import PartitionSpec as P

HEAD_WIDTH = 128
HOPS = 3
GROUP = 4
SLOTS = 4
MIB = 1 << 20

NT = (((1,), (1,)), ((), ()))
TN = (((0,), (0,)), ((), ()))


def dot(a, b, dims=(((1,), (0,)), ((), ()))):
    return lax.dot_general(a, b, dims, preferred_element_type=jnp.float32)


def between_groups(block, direction):
    groups, sharers = lax.axis_size("ctx"), lax.axis_size("head")
    route = []
    for group in range(groups):
        for head in range(sharers):
            to = (group + direction * (1 + head % 2)) % groups
            route.append((group * sharers + head, to * sharers + head))
    return lax.ppermute(block, ("ctx", "head"), route)


def with_partner(block, bit=1):
    return lax.ppermute(block, "head", [(i, i ^ bit) for i in range(lax.axis_size("head"))])


def params(limit_mib):
    return pltpu.CompilerParams(vmem_limit_bytes=limit_mib * MIB)


def cost(flops, moved):
    return pl.CostEstimate(flops=int(flops), bytes_accessed=int(moved), transcendentals=0)


def pack_kernel(lat_ref, rot_ref, out_ref):
    width = lat_ref.shape[1]
    rot = jnp.transpose(rot_ref[...].astype(jnp.float32)).astype(out_ref.dtype)
    out_ref[:, :width] = lat_ref[...]
    out_ref[:, width:] = jnp.concatenate([rot, rot], axis=1)


def project_kernel(
    nope_hbm, rope_hbm, dout_hbm, saved_hbm, wk_hbm, wv_hbm, rest_hbm,
    qx_ref, do_ref, stats_ref,
    nope, rope, dout, saved, wk, wv, flat_ref, sems, rest_sem,
):
    rows = nope.shape[0]
    width, total = wk.shape
    heads = total // HEAD_WIDTH
    quads = heads // GROUP
    half = rows // 2
    lanes = lax.broadcasted_iota(jnp.int32, (rows, HEAD_WIDTH), 1)
    arrays = (
        (wk_hbm, wk), (nope_hbm, nope), (wv_hbm, wv), (dout_hbm, dout), (saved_hbm, saved), (rope_hbm, rope),
    )

    groups = [(0, 1), (1, 2)] + [(i, min(i + 2, quads)) for i in range(2, quads, 2)]

    def copies(index):
        start, stop = groups[index]
        for i, (source, target) in enumerate(arrays):
            size = source.shape[1] // quads
            cols = slice(start * size, stop * size)
            yield pltpu.make_async_copy(source.at[:, cols], target.at[:, cols], sems.at[index, i])

    for index in range(len(groups)):
        for copy in copies(index):
            copy.start()
    rest_copy = pltpu.make_async_copy(rest_hbm, flat_ref.at[0, pl.ds(0, heads)], rest_sem)
    rest_copy.start()
    found = jnp.zeros((rows, HEAD_WIDTH), jnp.float32)
    for quad in range(quads):
        for index, (start, _) in enumerate(groups):
            if start == quad:
                for copy in copies(index):
                    copy.wait()
        for g in range(GROUP):
            at = quad * GROUP + g
            cols = slice(at * HEAD_WIDTH, (at + 1) * HEAD_WIDTH)
            place = slice(g * half, (g + 1) * half)
            d_out = dout[:, cols]
            q_abs = dot(nope[:, cols], wk[:, cols], NT).astype(jnp.bfloat16)
            d_lat = dot(d_out, wv[:, cols], NT).astype(jnp.bfloat16)
            pair = rope[:, (at // 2) * HEAD_WIDTH : (at // 2 + 1) * HEAD_WIDTH]
            mine = (lanes < HEAD_WIDTH // 2) if g % 2 == 0 else (lanes >= HEAD_WIDTH // 2)
            pair = jnp.where(mine, pair, jnp.zeros_like(pair))
            for late, part in ((0, slice(0, half)), (1, slice(half, rows))):
                qx_ref[late, quad, place, :width] = q_abs[part]
                qx_ref[late, quad, place, width:] = pair[part]
                do_ref[late, quad, place] = d_lat[part]
            prod = d_out.astype(jnp.float32) * saved[:, cols].astype(jnp.float32)
            delta = jnp.sum(prod, axis=1, keepdims=True)
            found = jnp.where(lanes == at, delta, found)
    rest_copy.wait()
    flat_ref[1] = jnp.transpose(found)
    low = lax.broadcasted_iota(jnp.int32, (heads // 2, rows), 1) < half
    for kind in range(2):
        even = flat_ref[kind, pl.ds(0, heads // 2, 2), :]
        odd = flat_ref[kind, pl.ds(1, heads // 2, 2), :]
        stats_ref[2 * kind] = jnp.where(low, even, pltpu.roll(odd, half, 1))
        stats_ref[2 * kind + 1] = jnp.where(low, pltpu.roll(even, half, 1), odd)


def place_keys(keys_ref, mine_ref, other_ref):
    half = mine_ref.shape[0] // 2
    even = lax.axis_index("head") % 2 == 0

    def place(near, far):
        for at, (ref, start) in enumerate(((near, 0), (far, 0), (far, half), (near, half))):
            keys_ref[at * half : (at + 1) * half] = ref[start : start + half]

    @pl.when(even)
    def _():
        place(mine_ref, other_ref)

    @pl.when(jnp.logical_not(even))
    def _():
        place(other_ref, mine_ref)


def weigh_quad(scale, rest_of, delta_of, parts, span, lane_tile, start, ds_ref, pt_ref):
    for i in range(span // lane_tile):
        lanes = slice(i * lane_tile, (i + 1) * lane_tile)
        rest, delta = rest_of(i), delta_of(i)
        met = [part(lanes) for part in parts]
        top = rest
        for s, _ in met:
            top = jnp.maximum(top, jnp.max(s, axis=0, keepdims=True))
        exps = [jnp.exp(s - top) for s, _ in met]
        mass = jnp.exp(rest - top)
        for e in exps:
            mass = mass + jnp.sum(e, axis=0, keepdims=True)
        inverse = 1.0 / mass
        cols = slice(start + i * lane_tile, start + (i + 1) * lane_tile)
        at = 0
        for e, (_, p) in zip(exps, met):
            prob = e * inverse
            place = slice(at, at + e.shape[0])
            pt_ref[place, cols] = prob.astype(jnp.bfloat16)
            ds_ref[place, cols] = (prob * (p - delta) * scale).astype(jnp.bfloat16)
            at += e.shape[0]


def key_terms(qx_ref, do_ref, late, picked, ds_ref, pt_ref):
    quads, span, wide = qx_ref.shape[1:]
    width = do_ref.shape[3]
    q = qx_ref[late].reshape(quads * span, wide)
    d = do_ref[late].reshape(quads * span, width)
    lat = dot(ds_ref[picked], q[:, :width]) + dot(pt_ref[picked], d)
    return lat, dot(ds_ref[picked], q[:, width:])


def put(ref, place, terms, picked):
    width = terms[0].shape[1]
    ref[place, :width] = terms[0][picked].astype(ref.dtype)
    ref[place, width:] = terms[1][picked].astype(ref.dtype)


def scores_kernel(
    scale, qx_ref, do_ref, stats_ref, own_ref, mine_ref, other_ref,
    dsl_ref, dse_ref, ptl_ref, pte_ref, keep_ref, give_ref, keys_ref, first_ref, s_ref, p_ref,
):
    rank = lax.axis_index("ctx")
    quads, span, _ = qx_ref.shape[1:]
    width = do_ref.shape[3]
    rows = own_ref.shape[0]
    half = rows // 2
    place_keys(keys_ref.at[pl.ds(rows, 2 * rows)], mine_ref, other_ref)
    keys_ref[:rows] = own_ref[...]
    first_ref[:half] = own_ref[:half]
    first_ref[half:] = keys_ref[rows : 2 * rows]
    key = lax.broadcasted_iota(jnp.int32, (half, rows), 0)
    causal = key <= lax.broadcasted_iota(jnp.int32, (half, rows), 1) % half

    def multiply(slot, late, quad, count):
        keys = keys_ref if late else first_ref
        s_ref[slot, :count] = dot(keys[:count], qx_ref[late, quad], NT)
        p_ref[slot, :count] = dot(keys[:count, :width], do_ref[late, quad], NT)

    def weigh(slot, late, quad, count):
        ds_ref, pt_ref = (dsl_ref, ptl_ref) if late else (dse_ref, pte_ref)
        tiles = span // rows
        diagonal = half if late else 0

        def plain(start, stop):
            return lambda lanes: (s_ref[slot, start:stop, lanes] * scale, p_ref[slot, start:stop, lanes])

        def masked(lanes):
            s, p = plain(diagonal, diagonal + half)(lanes)
            return jnp.where(causal, s, -jnp.inf), p

        parts = [plain(0, half)] if late else []
        parts.append(masked)
        if count > diagonal + half:
            parts.append(plain(diagonal + half, count))
        weigh_quad(
            scale,
            lambda i: stats_ref[late, tiles * quad + i : tiles * quad + i + 1],
            lambda i: stats_ref[2 + late, tiles * quad + i : tiles * quad + i + 1],
            parts, span, rows, quad * span, ds_ref, pt_ref,
        )

    def run(late_count, early_count):
        items = []
        for quad in range(quads):
            items.append((1, quad, rows + late_count))
            items.append((0, quad, half + early_count))
        multiply(0, *items[0])
        for i, item in enumerate(items):
            if i + 1 < len(items):
                multiply((i + 1) % SLOTS, *items[i + 1])
            weigh(i % SLOTS, *item)

    first, second = slice(0, half), slice(half, rows)
    terms = functools.partial(key_terms, qx_ref, do_ref)

    even = lax.axis_index("head") % 2 == 0

    def share(place, of, near, far):
        @pl.when(even)
        def _():
            put(keep_ref, place, of, near)
            put(give_ref, place, of, far)

        @pl.when(jnp.logical_not(even))
        def _():
            put(keep_ref, place, of, far)
            put(give_ref, place, of, near)

    @pl.when(rank >= HOPS - 1)
    def _():
        run(rows, rows)
        late = terms(1, pl.ds(rows, rows), dsl_ref, ptl_ref)
        early = terms(0, pl.ds(half, rows), dse_ref, pte_ref)
        share(first, (late[0] + early[0], late[1] + early[1]), first, second)
        for ref in (keep_ref, give_ref):
            ref[second] = jnp.zeros_like(ref[second])

    @pl.when(rank == 1)
    def _():
        dse_ref[rows:] = jnp.zeros_like(dse_ref[rows:])
        dsl_ref[2 * rows + half :] = jnp.zeros_like(dsl_ref[2 * rows + half :])
        run(rows + half, half)
        late = terms(1, pl.ds(rows, rows + half), dsl_ref, ptl_ref)
        early = terms(0, pl.ds(half, half), dse_ref, pte_ref)
        seconds = slice(rows, rows + half)
        both = tuple(
            jnp.concatenate([a[first] + b, a[second], a[seconds], jnp.zeros_like(b)], axis=0)
            for a, b in zip(late, early)
        )
        share(first, both, first, second)
        share(second, both, slice(rows + half, 2 * rows), seconds)

    @pl.when(rank == 0)
    def _():
        dse_ref[half:] = jnp.zeros_like(dse_ref[half:])
        run(2 * rows, 0)
        late = terms(1, pl.ds(rows, 2 * rows), dsl_ref, ptl_ref)
        share(first, late, first, second)
        share(second, late, slice(rows + half, 2 * rows), slice(rows, rows + half))


def own_kernel(qx_ref, do_ref, dsl_ref, dse_ref, ptl_ref, pte_ref, grad_ref):
    rows = grad_ref.shape[0]
    half = rows // 2
    first, second = slice(0, half), slice(half, rows)
    late = key_terms(qx_ref, do_ref, 1, pl.ds(0, rows), dsl_ref, ptl_ref)
    early = key_terms(qx_ref, do_ref, 0, pl.ds(0, half), dse_ref, pte_ref)
    put(grad_ref, first, (late[0][first] + early[0], late[1][first] + early[1]), first)
    put(grad_ref, second, late, second)


def pair_kernel(keep_ref, got_ref, out_ref):
    out_ref[...] = (keep_ref[...] + got_ref[...].astype(jnp.float32)).astype(out_ref.dtype)


def query_kernel(chosen, dsl_ref, dse_ref, own_ref, mine_ref, other_ref, wk_ref, *rest):
    last = len(rest) > 5
    if last:
        made_nope, made_rope, dnope_hbm, drope_hbm, keys_ref, first_ref, dq_ref, dnope, drope, sems = rest
    else:
        dnope, drope, keys_ref, first_ref, dq_ref = rest
    rank = lax.axis_index("ctx")
    rows, wide = own_ref.shape
    width = wk_ref.shape[0]
    half = rows // 2
    span = GROUP * half
    quads = dsl_ref.shape[1] // span
    lanes = lax.broadcasted_iota(jnp.int32, (rows, HEAD_WIDTH), 1)
    place_keys(keys_ref.at[pl.ds(rows, 2 * rows)], mine_ref, other_ref)
    keys_ref[:rows] = own_ref[...]
    first_ref[:half] = own_ref[:half]
    first_ref[half:] = keys_ref[rows : 2 * rows]

    def copies(quad):
        sources = (dnope, drope) if quad in chosen else (made_nope, made_rope)
        for i, (source, target) in enumerate(zip(sources, (dnope_hbm, drope_hbm))):
            size = source.shape[1] // quads
            cols = slice(quad * size, (quad + 1) * size)
            yield pltpu.make_async_copy(source.at[:, cols], target.at[:, cols], sems.at[quad, i])

    if last:
        for quad in range(chosen[0]):
            for copy in copies(quad):
                copy.start()

    def meet(quad, late_count):
        cols = slice(quad * span, (quad + 1) * span)
        slot = quad % 2
        late = dot(dsl_ref[:late_count, cols], keys_ref[:late_count], TN)
        early = dot(dse_ref[:, cols], first_ref[...], TN)
        dq_ref[slot, 1] = late.astype(jnp.bfloat16)
        dq_ref[slot, 0] = early.astype(jnp.bfloat16)

    def leave(quad):
        slot = quad % 2

        def head(g, place):
            mine = slice(g * half, (g + 1) * half)
            return jnp.concatenate([dq_ref[slot, 0, mine, place], dq_ref[slot, 1, mine, place]], axis=0)

        for g in range(GROUP):
            at = quad * GROUP + g
            out = slice(at * HEAD_WIDTH, (at + 1) * HEAD_WIDTH)
            dnope[:, out] = dot(head(g, slice(0, width)), wk_ref[:, out]).astype(jnp.bfloat16)
            if g % 2 == 1:
                both = slice(width, wide)
                pair = jnp.where(lanes < HEAD_WIDTH // 2, head(g - 1, both), head(g, both))
                drope[:, (at // 2) * HEAD_WIDTH : (at // 2 + 1) * HEAD_WIDTH] = pair
        if last:
            for copy in copies(quad):
                copy.start()

    def run(late_count):
        meet(chosen[0], late_count)
        for quad in chosen:
            if quad + 1 in chosen:
                meet(quad + 1, late_count)
            leave(quad)

    @pl.when(rank >= HOPS - 1)
    def _():
        run(2 * rows)

    @pl.when(rank < HOPS - 1)
    def _():
        run(3 * rows)

    if last:
        for quad in range(quads):
            for copy in copies(quad):
                copy.wait()


def finish_kernel(own_ref, other_ref, mine_ref, sent_ref, lat_ref, rot_ref):
    width = lat_ref.shape[1]
    narrow = rot_ref.shape[0]
    away = mine_ref[...].astype(jnp.float32) + sent_ref[...].astype(jnp.float32)
    total = (own_ref[...] + other_ref[...]) + away
    lat_ref[...] = total[:, :width]
    rot_ref[...] = jnp.transpose(total[:, width : width + narrow] + total[:, width + narrow :])


VMEM = pl.BlockSpec(memory_space=pltpu.VMEM)
HBM = pl.BlockSpec(memory_space=pltpu.HBM)


def in_hbm(*arrays):
    return [pltpu.with_memory_space_constraint(array, pltpu.HBM) for array in arrays]


def per_device(
    q_nope, q_rope, latent, k_rope, d_out, out_heads, lse_rest, key_up_weight, value_up_weight
):
    rows, width = latent.shape
    narrow = k_rope.shape[1]
    wide = width + 2 * narrow
    half = rows // 2
    heads = key_up_weight.shape[1] // HEAD_WIDTH
    quads, span = heads // GROUP, GROUP * half
    scale = (HEAD_WIDTH + narrow) ** (-0.5)
    bf16, f32 = jnp.bfloat16, jnp.float32
    total = heads * rows

    own = pl.pallas_call(
        pack_kernel,
        out_shape=jax.ShapeDtypeStruct((rows, wide), bf16),
        in_specs=[VMEM, VMEM],
        out_specs=VMEM,
        compiler_params=params(4),
        name="pack",
    )(*in_hbm(latent, jnp.transpose(k_rope)))
    mine = between_groups(own, 1)

    qx, do_lat, stats = pl.pallas_call(
        project_kernel,
        out_shape=(
            pltpu.VMEM((2, quads, span, wide), bf16),
            pltpu.VMEM((2, quads, span, width), bf16),
            pltpu.VMEM((4, heads // 2, rows), f32),
        ),
        in_specs=[HBM] * 7,
        out_specs=[VMEM] * 3,
        scratch_shapes=[
            pltpu.VMEM(q_nope.shape, bf16),
            pltpu.VMEM(q_rope.shape, bf16),
            pltpu.VMEM(d_out.shape, bf16),
            pltpu.VMEM(out_heads.shape, bf16),
            pltpu.VMEM(key_up_weight.shape, bf16),
            pltpu.VMEM(value_up_weight.shape, bf16),
            pltpu.VMEM((2, HEAD_WIDTH, rows), f32),
            pltpu.SemaphoreType.DMA((quads, 6)),
            pltpu.SemaphoreType.DMA,
        ],
        compiler_params=params(20),
        cost_estimate=cost(4 * total * HEAD_WIDTH * width, 12 * MIB),
        name="project",
    )(
        *in_hbm(
            q_nope, q_rope, d_out, out_heads, key_up_weight, value_up_weight, jnp.transpose(lse_rest)
        )
    )
    mine, stats = lax.optimization_barrier((mine, stats))
    other = with_partner(mine)

    late = pltpu.VMEM((3 * rows, quads * span), bf16)
    early = pltpu.VMEM((rows + half, quads * span), bf16)
    slots = pltpu.VMEM((SLOTS, 3 * rows, span), f32)
    *terms, keep, give = pl.pallas_call(
        functools.partial(scores_kernel, scale),
        out_shape=(
            late, early, late, early,
            jax.ShapeDtypeStruct((rows, wide), f32),
            jax.ShapeDtypeStruct((rows, wide), bf16),
        ),
        in_specs=[VMEM] * 6,
        out_specs=[VMEM] * 6,
        scratch_shapes=[
            pltpu.VMEM((3 * rows, wide), bf16),
            pltpu.VMEM((rows + half, wide), bf16),
            slots,
            slots,
        ],
        compiler_params=params(16),
        cost_estimate=cost(8 * total * rows * width, 16 * MIB),
        name="scores",
    )(qx, do_lat, stats, own, mine, other)
    got = with_partner(give)
    grad = pl.pallas_call(
        own_kernel,
        out_shape=jax.ShapeDtypeStruct((rows, wide), f32),
        in_specs=[VMEM] * 6,
        out_specs=VMEM,
        compiler_params=params(8),
        cost_estimate=cost(4 * total * rows * width, 16 * MIB),
        name="own",
    )(qx, do_lat, *terms)
    got, grad = lax.optimization_barrier((got, grad))
    summed = pl.pallas_call(
        pair_kernel,
        out_shape=jax.ShapeDtypeStruct((rows, wide), bf16),
        in_specs=[VMEM] * 2,
        out_specs=VMEM,
        compiler_params=params(4),
        name="pair",
    )(keep, got)
    arrived = between_groups(summed, -1)

    def queries(name, chosen, *made):
        shapes = (rows, heads * HEAD_WIDTH), (rows, heads * narrow)
        kind = functools.partial(jax.ShapeDtypeStruct, dtype=bf16) if made else functools.partial(pltpu.VMEM, dtype=bf16)
        own_copies = [pltpu.VMEM(shape, bf16) for shape in shapes] + [pltpu.SemaphoreType.DMA((quads, 2))]
        return pl.pallas_call(
            functools.partial(query_kernel, chosen),
            out_shape=tuple(kind(shape) for shape in shapes),
            in_specs=[VMEM] * (6 + len(made)),
            out_specs=[HBM if made else VMEM] * 2,
            scratch_shapes=[
                pltpu.VMEM((3 * rows, wide), bf16),
                pltpu.VMEM((rows + half, wide), bf16),
                pltpu.VMEM((2, 2, span, wide), bf16),
            ]
            + (own_copies if made else []),
            compiler_params=params(12),
            cost_estimate=cost(3 * total * rows * width, 8 * MIB),
            name=name,
        )(terms[0], terms[1], own, mine, other, key_up_weight, *made)

    sharers = lax.axis_size("head")
    bit = 1
    while 2 * bit < sharers:
        grad = grad + with_partner(grad, bit)
        bit *= 2
    grad_other = with_partner(grad, bit)
    cut = quads - 1
    made = queries("query", range(cut))
    arrived, *made = lax.optimization_barrier((arrived, *made))
    bit = 1
    while 2 * bit < sharers:
        arrived = (arrived.astype(f32) + with_partner(arrived, bit).astype(f32)).astype(bf16)
        bit *= 2
    arrived_other = with_partner(arrived, bit)
    d_q_nope, d_q_rope = queries("query_rest", range(cut, quads), *made)
    arrived_other, d_q_nope = lax.optimization_barrier((arrived_other, d_q_nope))
    latent_gradient, d_k_rope = pl.pallas_call(
        finish_kernel,
        out_shape=(
            jax.ShapeDtypeStruct((rows, width), f32),
            jax.ShapeDtypeStruct((narrow, rows), f32),
        ),
        in_specs=[VMEM] * 4,
        out_specs=[VMEM] * 2,
        compiler_params=params(4),
        name="finish",
    )(grad, grad_other, arrived, arrived_other)
    return d_q_nope, d_q_rope, latent_gradient, jnp.transpose(d_k_rope)


def solution(mesh):
    placed = (
        P("ctx", "head"),
        P("ctx", "head"),
        P("ctx", None),
        P("ctx", None),
        P("ctx", "head"),
        P("ctx", "head"),
        P("ctx", "head"),
        P(None, "head"),
        P(None, "head"),
    )
    return jax.shard_map(
        per_device,
        mesh=mesh,
        in_specs=placed,
        out_specs=(P("ctx", "head"), P("ctx", "head"), P("ctx", None), P("ctx", None)),
        check_vma=False,
    )
```

```python
import functools

import jax
import jax.numpy as jnp
from jax import lax
from jax.experimental import pallas as pl
from jax.experimental.pallas import tpu as pltpu
from jax.sharding import PartitionSpec as P

HEAD_WIDTH = 128
HOPS = 3
GROUP = 4
SLOTS = 4
MIB = 1 << 20

NT = (((1,), (1,)), ((), ()))
TN = (((0,), (0,)), ((), ()))


def dot(a, b, dims=(((1,), (0,)), ((), ()))):
    return lax.dot_general(a, b, dims, preferred_element_type=jnp.float32)


def between_groups(block, direction):
    groups, sharers = lax.axis_size("ctx"), lax.axis_size("head")
    route = []
    for group in range(groups):
        for head in range(sharers):
            to = (group + direction * (1 + head % 2)) % groups
            route.append((group * sharers + head, to * sharers + head))
    return lax.ppermute(block, ("ctx", "head"), route)


def with_partner(block, bit=1):
    return lax.ppermute(block, "head", [(i, i ^ bit) for i in range(lax.axis_size("head"))])


def params(limit_mib):
    return pltpu.CompilerParams(vmem_limit_bytes=limit_mib * MIB)


def cost(flops, moved):
    return pl.CostEstimate(flops=int(flops), bytes_accessed=int(moved), transcendentals=0)


def pack_kernel(lat_ref, rot_ref, out_ref):
    width = lat_ref.shape[1]
    rot = jnp.transpose(rot_ref[...].astype(jnp.float32)).astype(out_ref.dtype)
    out_ref[:, :width] = lat_ref[...]
    out_ref[:, width:] = jnp.concatenate([rot, rot], axis=1)


def project_quads(chosen, arrive, found, nope, rope, dout, saved, wk, wv, qx_ref, do_ref):
    rows = nope.shape[0]
    width = wk.shape[0]
    half = rows // 2
    lanes = lax.broadcasted_iota(jnp.int32, (rows, HEAD_WIDTH), 1)
    for quad in chosen:
        arrive(quad)
        for g in range(GROUP):
            at = quad * GROUP + g
            cols = slice(at * HEAD_WIDTH, (at + 1) * HEAD_WIDTH)
            place = slice(g * half, (g + 1) * half)
            d_out = dout[:, cols]
            q_abs = dot(nope[:, cols], wk[:, cols], NT).astype(jnp.bfloat16)
            d_lat = dot(d_out, wv[:, cols], NT).astype(jnp.bfloat16)
            pair = rope[:, (at // 2) * HEAD_WIDTH : (at // 2 + 1) * HEAD_WIDTH]
            mine = (lanes < HEAD_WIDTH // 2) if g % 2 == 0 else (lanes >= HEAD_WIDTH // 2)
            pair = jnp.where(mine, pair, jnp.zeros_like(pair))
            for late, part in ((0, slice(0, half)), (1, slice(half, rows))):
                qx_ref[late, quad, place, :width] = q_abs[part]
                qx_ref[late, quad, place, width:] = pair[part]
                do_ref[late, quad, place] = d_lat[part]
            prod = d_out.astype(jnp.float32) * saved[:, cols].astype(jnp.float32)
            delta = jnp.sum(prod, axis=1, keepdims=True)
            found = jnp.where(lanes == at, delta, found)
    return found


def project_kernel(chosen, *refs):
    sources, (qx_ref, do_ref, found_ref), targets, (sems,) = refs[:6], refs[6:9], refs[9:15], refs[15:]
    quads = qx_ref.shape[1]
    groups = [(0, 1), (1, 2)] + [(i, min(i + 2, quads)) for i in range(2, quads, 2)]

    def copies(index):
        start, stop = groups[index]
        for i in (4, 0, 5, 2, 3, 1):
            size = sources[i].shape[1] // quads
            cols = slice(start * size, stop * size)
            yield pltpu.make_async_copy(sources[i].at[:, cols], targets[i].at[:, cols], sems.at[index, i])

    def arrive(quad):
        for index, (start, _) in enumerate(groups):
            if start == quad:
                for copy in copies(index):
                    copy.wait()

    for index in range(len(groups)):
        for copy in copies(index):
            copy.start()
    found = jnp.zeros(found_ref.shape, jnp.float32)
    found_ref[...] = project_quads(chosen, arrive, found, *targets, qx_ref, do_ref)
    for quad in range(len(chosen), quads):
        arrive(quad)


def project_rest_kernel(chosen, *refs):
    (_, _, found_ref), arrays, (rest_hbm,), (qx_ref, do_ref, stats_ref) = refs[:3], refs[3:9], refs[9:10], refs[10:13]
    flat_ref, rest_sem = refs[13:]
    rows = arrays[0].shape[0]
    half = rows // 2
    heads = qx_ref.shape[1] * GROUP
    rest_copy = pltpu.make_async_copy(rest_hbm, flat_ref.at[0, pl.ds(0, heads)], rest_sem)
    rest_copy.start()
    found = project_quads(chosen, lambda quad: None, found_ref[...], *arrays, qx_ref, do_ref)
    flat_ref[1] = jnp.transpose(found)
    rest_copy.wait()
    low = lax.broadcasted_iota(jnp.int32, (heads // 2, rows), 1) < half
    for kind in range(2):
        even = flat_ref[kind, pl.ds(0, heads // 2, 2), :]
        odd = flat_ref[kind, pl.ds(1, heads // 2, 2), :]
        stats_ref[2 * kind] = jnp.where(low, even, pltpu.roll(odd, half, 1))
        stats_ref[2 * kind + 1] = jnp.where(low, pltpu.roll(even, half, 1), odd)


def place_keys(keys_ref, mine_ref, other_ref):
    half = mine_ref.shape[0] // 2
    even = lax.axis_index("head") % 2 == 0

    def place(near, far):
        for at, (ref, start) in enumerate(((near, 0), (far, 0), (far, half), (near, half))):
            keys_ref[at * half : (at + 1) * half] = ref[start : start + half]

    @pl.when(even)
    def _():
        place(mine_ref, other_ref)

    @pl.when(jnp.logical_not(even))
    def _():
        place(other_ref, mine_ref)


def weigh_quad(scale, rest_of, delta_of, parts, span, lane_tile, start, ds_ref, pt_ref):
    for i in range(span // lane_tile):
        lanes = slice(i * lane_tile, (i + 1) * lane_tile)
        rest, delta = rest_of(i), delta_of(i)
        met = [part(lanes) for part in parts]
        top = rest
        for s, _ in met:
            top = jnp.maximum(top, jnp.max(s, axis=0, keepdims=True))
        exps = [jnp.exp(s - top) for s, _ in met]
        mass = jnp.exp(rest - top)
        for e in exps:
            mass = mass + jnp.sum(e, axis=0, keepdims=True)
        inverse = 1.0 / mass
        cols = slice(start + i * lane_tile, start + (i + 1) * lane_tile)
        at = 0
        for e, (_, p) in zip(exps, met):
            prob = e * inverse
            place = slice(at, at + e.shape[0])
            pt_ref[place, cols] = prob.astype(jnp.bfloat16)
            ds_ref[place, cols] = (prob * (p - delta) * scale).astype(jnp.bfloat16)
            at += e.shape[0]


def key_terms(qx_ref, do_ref, late, picked, ds_ref, pt_ref):
    quads, span, wide = qx_ref.shape[1:]
    width = do_ref.shape[3]
    q = qx_ref[late].reshape(quads * span, wide)
    d = do_ref[late].reshape(quads * span, width)
    lat = dot(ds_ref[picked], q[:, :width]) + dot(pt_ref[picked], d)
    return lat, dot(ds_ref[picked], q[:, width:])


def put(ref, place, terms, picked):
    width = terms[0].shape[1]
    ref[place, :width] = terms[0][picked].astype(ref.dtype)
    ref[place, width:] = terms[1][picked].astype(ref.dtype)


def scores_kernel(
    scale, qx_ref, do_ref, stats_ref, own_ref, mine_ref, other_ref,
    dsl_ref, dse_ref, ptl_ref, pte_ref, keep_ref, give_ref, keys_ref, first_ref, s_ref, p_ref,
):
    rank = lax.axis_index("ctx")
    quads, span, _ = qx_ref.shape[1:]
    width = do_ref.shape[3]
    rows = own_ref.shape[0]
    half = rows // 2
    place_keys(keys_ref.at[pl.ds(rows, 2 * rows)], mine_ref, other_ref)
    keys_ref[:rows] = own_ref[...]
    first_ref[:half] = own_ref[:half]
    first_ref[half:] = keys_ref[rows : 2 * rows]
    key = lax.broadcasted_iota(jnp.int32, (half, rows), 0)
    causal = key <= lax.broadcasted_iota(jnp.int32, (half, rows), 1) % half

    def multiply(slot, late, quad, count):
        keys = keys_ref if late else first_ref
        s_ref[slot, :count] = dot(keys[:count], qx_ref[late, quad], NT)
        p_ref[slot, :count] = dot(keys[:count, :width], do_ref[late, quad], NT)

    def weigh(slot, late, quad, count):
        ds_ref, pt_ref = (dsl_ref, ptl_ref) if late else (dse_ref, pte_ref)
        tiles = span // rows
        diagonal = half if late else 0

        def plain(start, stop):
            return lambda lanes: (s_ref[slot, start:stop, lanes] * scale, p_ref[slot, start:stop, lanes])

        def masked(lanes):
            s, p = plain(diagonal, diagonal + half)(lanes)
            return jnp.where(causal, s, -jnp.inf), p

        parts = [plain(0, half)] if late else []
        parts.append(masked)
        if count > diagonal + half:
            parts.append(plain(diagonal + half, count))
        weigh_quad(
            scale,
            lambda i: stats_ref[late, tiles * quad + i : tiles * quad + i + 1],
            lambda i: stats_ref[2 + late, tiles * quad + i : tiles * quad + i + 1],
            parts, span, rows, quad * span, ds_ref, pt_ref,
        )

    def run(late_count, early_count):
        items = []
        for quad in range(quads):
            items.append((1, quad, rows + late_count))
            items.append((0, quad, half + early_count))
        multiply(0, *items[0])
        for i, item in enumerate(items):
            if i + 1 < len(items):
                multiply((i + 1) % SLOTS, *items[i + 1])
            weigh(i % SLOTS, *item)

    first, second = slice(0, half), slice(half, rows)
    terms = functools.partial(key_terms, qx_ref, do_ref)

    even = lax.axis_index("head") % 2 == 0

    def share(place, of, near, far):
        @pl.when(even)
        def _():
            put(keep_ref, place, of, near)
            put(give_ref, place, of, far)

        @pl.when(jnp.logical_not(even))
        def _():
            put(keep_ref, place, of, far)
            put(give_ref, place, of, near)

    @pl.when(rank >= HOPS - 1)
    def _():
        run(rows, rows)
        late = terms(1, pl.ds(rows, rows), dsl_ref, ptl_ref)
        early = terms(0, pl.ds(half, rows), dse_ref, pte_ref)
        share(first, (late[0] + early[0], late[1] + early[1]), first, second)
        for ref in (keep_ref, give_ref):
            ref[second] = jnp.zeros_like(ref[second])

    @pl.when(rank == 1)
    def _():
        dse_ref[rows:] = jnp.zeros_like(dse_ref[rows:])
        dsl_ref[2 * rows + half :] = jnp.zeros_like(dsl_ref[2 * rows + half :])
        run(rows + half, half)
        late = terms(1, pl.ds(rows, rows + half), dsl_ref, ptl_ref)
        early = terms(0, pl.ds(half, half), dse_ref, pte_ref)
        seconds = slice(rows, rows + half)
        both = tuple(
            jnp.concatenate([a[first] + b, a[second], a[seconds], jnp.zeros_like(b)], axis=0)
            for a, b in zip(late, early)
        )
        share(first, both, first, second)
        share(second, both, slice(rows + half, 2 * rows), seconds)

    @pl.when(rank == 0)
    def _():
        dse_ref[half:] = jnp.zeros_like(dse_ref[half:])
        run(2 * rows, 0)
        late = terms(1, pl.ds(rows, 2 * rows), dsl_ref, ptl_ref)
        share(first, late, first, second)
        share(second, late, slice(rows + half, 2 * rows), slice(rows, rows + half))


def own_kernel(qx_ref, do_ref, dsl_ref, dse_ref, ptl_ref, pte_ref, grad_ref):
    rows = grad_ref.shape[0]
    half = rows // 2
    first, second = slice(0, half), slice(half, rows)
    late = key_terms(qx_ref, do_ref, 1, pl.ds(0, rows), dsl_ref, ptl_ref)
    early = key_terms(qx_ref, do_ref, 0, pl.ds(0, half), dse_ref, pte_ref)
    put(grad_ref, first, (late[0][first] + early[0], late[1][first] + early[1]), first)
    put(grad_ref, second, late, second)


def pair_kernel(keep_ref, got_ref, out_ref):
    out_ref[...] = (keep_ref[...] + got_ref[...].astype(jnp.float32)).astype(out_ref.dtype)


def query_kernel(chosen, dsl_ref, dse_ref, own_ref, mine_ref, other_ref, wk_ref, *rest):
    last = len(rest) > 5
    if last:
        made_nope, made_rope, dnope_hbm, drope_hbm, keys_ref, first_ref, dq_ref, dnope, drope, sems = rest
    else:
        dnope, drope, keys_ref, first_ref, dq_ref = rest
    rank = lax.axis_index("ctx")
    rows, wide = own_ref.shape
    width = wk_ref.shape[0]
    half = rows // 2
    span = GROUP * half
    quads = dsl_ref.shape[1] // span
    lanes = lax.broadcasted_iota(jnp.int32, (rows, HEAD_WIDTH), 1)
    place_keys(keys_ref.at[pl.ds(rows, 2 * rows)], mine_ref, other_ref)
    keys_ref[:rows] = own_ref[...]
    first_ref[:half] = own_ref[:half]
    first_ref[half:] = keys_ref[rows : 2 * rows]

    def copies(quad):
        sources = (dnope, drope) if quad in chosen else (made_nope, made_rope)
        for i, (source, target) in enumerate(zip(sources, (dnope_hbm, drope_hbm))):
            size = source.shape[1] // quads
            cols = slice(quad * size, (quad + 1) * size)
            yield pltpu.make_async_copy(source.at[:, cols], target.at[:, cols], sems.at[quad, i])

    if last:
        for quad in range(chosen[0]):
            for copy in copies(quad):
                copy.start()

    def meet(quad, late_count):
        cols = slice(quad * span, (quad + 1) * span)
        slot = quad % 2
        late = dot(dsl_ref[:late_count, cols], keys_ref[:late_count], TN)
        early = dot(dse_ref[:, cols], first_ref[...], TN)
        dq_ref[slot, 1] = late.astype(jnp.bfloat16)
        dq_ref[slot, 0] = early.astype(jnp.bfloat16)

    def leave(quad):
        slot = quad % 2

        def head(g, place):
            mine = slice(g * half, (g + 1) * half)
            return jnp.concatenate([dq_ref[slot, 0, mine, place], dq_ref[slot, 1, mine, place]], axis=0)

        for g in range(GROUP):
            at = quad * GROUP + g
            out = slice(at * HEAD_WIDTH, (at + 1) * HEAD_WIDTH)
            dnope[:, out] = dot(head(g, slice(0, width)), wk_ref[:, out]).astype(jnp.bfloat16)
            if g % 2 == 1:
                both = slice(width, wide)
                pair = jnp.where(lanes < HEAD_WIDTH // 2, head(g - 1, both), head(g, both))
                drope[:, (at // 2) * HEAD_WIDTH : (at // 2 + 1) * HEAD_WIDTH] = pair
        if last:
            for copy in copies(quad):
                copy.start()

    def run(late_count):
        meet(chosen[0], late_count)
        for quad in chosen:
            if quad + 1 in chosen:
                meet(quad + 1, late_count)
            leave(quad)

    @pl.when(rank >= HOPS - 1)
    def _():
        run(2 * rows)

    @pl.when(rank < HOPS - 1)
    def _():
        run(3 * rows)

    if last:
        for quad in range(quads):
            for copy in copies(quad):
                copy.wait()


def finish_kernel(own_ref, other_ref, mine_ref, sent_ref, lat_ref, rot_ref):
    width = lat_ref.shape[1]
    narrow = rot_ref.shape[0]
    away = mine_ref[...].astype(jnp.float32) + sent_ref[...].astype(jnp.float32)
    total = (own_ref[...] + other_ref[...]) + away
    lat_ref[...] = total[:, :width]
    rot_ref[...] = jnp.transpose(total[:, width : width + narrow] + total[:, width + narrow :])


VMEM = pl.BlockSpec(memory_space=pltpu.VMEM)
HBM = pl.BlockSpec(memory_space=pltpu.HBM)


def in_hbm(*arrays):
    return [pltpu.with_memory_space_constraint(array, pltpu.HBM) for array in arrays]


def per_device(
    q_nope, q_rope, latent, k_rope, d_out, out_heads, lse_rest, key_up_weight, value_up_weight
):
    rows, width = latent.shape
    narrow = k_rope.shape[1]
    wide = width + 2 * narrow
    half = rows // 2
    heads = key_up_weight.shape[1] // HEAD_WIDTH
    quads, span = heads // GROUP, GROUP * half
    scale = (HEAD_WIDTH + narrow) ** (-0.5)
    bf16, f32 = jnp.bfloat16, jnp.float32
    total = heads * rows

    own = pl.pallas_call(
        pack_kernel,
        out_shape=jax.ShapeDtypeStruct((rows, wide), bf16),
        in_specs=[VMEM, VMEM],
        out_specs=VMEM,
        compiler_params=params(4),
        name="pack",
    )(*in_hbm(latent, jnp.transpose(k_rope)))
    mine = between_groups(own, 1)

    qx_shape = pltpu.VMEM((2, quads, span, wide), bf16)
    do_shape = pltpu.VMEM((2, quads, span, width), bf16)
    streamed = (q_nope, q_rope, d_out, out_heads, key_up_weight, value_up_weight)
    held = quads - quads // 4
    qx, do_lat, found, *loaded = pl.pallas_call(
        functools.partial(project_kernel, range(held)),
        out_shape=(qx_shape, do_shape, pltpu.VMEM((rows, HEAD_WIDTH), f32))
        + tuple(pltpu.VMEM(array.shape, bf16) for array in streamed),
        in_specs=[HBM] * 6,
        out_specs=[VMEM] * 9,
        scratch_shapes=[pltpu.SemaphoreType.DMA((quads, 6))],
        compiler_params=params(8),
        cost_estimate=cost(4 * total * HEAD_WIDTH * width, 12 * MIB),
        name="project",
    )(*in_hbm(*streamed))
    mine, found = lax.optimization_barrier((mine, found))
    other = with_partner(mine)
    qx, do_lat, stats = pl.pallas_call(
        functools.partial(project_rest_kernel, range(held, quads)),
        out_shape=(qx_shape, do_shape, pltpu.VMEM((4, heads // 2, rows), f32)),
        in_specs=[VMEM] * 9 + [HBM],
        out_specs=[VMEM] * 3,
        input_output_aliases={0: 0, 1: 1},
        scratch_shapes=[pltpu.VMEM((2, HEAD_WIDTH, rows), f32), pltpu.SemaphoreType.DMA],
        compiler_params=params(8),
        cost_estimate=cost(total * HEAD_WIDTH * width, 4 * MIB),
        name="project_rest",
    )(qx, do_lat, found, *loaded, *in_hbm(jnp.transpose(lse_rest)))
    other, stats = lax.optimization_barrier((other, stats))

    late = pltpu.VMEM((3 * rows, quads * span), bf16)
    early = pltpu.VMEM((rows + half, quads * span), bf16)
    slots = pltpu.VMEM((SLOTS, 3 * rows, span), f32)
    *terms, keep, give = pl.pallas_call(
        functools.partial(scores_kernel, scale),
        out_shape=(
            late, early, late, early,
            jax.ShapeDtypeStruct((rows, wide), f32),
            jax.ShapeDtypeStruct((rows, wide), bf16),
        ),
        in_specs=[VMEM] * 6,
        out_specs=[VMEM] * 6,
        scratch_shapes=[
            pltpu.VMEM((3 * rows, wide), bf16),
            pltpu.VMEM((rows + half, wide), bf16),
            slots,
            slots,
        ],
        compiler_params=params(16),
        cost_estimate=cost(8 * total * rows * width, 16 * MIB),
        name="scores",
    )(qx, do_lat, stats, own, mine, other)
    got = with_partner(give)
    grad = pl.pallas_call(
        own_kernel,
        out_shape=jax.ShapeDtypeStruct((rows, wide), f32),
        in_specs=[VMEM] * 6,
        out_specs=VMEM,
        compiler_params=params(8),
        cost_estimate=cost(4 * total * rows * width, 16 * MIB),
        name="own",
    )(qx, do_lat, *terms)
    got, grad = lax.optimization_barrier((got, grad))
    summed = pl.pallas_call(
        pair_kernel,
        out_shape=jax.ShapeDtypeStruct((rows, wide), bf16),
        in_specs=[VMEM] * 2,
        out_specs=VMEM,
        compiler_params=params(4),
        name="pair",
    )(keep, got)
    arrived = between_groups(summed, -1)

    def queries(name, chosen, *made):
        shapes = (rows, heads * HEAD_WIDTH), (rows, heads * narrow)
        kind = functools.partial(jax.ShapeDtypeStruct, dtype=bf16) if made else functools.partial(pltpu.VMEM, dtype=bf16)
        own_copies = [pltpu.VMEM(shape, bf16) for shape in shapes] + [pltpu.SemaphoreType.DMA((quads, 2))]
        return pl.pallas_call(
            functools.partial(query_kernel, chosen),
            out_shape=tuple(kind(shape) for shape in shapes),
            in_specs=[VMEM] * (6 + len(made)),
            out_specs=[HBM if made else VMEM] * 2,
            scratch_shapes=[
                pltpu.VMEM((3 * rows, wide), bf16),
                pltpu.VMEM((rows + half, wide), bf16),
                pltpu.VMEM((2, 2, span, wide), bf16),
            ]
            + (own_copies if made else []),
            compiler_params=params(12),
            cost_estimate=cost(3 * total * rows * width, 8 * MIB),
            name=name,
        )(terms[0], terms[1], own, mine, other, loaded[4], *made)

    sharers = lax.axis_size("head")
    bit = 1
    while 2 * bit < sharers:
        grad = grad + with_partner(grad, bit)
        bit *= 2
    grad_other = with_partner(grad, bit)
    cut = quads - 1
    made = queries("query", range(cut))
    arrived, *made = lax.optimization_barrier((arrived, *made))
    bit = 1
    while 2 * bit < sharers:
        arrived = (arrived.astype(f32) + with_partner(arrived, bit).astype(f32)).astype(bf16)
        bit *= 2
    arrived_other = with_partner(arrived, bit)
    d_q_nope, d_q_rope = queries("query_rest", range(cut, quads), *made)
    arrived_other, d_q_nope = lax.optimization_barrier((arrived_other, d_q_nope))
    latent_gradient, d_k_rope = pl.pallas_call(
        finish_kernel,
        out_shape=(
            jax.ShapeDtypeStruct((rows, width), f32),
            jax.ShapeDtypeStruct((narrow, rows), f32),
        ),
        in_specs=[VMEM] * 4,
        out_specs=[VMEM] * 2,
        compiler_params=params(4),
        name="finish",
    )(grad, grad_other, arrived, arrived_other)
    return d_q_nope, d_q_rope, latent_gradient, jnp.transpose(d_k_rope)


def solution(mesh):
    placed = (
        P("ctx", "head"),
        P("ctx", "head"),
        P("ctx", None),
        P("ctx", None),
        P("ctx", "head"),
        P("ctx", "head"),
        P("ctx", "head"),
        P(None, "head"),
        P(None, "head"),
    )
    return jax.shard_map(
        per_device,
        mesh=mesh,
        in_specs=placed,
        out_specs=(P("ctx", "head"), P("ctx", "head"), P("ctx", None), P("ctx", None)),
        check_vma=False,
    )
```

```python
import functools

import jax
import jax.numpy as jnp
from jax import lax
from jax.experimental import pallas as pl
from jax.experimental.pallas import tpu as pltpu
from jax.sharding import PartitionSpec as P

HEAD_WIDTH = 128
HOPS = 3
GROUP = 4
SLOTS = 4
MIB = 1 << 20

NT = (((1,), (1,)), ((), ()))
TN = (((0,), (0,)), ((), ()))


def dot(a, b, dims=(((1,), (0,)), ((), ()))):
    return lax.dot_general(a, b, dims, preferred_element_type=jnp.float32)


def between_groups(block, direction):
    groups, sharers = lax.axis_size("ctx"), lax.axis_size("head")
    route = []
    for group in range(groups):
        for head in range(sharers):
            to = (group + direction * (1 + head % 2)) % groups
            route.append((group * sharers + head, to * sharers + head))
    return lax.ppermute(block, ("ctx", "head"), route)


def with_partner(block, bit=1):
    return lax.ppermute(block, "head", [(i, i ^ bit) for i in range(lax.axis_size("head"))])


def params(limit_mib):
    return pltpu.CompilerParams(vmem_limit_bytes=limit_mib * MIB)


def cost(flops, moved):
    return pl.CostEstimate(flops=int(flops), bytes_accessed=int(moved), transcendentals=0)


def pack_kernel(lat_ref, rot_ref, out_ref):
    width = lat_ref.shape[1]
    rot = jnp.transpose(rot_ref[...].astype(jnp.float32)).astype(out_ref.dtype)
    out_ref[:, :width] = lat_ref[...]
    out_ref[:, width:] = jnp.concatenate([rot, rot], axis=1)


def project_quads(chosen, arrive, found, nope, rope, dout, saved, wk, wv, qx_ref, do_ref):
    rows = nope.shape[0]
    width = wk.shape[0]
    half = rows // 2
    lanes = lax.broadcasted_iota(jnp.int32, (rows, HEAD_WIDTH), 1)
    for quad in chosen:
        arrive(quad)
        for g in range(GROUP):
            at = quad * GROUP + g
            cols = slice(at * HEAD_WIDTH, (at + 1) * HEAD_WIDTH)
            place = slice(g * half, (g + 1) * half)
            d_out = dout[:, cols]
            q_abs = dot(nope[:, cols], wk[:, cols], NT).astype(jnp.bfloat16)
            d_lat = dot(d_out, wv[:, cols], NT).astype(jnp.bfloat16)
            pair = rope[:, (at // 2) * HEAD_WIDTH : (at // 2 + 1) * HEAD_WIDTH]
            mine = (lanes < HEAD_WIDTH // 2) if g % 2 == 0 else (lanes >= HEAD_WIDTH // 2)
            pair = jnp.where(mine, pair, jnp.zeros_like(pair))
            for late, part in ((0, slice(0, half)), (1, slice(half, rows))):
                qx_ref[late, quad, place, :width] = q_abs[part]
                qx_ref[late, quad, place, width:] = pair[part]
                do_ref[late, quad, place] = d_lat[part]
            prod = d_out.astype(jnp.float32) * saved[:, cols].astype(jnp.float32)
            delta = jnp.sum(prod, axis=1, keepdims=True)
            found = jnp.where(lanes == at, delta, found)
    return found


def project_kernel(chosen, *refs):
    sources, (qx_ref, do_ref, found_ref), targets, (sems,) = refs[:6], refs[6:9], refs[9:15], refs[15:]
    quads = qx_ref.shape[1]
    groups = [(0, 1), (1, 2)] + [(i, min(i + 2, quads)) for i in range(2, quads, 2)]

    def copies(index):
        start, stop = groups[index]
        for i in (4, 0, 5, 2, 3, 1):
            size = sources[i].shape[1] // quads
            cols = slice(start * size, stop * size)
            yield pltpu.make_async_copy(sources[i].at[:, cols], targets[i].at[:, cols], sems.at[index, i])

    def arrive(quad):
        for index, (start, _) in enumerate(groups):
            if start == quad:
                for copy in copies(index):
                    copy.wait()

    for index in range(len(groups)):
        for copy in copies(index):
            copy.start()
    found = jnp.zeros(found_ref.shape, jnp.float32)
    found_ref[...] = project_quads(chosen, arrive, found, *targets, qx_ref, do_ref)
    for quad in range(len(chosen), quads):
        arrive(quad)


def project_rest_kernel(chosen, *refs):
    (_, _, found_ref), arrays, (rest_hbm,), (qx_ref, do_ref, stats_ref) = refs[:3], refs[3:9], refs[9:10], refs[10:13]
    flat_ref, rest_sem = refs[13:]
    rows = arrays[0].shape[0]
    half = rows // 2
    heads = qx_ref.shape[1] * GROUP
    rest_copy = pltpu.make_async_copy(rest_hbm, flat_ref.at[0, pl.ds(0, heads)], rest_sem)
    rest_copy.start()
    found = project_quads(chosen, lambda quad: None, found_ref[...], *arrays, qx_ref, do_ref)
    flat_ref[1] = jnp.transpose(found)
    rest_copy.wait()
    low = lax.broadcasted_iota(jnp.int32, (heads // 2, rows), 1) < half
    for kind in range(2):
        even = flat_ref[kind, pl.ds(0, heads // 2, 2), :]
        odd = flat_ref[kind, pl.ds(1, heads // 2, 2), :]
        stats_ref[2 * kind] = jnp.where(low, even, pltpu.roll(odd, half, 1))
        stats_ref[2 * kind + 1] = jnp.where(low, pltpu.roll(even, half, 1), odd)


def place_keys(keys_ref, mine_ref, other_ref):
    half = mine_ref.shape[0] // 2
    even = lax.axis_index("head") % 2 == 0

    def place(near, far):
        for at, (ref, start) in enumerate(((near, 0), (far, 0), (far, half), (near, half))):
            keys_ref[at * half : (at + 1) * half] = ref[start : start + half]

    @pl.when(even)
    def _():
        place(mine_ref, other_ref)

    @pl.when(jnp.logical_not(even))
    def _():
        place(other_ref, mine_ref)


def weigh_quad(scale, rest_of, delta_of, parts, span, lane_tile, start, ds_ref, pt_ref):
    for i in range(span // lane_tile):
        lanes = slice(i * lane_tile, (i + 1) * lane_tile)
        rest, delta = rest_of(i), delta_of(i)
        met = [part(lanes) for part in parts]
        top = rest
        for s, _ in met:
            top = jnp.maximum(top, jnp.max(s, axis=0, keepdims=True))
        exps = [jnp.exp(s - top) for s, _ in met]
        mass = jnp.exp(rest - top)
        for e in exps:
            mass = mass + jnp.sum(e, axis=0, keepdims=True)
        inverse = 1.0 / mass
        cols = slice(start + i * lane_tile, start + (i + 1) * lane_tile)
        at = 0
        for e, (_, p) in zip(exps, met):
            prob = e * inverse
            place = slice(at, at + e.shape[0])
            pt_ref[place, cols] = prob.astype(jnp.bfloat16)
            ds_ref[place, cols] = (prob * (p - delta) * scale).astype(jnp.bfloat16)
            at += e.shape[0]


def key_terms(qx_ref, do_ref, late, picked, ds_ref, pt_ref):
    quads, span, wide = qx_ref.shape[1:]
    width = do_ref.shape[3]
    q = qx_ref[late].reshape(quads * span, wide)
    d = do_ref[late].reshape(quads * span, width)
    lat = dot(ds_ref[picked], q[:, :width]) + dot(pt_ref[picked], d)
    return lat, dot(ds_ref[picked], q[:, width:])


def put(ref, place, terms, picked):
    width = terms[0].shape[1]
    ref[place, :width] = terms[0][picked].astype(ref.dtype)
    ref[place, width:] = terms[1][picked].astype(ref.dtype)


def ahead_kernel(scale, qx_ref, do_ref, own_ref, sl_ref, se_ref, pl_ref, pe_ref):
    quads, rows, span = sl_ref.shape
    half = rows // 2
    width = do_ref.shape[3]

    @pl.when(lax.axis_index("ctx") == 0)
    def _():
        key = lax.broadcasted_iota(jnp.int32, (half, span), 0)
        causal = key <= lax.broadcasted_iota(jnp.int32, (half, span), 1) % half
        for quad in range(quads):
            s = dot(own_ref[...], qx_ref[1, quad], NT) * scale
            sl_ref[quad, :half] = s[:half]
            sl_ref[quad, half:] = jnp.where(causal, s[half:], -jnp.inf)
            pl_ref[quad] = dot(own_ref[:, :width], do_ref[1, quad], NT)
            s = dot(own_ref[:half], qx_ref[0, quad], NT) * scale
            se_ref[quad] = jnp.where(causal, s, -jnp.inf)
            pe_ref[quad] = dot(own_ref[:half, :width], do_ref[0, quad], NT)


def scores_kernel(
    scale, qx_ref, do_ref, stats_ref, own_ref, mine_ref, other_ref, sl_ref, se_ref, pl_ref, pe_ref,
    dsl_ref, dse_ref, ptl_ref, pte_ref, keep_ref, give_ref, keys_ref, first_ref, s_ref, p_ref,
):
    rank = lax.axis_index("ctx")
    quads, span, _ = qx_ref.shape[1:]
    width = do_ref.shape[3]
    rows = own_ref.shape[0]
    half = rows // 2
    place_keys(keys_ref.at[pl.ds(rows, 2 * rows)], mine_ref, other_ref)
    keys_ref[:rows] = own_ref[...]
    first_ref[:half] = own_ref[:half]
    first_ref[half:] = keys_ref[rows : 2 * rows]
    key = lax.broadcasted_iota(jnp.int32, (half, rows), 0)
    causal = key <= lax.broadcasted_iota(jnp.int32, (half, rows), 1) % half

    def multiply(slot, late, quad, count):
        keys = keys_ref if late else first_ref
        s_ref[slot, :count] = dot(keys[:count], qx_ref[late, quad], NT)
        p_ref[slot, :count] = dot(keys[:count, :width], do_ref[late, quad], NT)

    def multiply_away(slot, late, quad):
        if late:
            s_ref[slot, : 2 * rows] = dot(keys_ref[rows:], qx_ref[late, quad], NT)
            p_ref[slot, : 2 * rows] = dot(keys_ref[rows:, :width], do_ref[late, quad], NT)

    def plain_of(slot):
        def plain(start, stop):
            return lambda lanes: (s_ref[slot, start:stop, lanes] * scale, p_ref[slot, start:stop, lanes])

        return plain

    def weigh_away(slot, late, quad):
        own_s, own_p = (sl_ref, pl_ref) if late else (se_ref, pe_ref)
        ready = lambda lanes: (own_s[quad, :, lanes], own_p[quad, :, lanes])
        weigh_parts(late, quad, [ready] + ([plain_of(slot)(0, 2 * rows)] if late else []))

    def weigh_parts(late, quad, parts):
        ds_ref, pt_ref = (dsl_ref, ptl_ref) if late else (dse_ref, pte_ref)
        tiles = span // rows
        weigh_quad(
            scale,
            lambda i: stats_ref[late, tiles * quad + i : tiles * quad + i + 1],
            lambda i: stats_ref[2 + late, tiles * quad + i : tiles * quad + i + 1],
            parts, span, rows, quad * span, ds_ref, pt_ref,
        )

    def weigh(slot, late, quad, count):
        diagonal = half if late else 0
        plain = plain_of(slot)

        def masked(lanes):
            s, p = plain(diagonal, diagonal + half)(lanes)
            return jnp.where(causal, s, -jnp.inf), p

        parts = [plain(0, half)] if late else []
        parts.append(masked)
        if count > diagonal + half:
            parts.append(plain(diagonal + half, count))
        weigh_parts(late, quad, parts)

    def run(late_count, early_count, known=0):
        items = []
        for quad in range(quads):
            for late, count in ((1, rows + late_count), (0, half + early_count)):
                if quad < known:
                    items.append((multiply_away, weigh_away, (late, quad)))
                else:
                    items.append((multiply, weigh, (late, quad, count)))
        items[0][0](0, *items[0][2])
        for i, (_, weigh_item, item) in enumerate(items):
            if i + 1 < len(items):
                items[i + 1][0]((i + 1) % SLOTS, *items[i + 1][2])
            weigh_item(i % SLOTS, *item)

    first, second = slice(0, half), slice(half, rows)
    terms = functools.partial(key_terms, qx_ref, do_ref)

    even = lax.axis_index("head") % 2 == 0

    def share(place, of, near, far):
        @pl.when(even)
        def _():
            put(keep_ref, place, of, near)
            put(give_ref, place, of, far)

        @pl.when(jnp.logical_not(even))
        def _():
            put(keep_ref, place, of, far)
            put(give_ref, place, of, near)

    @pl.when(rank >= HOPS - 1)
    def _():
        run(rows, rows)
        late = terms(1, pl.ds(rows, rows), dsl_ref, ptl_ref)
        early = terms(0, pl.ds(half, rows), dse_ref, pte_ref)
        share(first, (late[0] + early[0], late[1] + early[1]), first, second)
        for ref in (keep_ref, give_ref):
            ref[second] = jnp.zeros_like(ref[second])

    @pl.when(rank == 1)
    def _():
        dse_ref[rows:] = jnp.zeros_like(dse_ref[rows:])
        dsl_ref[2 * rows + half :] = jnp.zeros_like(dsl_ref[2 * rows + half :])
        run(rows + half, half)
        late = terms(1, pl.ds(rows, rows + half), dsl_ref, ptl_ref)
        early = terms(0, pl.ds(half, half), dse_ref, pte_ref)
        seconds = slice(rows, rows + half)
        both = tuple(
            jnp.concatenate([a[first] + b, a[second], a[seconds], jnp.zeros_like(b)], axis=0)
            for a, b in zip(late, early)
        )
        share(first, both, first, second)
        share(second, both, slice(rows + half, 2 * rows), seconds)

    @pl.when(rank == 0)
    def _():
        dse_ref[half:] = jnp.zeros_like(dse_ref[half:])
        run(2 * rows, 0, sl_ref.shape[0])
        late = terms(1, pl.ds(rows, 2 * rows), dsl_ref, ptl_ref)
        share(first, late, first, second)
        share(second, late, slice(rows + half, 2 * rows), slice(rows, rows + half))


def own_kernel(qx_ref, do_ref, dsl_ref, dse_ref, ptl_ref, pte_ref, grad_ref):
    rows = grad_ref.shape[0]
    half = rows // 2
    first, second = slice(0, half), slice(half, rows)
    late = key_terms(qx_ref, do_ref, 1, pl.ds(0, rows), dsl_ref, ptl_ref)
    early = key_terms(qx_ref, do_ref, 0, pl.ds(0, half), dse_ref, pte_ref)
    put(grad_ref, first, (late[0][first] + early[0], late[1][first] + early[1]), first)
    put(grad_ref, second, late, second)


def pair_kernel(keep_ref, got_ref, out_ref):
    out_ref[...] = (keep_ref[...] + got_ref[...].astype(jnp.float32)).astype(out_ref.dtype)


def query_kernel(chosen, dsl_ref, dse_ref, own_ref, mine_ref, other_ref, wk_ref, *rest):
    last = len(rest) > 5
    if last:
        made_nope, made_rope, dnope_hbm, drope_hbm, keys_ref, first_ref, dq_ref, dnope, drope, sems = rest
    else:
        dnope, drope, keys_ref, first_ref, dq_ref = rest
    rank = lax.axis_index("ctx")
    rows, wide = own_ref.shape
    width = wk_ref.shape[0]
    half = rows // 2
    span = GROUP * half
    quads = dsl_ref.shape[1] // span
    lanes = lax.broadcasted_iota(jnp.int32, (rows, HEAD_WIDTH), 1)
    place_keys(keys_ref.at[pl.ds(rows, 2 * rows)], mine_ref, other_ref)
    keys_ref[:rows] = own_ref[...]
    first_ref[:half] = own_ref[:half]
    first_ref[half:] = keys_ref[rows : 2 * rows]

    def copies(quad):
        sources = (dnope, drope) if quad in chosen else (made_nope, made_rope)
        for i, (source, target) in enumerate(zip(sources, (dnope_hbm, drope_hbm))):
            size = source.shape[1] // quads
            cols = slice(quad * size, (quad + 1) * size)
            yield pltpu.make_async_copy(source.at[:, cols], target.at[:, cols], sems.at[quad, i])

    if last:
        for quad in range(chosen[0]):
            for copy in copies(quad):
                copy.start()

    def meet(quad, late_count):
        cols = slice(quad * span, (quad + 1) * span)
        slot = quad % 2
        late = dot(dsl_ref[:late_count, cols], keys_ref[:late_count], TN)
        early = dot(dse_ref[:, cols], first_ref[...], TN)
        dq_ref[slot, 1] = late.astype(jnp.bfloat16)
        dq_ref[slot, 0] = early.astype(jnp.bfloat16)

    def leave(quad):
        slot = quad % 2

        def head(g, place):
            mine = slice(g * half, (g + 1) * half)
            return jnp.concatenate([dq_ref[slot, 0, mine, place], dq_ref[slot, 1, mine, place]], axis=0)

        for g in range(GROUP):
            at = quad * GROUP + g
            out = slice(at * HEAD_WIDTH, (at + 1) * HEAD_WIDTH)
            dnope[:, out] = dot(head(g, slice(0, width)), wk_ref[:, out]).astype(jnp.bfloat16)
            if g % 2 == 1:
                both = slice(width, wide)
                pair = jnp.where(lanes < HEAD_WIDTH // 2, head(g - 1, both), head(g, both))
                drope[:, (at // 2) * HEAD_WIDTH : (at // 2 + 1) * HEAD_WIDTH] = pair
        if last:
            for copy in copies(quad):
                copy.start()

    def run(late_count):
        meet(chosen[0], late_count)
        for quad in chosen:
            if quad + 1 in chosen:
                meet(quad + 1, late_count)
            leave(quad)

    @pl.when(rank >= HOPS - 1)
    def _():
        run(2 * rows)

    @pl.when(rank < HOPS - 1)
    def _():
        run(3 * rows)

    if last:
        for quad in range(quads):
            for copy in copies(quad):
                copy.wait()


def finish_kernel(own_ref, other_ref, mine_ref, sent_ref, lat_ref, rot_ref):
    width = lat_ref.shape[1]
    narrow = rot_ref.shape[0]
    away = mine_ref[...].astype(jnp.float32) + sent_ref[...].astype(jnp.float32)
    total = (own_ref[...] + other_ref[...]) + away
    lat_ref[...] = total[:, :width]
    rot_ref[...] = jnp.transpose(total[:, width : width + narrow] + total[:, width + narrow :])


VMEM = pl.BlockSpec(memory_space=pltpu.VMEM)
HBM = pl.BlockSpec(memory_space=pltpu.HBM)


def in_hbm(*arrays):
    return [pltpu.with_memory_space_constraint(array, pltpu.HBM) for array in arrays]


def per_device(
    q_nope, q_rope, latent, k_rope, d_out, out_heads, lse_rest, key_up_weight, value_up_weight
):
    rows, width = latent.shape
    narrow = k_rope.shape[1]
    wide = width + 2 * narrow
    half = rows // 2
    heads = key_up_weight.shape[1] // HEAD_WIDTH
    quads, span = heads // GROUP, GROUP * half
    scale = (HEAD_WIDTH + narrow) ** (-0.5)
    bf16, f32 = jnp.bfloat16, jnp.float32
    total = heads * rows

    own = pl.pallas_call(
        pack_kernel,
        out_shape=jax.ShapeDtypeStruct((rows, wide), bf16),
        in_specs=[VMEM, VMEM],
        out_specs=VMEM,
        compiler_params=params(4),
        name="pack",
    )(*in_hbm(latent, jnp.transpose(k_rope)))
    mine = between_groups(own, 1)

    qx_shape = pltpu.VMEM((2, quads, span, wide), bf16)
    do_shape = pltpu.VMEM((2, quads, span, width), bf16)
    streamed = (q_nope, q_rope, d_out, out_heads, key_up_weight, value_up_weight)
    held = quads - quads // 4
    qx, do_lat, found, *loaded = pl.pallas_call(
        functools.partial(project_kernel, range(held)),
        out_shape=(qx_shape, do_shape, pltpu.VMEM((rows, HEAD_WIDTH), f32))
        + tuple(pltpu.VMEM(array.shape, bf16) for array in streamed),
        in_specs=[HBM] * 6,
        out_specs=[VMEM] * 9,
        scratch_shapes=[pltpu.SemaphoreType.DMA((quads, 6))],
        compiler_params=params(8),
        cost_estimate=cost(4 * total * HEAD_WIDTH * width, 12 * MIB),
        name="project",
    )(*in_hbm(*streamed))
    late_own = pltpu.VMEM((held, rows, span), f32)
    early_own = pltpu.VMEM((held, half, span), f32)
    ahead = pl.pallas_call(
        functools.partial(ahead_kernel, scale),
        out_shape=(late_own, early_own, late_own, early_own),
        in_specs=[VMEM] * 3,
        out_specs=[VMEM] * 4,
        compiler_params=params(4),
        cost_estimate=cost(MIB, MIB),
        name="ahead",
    )(qx, do_lat, own)
    mine, found, *ahead = lax.optimization_barrier((mine, found, *ahead))
    other = with_partner(mine)
    qx, do_lat, stats = pl.pallas_call(
        functools.partial(project_rest_kernel, range(held, quads)),
        out_shape=(qx_shape, do_shape, pltpu.VMEM((4, heads // 2, rows), f32)),
        in_specs=[VMEM] * 9 + [HBM],
        out_specs=[VMEM] * 3,
        input_output_aliases={0: 0, 1: 1},
        scratch_shapes=[pltpu.VMEM((2, HEAD_WIDTH, rows), f32), pltpu.SemaphoreType.DMA],
        compiler_params=params(8),
        cost_estimate=cost(total * HEAD_WIDTH * width, 4 * MIB),
        name="project_rest",
    )(qx, do_lat, found, *loaded, *in_hbm(jnp.transpose(lse_rest)))
    other, stats = lax.optimization_barrier((other, stats))

    late = pltpu.VMEM((3 * rows, quads * span), bf16)
    early = pltpu.VMEM((rows + half, quads * span), bf16)
    slots = pltpu.VMEM((SLOTS, 3 * rows, span), f32)
    *terms, keep, give = pl.pallas_call(
        functools.partial(scores_kernel, scale),
        out_shape=(
            late, early, late, early,
            jax.ShapeDtypeStruct((rows, wide), f32),
            jax.ShapeDtypeStruct((rows, wide), bf16),
        ),
        in_specs=[VMEM] * 10,
        out_specs=[VMEM] * 6,
        scratch_shapes=[
            pltpu.VMEM((3 * rows, wide), bf16),
            pltpu.VMEM((rows + half, wide), bf16),
            slots,
            slots,
        ],
        compiler_params=params(16),
        cost_estimate=cost(8 * total * rows * width, 16 * MIB),
        name="scores",
    )(qx, do_lat, stats, own, mine, other, *ahead)
    got = with_partner(give)
    grad = pl.pallas_call(
        own_kernel,
        out_shape=jax.ShapeDtypeStruct((rows, wide), f32),
        in_specs=[VMEM] * 6,
        out_specs=VMEM,
        compiler_params=params(8),
        cost_estimate=cost(4 * total * rows * width, 16 * MIB),
        name="own",
    )(qx, do_lat, *terms)
    got, grad = lax.optimization_barrier((got, grad))
    summed = pl.pallas_call(
        pair_kernel,
        out_shape=jax.ShapeDtypeStruct((rows, wide), bf16),
        in_specs=[VMEM] * 2,
        out_specs=VMEM,
        compiler_params=params(4),
        name="pair",
    )(keep, got)
    arrived = between_groups(summed, -1)

    def queries(name, chosen, *made):
        shapes = (rows, heads * HEAD_WIDTH), (rows, heads * narrow)
        kind = functools.partial(jax.ShapeDtypeStruct, dtype=bf16) if made else functools.partial(pltpu.VMEM, dtype=bf16)
        own_copies = [pltpu.VMEM(shape, bf16) for shape in shapes] + [pltpu.SemaphoreType.DMA((quads, 2))]
        return pl.pallas_call(
            functools.partial(query_kernel, chosen),
            out_shape=tuple(kind(shape) for shape in shapes),
            in_specs=[VMEM] * (6 + len(made)),
            out_specs=[HBM if made else VMEM] * 2,
            scratch_shapes=[
                pltpu.VMEM((3 * rows, wide), bf16),
                pltpu.VMEM((rows + half, wide), bf16),
                pltpu.VMEM((2, 2, span, wide), bf16),
            ]
            + (own_copies if made else []),
            compiler_params=params(12),
            cost_estimate=cost(3 * total * rows * width, 8 * MIB),
            name=name,
        )(terms[0], terms[1], own, mine, other, loaded[4], *made)

    sharers = lax.axis_size("head")
    bit = 1
    while 2 * bit < sharers:
        grad = grad + with_partner(grad, bit)
        bit *= 2
    grad_other = with_partner(grad, bit)
    cut = quads - 1
    made = queries("query", range(cut))
    arrived, *made = lax.optimization_barrier((arrived, *made))
    bit = 1
    while 2 * bit < sharers:
        arrived = (arrived.astype(f32) + with_partner(arrived, bit).astype(f32)).astype(bf16)
        bit *= 2
    arrived_other = with_partner(arrived, bit)
    d_q_nope, d_q_rope = queries("query_rest", range(cut, quads), *made)
    arrived_other, d_q_nope = lax.optimization_barrier((arrived_other, d_q_nope))
    latent_gradient, d_k_rope = pl.pallas_call(
        finish_kernel,
        out_shape=(
            jax.ShapeDtypeStruct((rows, width), f32),
            jax.ShapeDtypeStruct((narrow, rows), f32),
        ),
        in_specs=[VMEM] * 4,
        out_specs=[VMEM] * 2,
        compiler_params=params(4),
        name="finish",
    )(grad, grad_other, arrived, arrived_other)
    return d_q_nope, d_q_rope, latent_gradient, jnp.transpose(d_k_rope)


def solution(mesh):
    placed = (
        P("ctx", "head"),
        P("ctx", "head"),
        P("ctx", None),
        P("ctx", None),
        P("ctx", "head"),
        P("ctx", "head"),
        P("ctx", "head"),
        P(None, "head"),
        P(None, "head"),
    )
    return jax.shard_map(
        per_device,
        mesh=mesh,
        in_specs=placed,
        out_specs=(P("ctx", "head"), P("ctx", "head"), P("ctx", None), P("ctx", None)),
        check_vma=False,
    )
```

```python
import functools

import jax
import jax.numpy as jnp
from jax import lax
from jax.experimental import pallas as pl
from jax.experimental.pallas import tpu as pltpu
from jax.sharding import PartitionSpec as P

HEAD_WIDTH = 128
HOPS = 3
GROUP = 4
SLOTS = 4
MIB = 1 << 20

NT = (((1,), (1,)), ((), ()))
TN = (((0,), (0,)), ((), ()))


def dot(a, b, dims=(((1,), (0,)), ((), ()))):
    return lax.dot_general(a, b, dims, preferred_element_type=jnp.float32)


def between_groups(block, direction):
    groups, sharers = lax.axis_size("ctx"), lax.axis_size("head")
    route = []
    for group in range(groups):
        for head in range(sharers):
            to = (group + direction * (1 + head % 2)) % groups
            route.append((group * sharers + head, to * sharers + head))
    return lax.ppermute(block, ("ctx", "head"), route)


def with_partner(block, bit=1):
    return lax.ppermute(block, "head", [(i, i ^ bit) for i in range(lax.axis_size("head"))])


def params(limit_mib):
    return pltpu.CompilerParams(vmem_limit_bytes=limit_mib * MIB)


def cost(flops, moved):
    return pl.CostEstimate(flops=int(flops), bytes_accessed=int(moved), transcendentals=0)


def pack_kernel(lat_ref, rot_ref, out_ref):
    width = lat_ref.shape[1]
    rot = jnp.transpose(rot_ref[...].astype(jnp.float32)).astype(out_ref.dtype)
    out_ref[:, :width] = lat_ref[...]
    out_ref[:, width:] = jnp.concatenate([rot, rot], axis=1)


def project_quads(chosen, arrive, found, nope, rope, dout, saved, wk, wv, qx_ref, do_ref):
    rows = nope.shape[0]
    width = wk.shape[0]
    half = rows // 2
    lanes = lax.broadcasted_iota(jnp.int32, (rows, HEAD_WIDTH), 1)
    for quad in chosen:
        arrive(quad)
        for g in range(GROUP):
            at = quad * GROUP + g
            cols = slice(at * HEAD_WIDTH, (at + 1) * HEAD_WIDTH)
            place = slice(g * half, (g + 1) * half)
            d_out = dout[:, cols]
            q_abs = dot(nope[:, cols], wk[:, cols], NT).astype(jnp.bfloat16)
            d_lat = dot(d_out, wv[:, cols], NT).astype(jnp.bfloat16)
            pair = rope[:, (at // 2) * HEAD_WIDTH : (at // 2 + 1) * HEAD_WIDTH]
            mine = (lanes < HEAD_WIDTH // 2) if g % 2 == 0 else (lanes >= HEAD_WIDTH // 2)
            pair = jnp.where(mine, pair, jnp.zeros_like(pair))
            for late, part in ((0, slice(0, half)), (1, slice(half, rows))):
                qx_ref[late, quad, place, :width] = q_abs[part]
                qx_ref[late, quad, place, width:] = pair[part]
                do_ref[late, quad, place] = d_lat[part]
            prod = d_out.astype(jnp.float32) * saved[:, cols].astype(jnp.float32)
            delta = jnp.sum(prod, axis=1, keepdims=True)
            found = jnp.where(lanes == at, delta, found)
    return found


def project_kernel(chosen, *refs):
    sources, (qx_ref, do_ref, found_ref), targets, (sems,) = refs[:6], refs[6:9], refs[9:15], refs[15:]
    quads = qx_ref.shape[1]
    groups = [(0, 1), (1, 2)] + [(i, min(i + 2, quads)) for i in range(2, quads, 2)]

    def copies(index):
        start, stop = groups[index]
        for i in (4, 0, 5, 2, 3, 1):
            size = sources[i].shape[1] // quads
            cols = slice(start * size, stop * size)
            yield pltpu.make_async_copy(sources[i].at[:, cols], targets[i].at[:, cols], sems.at[index, i])

    def arrive(quad):
        for index, (start, _) in enumerate(groups):
            if start == quad:
                for copy in copies(index):
                    copy.wait()

    for index in range(len(groups)):
        for copy in copies(index):
            copy.start()
    found = jnp.zeros(found_ref.shape, jnp.float32)
    found_ref[...] = project_quads(chosen, arrive, found, *targets, qx_ref, do_ref)
    for quad in range(len(chosen), quads):
        arrive(quad)


def project_rest_kernel(chosen, *refs):
    (_, _, found_ref), arrays, (rest_hbm,), (qx_ref, do_ref, stats_ref) = refs[:3], refs[3:9], refs[9:10], refs[10:13]
    flat_ref, rest_sem = refs[13:]
    rows = arrays[0].shape[0]
    half = rows // 2
    heads = qx_ref.shape[1] * GROUP
    rest_copy = pltpu.make_async_copy(rest_hbm, flat_ref.at[0, pl.ds(0, heads)], rest_sem)
    rest_copy.start()
    found = project_quads(chosen, lambda quad: None, found_ref[...], *arrays, qx_ref, do_ref)
    flat_ref[1] = jnp.transpose(found)
    rest_copy.wait()
    low = lax.broadcasted_iota(jnp.int32, (heads // 2, rows), 1) < half
    for kind in range(2):
        even = flat_ref[kind, pl.ds(0, heads // 2, 2), :]
        odd = flat_ref[kind, pl.ds(1, heads // 2, 2), :]
        stats_ref[2 * kind] = jnp.where(low, even, pltpu.roll(odd, half, 1))
        stats_ref[2 * kind + 1] = jnp.where(low, pltpu.roll(even, half, 1), odd)


def place_keys(keys_ref, mine_ref, other_ref):
    half = mine_ref.shape[0] // 2
    even = lax.axis_index("head") % 2 == 0

    def place(near, far):
        for at, (ref, start) in enumerate(((near, 0), (far, 0), (far, half), (near, half))):
            keys_ref[at * half : (at + 1) * half] = ref[start : start + half]

    @pl.when(even)
    def _():
        place(mine_ref, other_ref)

    @pl.when(jnp.logical_not(even))
    def _():
        place(other_ref, mine_ref)


def weigh_quad(scale, rest_of, delta_of, parts, span, lane_tile, start, ds_ref, pt_ref):
    for i in range(span // lane_tile):
        lanes = slice(i * lane_tile, (i + 1) * lane_tile)
        rest, delta = rest_of(i), delta_of(i)
        met = [part(lanes) for part in parts]
        top = rest
        for s, _ in met:
            top = jnp.maximum(top, jnp.max(s, axis=0, keepdims=True))
        exps = [jnp.exp(s - top) for s, _ in met]
        mass = jnp.exp(rest - top)
        for e in exps:
            mass = mass + jnp.sum(e, axis=0, keepdims=True)
        inverse = 1.0 / mass
        cols = slice(start + i * lane_tile, start + (i + 1) * lane_tile)
        at = 0
        for e, (_, p) in zip(exps, met):
            prob = e * inverse
            place = slice(at, at + e.shape[0])
            pt_ref[place, cols] = prob.astype(jnp.bfloat16)
            ds_ref[place, cols] = (prob * (p - delta) * scale).astype(jnp.bfloat16)
            at += e.shape[0]


def key_terms(qx_ref, do_ref, late, picked, ds_ref, pt_ref):
    quads, span, wide = qx_ref.shape[1:]
    width = do_ref.shape[3]
    q = qx_ref[late].reshape(quads * span, wide)
    d = do_ref[late].reshape(quads * span, width)
    lat = dot(ds_ref[picked], q[:, :width]) + dot(pt_ref[picked], d)
    return lat, dot(ds_ref[picked], q[:, width:])


def put(ref, place, terms, picked):
    width = terms[0].shape[1]
    ref[place, :width] = terms[0][picked].astype(ref.dtype)
    ref[place, width:] = terms[1][picked].astype(ref.dtype)


def ahead_kernel(scale, qx_ref, do_ref, own_ref, sl_ref, se_ref, pl_ref, pe_ref):
    quads, rows, span = sl_ref.shape
    half = rows // 2
    width = do_ref.shape[3]

    @pl.when(lax.axis_index("ctx") == 0)
    def _():
        key = lax.broadcasted_iota(jnp.int32, (half, span), 0)
        causal = key <= lax.broadcasted_iota(jnp.int32, (half, span), 1) % half
        for quad in range(quads):
            s = dot(own_ref[...], qx_ref[1, quad], NT) * scale
            sl_ref[quad, :half] = s[:half]
            sl_ref[quad, half:] = jnp.where(causal, s[half:], -jnp.inf)
            pl_ref[quad] = dot(own_ref[:, :width], do_ref[1, quad], NT)
            s = dot(own_ref[:half], qx_ref[0, quad], NT) * scale
            se_ref[quad] = jnp.where(causal, s, -jnp.inf)
            pe_ref[quad] = dot(own_ref[:half, :width], do_ref[0, quad], NT)


def scores_kernel(
    scale, qx_ref, do_ref, stats_ref, own_ref, mine_ref, other_ref, sl_ref, se_ref, pl_ref, pe_ref,
    dsl_ref, dse_ref, ptl_ref, pte_ref, keep_ref, give_ref, keys_ref, first_ref, s_ref, p_ref,
):
    rank = lax.axis_index("ctx")
    quads, span, _ = qx_ref.shape[1:]
    width = do_ref.shape[3]
    rows = own_ref.shape[0]
    half = rows // 2
    place_keys(keys_ref.at[pl.ds(rows, 2 * rows)], mine_ref, other_ref)
    keys_ref[:rows] = own_ref[...]
    first_ref[:half] = own_ref[:half]
    first_ref[half:] = keys_ref[rows : 2 * rows]
    key = lax.broadcasted_iota(jnp.int32, (half, rows), 0)
    causal = key <= lax.broadcasted_iota(jnp.int32, (half, rows), 1) % half

    def multiply(slot, late, quad, count):
        keys = keys_ref if late else first_ref
        s_ref[slot, :count] = dot(keys[:count], qx_ref[late, quad], NT)
        p_ref[slot, :count] = dot(keys[:count, :width], do_ref[late, quad], NT)

    def multiply_away(slot, late, quad):
        if late:
            s_ref[slot, : 2 * rows] = dot(keys_ref[rows:], qx_ref[late, quad], NT)
            p_ref[slot, : 2 * rows] = dot(keys_ref[rows:, :width], do_ref[late, quad], NT)

    def plain_of(slot):
        def plain(start, stop):
            return lambda lanes: (s_ref[slot, start:stop, lanes] * scale, p_ref[slot, start:stop, lanes])

        return plain

    def weigh_away(slot, late, quad):
        own_s, own_p = (sl_ref, pl_ref) if late else (se_ref, pe_ref)
        ready = lambda lanes: (own_s[quad, :, lanes], own_p[quad, :, lanes])
        weigh_parts(late, quad, [ready] + ([plain_of(slot)(0, 2 * rows)] if late else []))

    def weigh_parts(late, quad, parts):
        ds_ref, pt_ref = (dsl_ref, ptl_ref) if late else (dse_ref, pte_ref)
        tiles = span // rows
        weigh_quad(
            scale,
            lambda i: stats_ref[late, tiles * quad + i : tiles * quad + i + 1],
            lambda i: stats_ref[2 + late, tiles * quad + i : tiles * quad + i + 1],
            parts, span, rows, quad * span, ds_ref, pt_ref,
        )

    def weigh(slot, late, quad, count):
        diagonal = half if late else 0
        plain = plain_of(slot)

        def masked(lanes):
            s, p = plain(diagonal, diagonal + half)(lanes)
            return jnp.where(causal, s, -jnp.inf), p

        parts = [plain(0, half)] if late else []
        parts.append(masked)
        if count > diagonal + half:
            parts.append(plain(diagonal + half, count))
        weigh_parts(late, quad, parts)

    def run(late_count, early_count, known=0):
        items = []
        for quad in range(quads):
            for late, count in ((1, rows + late_count), (0, half + early_count)):
                if quad < known:
                    items.append((multiply_away, weigh_away, (late, quad)))
                else:
                    items.append((multiply, weigh, (late, quad, count)))
        items[0][0](0, *items[0][2])
        for i, (_, weigh_item, item) in enumerate(items):
            if i + 1 < len(items):
                items[i + 1][0]((i + 1) % SLOTS, *items[i + 1][2])
            weigh_item(i % SLOTS, *item)

    first, second = slice(0, half), slice(half, rows)
    terms = functools.partial(key_terms, qx_ref, do_ref)

    even = lax.axis_index("head") % 2 == 0

    def share(place, of, near, far):
        @pl.when(even)
        def _():
            put(keep_ref, place, of, near)
            put(give_ref, place, of, far)

        @pl.when(jnp.logical_not(even))
        def _():
            put(keep_ref, place, of, far)
            put(give_ref, place, of, near)

    @pl.when(rank >= HOPS - 1)
    def _():
        run(rows, rows)
        late = terms(1, pl.ds(rows, rows), dsl_ref, ptl_ref)
        early = terms(0, pl.ds(half, rows), dse_ref, pte_ref)
        share(first, (late[0] + early[0], late[1] + early[1]), first, second)
        for ref in (keep_ref, give_ref):
            ref[second] = jnp.zeros_like(ref[second])

    @pl.when(rank == 1)
    def _():
        dse_ref[rows:] = jnp.zeros_like(dse_ref[rows:])
        dsl_ref[2 * rows + half :] = jnp.zeros_like(dsl_ref[2 * rows + half :])
        run(rows + half, half)
        late = terms(1, pl.ds(rows, rows + half), dsl_ref, ptl_ref)
        early = terms(0, pl.ds(half, half), dse_ref, pte_ref)
        seconds = slice(rows, rows + half)
        both = tuple(
            jnp.concatenate([a[first] + b, a[second], a[seconds], jnp.zeros_like(b)], axis=0)
            for a, b in zip(late, early)
        )
        share(first, both, first, second)
        share(second, both, slice(rows + half, 2 * rows), seconds)

    @pl.when(rank == 0)
    def _():
        dse_ref[half:] = jnp.zeros_like(dse_ref[half:])
        run(2 * rows, 0, sl_ref.shape[0])
        late = terms(1, pl.ds(rows, 2 * rows), dsl_ref, ptl_ref)
        share(first, late, first, second)
        share(second, late, slice(rows + half, 2 * rows), slice(rows, rows + half))


def own_terms(qx_ref, do_ref, dsl_ref, dse_ref, ptl_ref, pte_ref, grad_ref):
    rows = grad_ref.shape[0]
    half = rows // 2
    first, second = slice(0, half), slice(half, rows)
    late = key_terms(qx_ref, do_ref, 1, pl.ds(0, rows), dsl_ref, ptl_ref)
    early = key_terms(qx_ref, do_ref, 0, pl.ds(0, half), dse_ref, pte_ref)
    put(grad_ref, first, (late[0][first] + early[0], late[1][first] + early[1]), first)
    put(grad_ref, second, late, second)


def own_early_kernel(*refs):
    @pl.when(lax.axis_index("ctx") < HOPS - 1)
    def _():
        own_terms(*refs)


def own_late_kernel(*refs):
    *given, made_ref, grad_ref = refs
    wrapped = lax.axis_index("ctx") < HOPS - 1

    @pl.when(wrapped)
    def _():
        grad_ref[...] = made_ref[...]

    @pl.when(jnp.logical_not(wrapped))
    def _():
        own_terms(*given, grad_ref)


def pair_kernel(keep_ref, got_ref, out_ref):
    out_ref[...] = (keep_ref[...] + got_ref[...].astype(jnp.float32)).astype(out_ref.dtype)


def query_kernel(chosen, dsl_ref, dse_ref, own_ref, mine_ref, other_ref, wk_ref, *rest):
    last = len(rest) > 5
    if last:
        made_nope, made_rope, dnope_hbm, drope_hbm, keys_ref, first_ref, dq_ref, dnope, drope, sems = rest
    else:
        dnope, drope, keys_ref, first_ref, dq_ref = rest
    rank = lax.axis_index("ctx")
    rows, wide = own_ref.shape
    width = wk_ref.shape[0]
    half = rows // 2
    span = GROUP * half
    quads = dsl_ref.shape[1] // span
    lanes = lax.broadcasted_iota(jnp.int32, (rows, HEAD_WIDTH), 1)
    place_keys(keys_ref.at[pl.ds(rows, 2 * rows)], mine_ref, other_ref)
    keys_ref[:rows] = own_ref[...]
    first_ref[:half] = own_ref[:half]
    first_ref[half:] = keys_ref[rows : 2 * rows]

    def copies(quad):
        sources = (dnope, drope) if quad in chosen else (made_nope, made_rope)
        for i, (source, target) in enumerate(zip(sources, (dnope_hbm, drope_hbm))):
            size = source.shape[1] // quads
            cols = slice(quad * size, (quad + 1) * size)
            yield pltpu.make_async_copy(source.at[:, cols], target.at[:, cols], sems.at[quad, i])

    if last:
        for quad in range(chosen[0]):
            for copy in copies(quad):
                copy.start()

    def meet(quad, late_count):
        cols = slice(quad * span, (quad + 1) * span)
        slot = quad % 2
        late = dot(dsl_ref[:late_count, cols], keys_ref[:late_count], TN)
        early = dot(dse_ref[:, cols], first_ref[...], TN)
        dq_ref[slot, 1] = late.astype(jnp.bfloat16)
        dq_ref[slot, 0] = early.astype(jnp.bfloat16)

    def leave(quad):
        slot = quad % 2

        def head(g, place):
            mine = slice(g * half, (g + 1) * half)
            return jnp.concatenate([dq_ref[slot, 0, mine, place], dq_ref[slot, 1, mine, place]], axis=0)

        for g in range(GROUP):
            at = quad * GROUP + g
            out = slice(at * HEAD_WIDTH, (at + 1) * HEAD_WIDTH)
            dnope[:, out] = dot(head(g, slice(0, width)), wk_ref[:, out]).astype(jnp.bfloat16)
            if g % 2 == 1:
                both = slice(width, wide)
                pair = jnp.where(lanes < HEAD_WIDTH // 2, head(g - 1, both), head(g, both))
                drope[:, (at // 2) * HEAD_WIDTH : (at // 2 + 1) * HEAD_WIDTH] = pair
        if last:
            for copy in copies(quad):
                copy.start()

    def run(late_count):
        meet(chosen[0], late_count)
        for quad in chosen:
            if quad + 1 in chosen:
                meet(quad + 1, late_count)
            leave(quad)

    @pl.when(rank >= HOPS - 1)
    def _():
        run(2 * rows)

    @pl.when(rank < HOPS - 1)
    def _():
        run(3 * rows)

    if last:
        for quad in range(quads):
            for copy in copies(quad):
                copy.wait()


def finish_kernel(own_ref, other_ref, mine_ref, sent_ref, lat_ref, rot_ref):
    width = lat_ref.shape[1]
    narrow = rot_ref.shape[0]
    away = mine_ref[...].astype(jnp.float32) + sent_ref[...].astype(jnp.float32)
    total = (own_ref[...] + other_ref[...]) + away
    lat_ref[...] = total[:, :width]
    rot_ref[...] = jnp.transpose(total[:, width : width + narrow] + total[:, width + narrow :])


VMEM = pl.BlockSpec(memory_space=pltpu.VMEM)
HBM = pl.BlockSpec(memory_space=pltpu.HBM)


def in_hbm(*arrays):
    return [pltpu.with_memory_space_constraint(array, pltpu.HBM) for array in arrays]


def per_device(
    q_nope, q_rope, latent, k_rope, d_out, out_heads, lse_rest, key_up_weight, value_up_weight
):
    rows, width = latent.shape
    narrow = k_rope.shape[1]
    wide = width + 2 * narrow
    half = rows // 2
    heads = key_up_weight.shape[1] // HEAD_WIDTH
    quads, span = heads // GROUP, GROUP * half
    scale = (HEAD_WIDTH + narrow) ** (-0.5)
    bf16, f32 = jnp.bfloat16, jnp.float32
    total = heads * rows

    own = pl.pallas_call(
        pack_kernel,
        out_shape=jax.ShapeDtypeStruct((rows, wide), bf16),
        in_specs=[VMEM, VMEM],
        out_specs=VMEM,
        compiler_params=params(4),
        name="pack",
    )(*in_hbm(latent, jnp.transpose(k_rope)))
    mine = between_groups(own, 1)

    qx_shape = pltpu.VMEM((2, quads, span, wide), bf16)
    do_shape = pltpu.VMEM((2, quads, span, width), bf16)
    streamed = (q_nope, q_rope, d_out, out_heads, key_up_weight, value_up_weight)
    held = quads - 3 * quads // 8
    qx, do_lat, found, *loaded = pl.pallas_call(
        functools.partial(project_kernel, range(held)),
        out_shape=(qx_shape, do_shape, pltpu.VMEM((rows, HEAD_WIDTH), f32))
        + tuple(pltpu.VMEM(array.shape, bf16) for array in streamed),
        in_specs=[HBM] * 6,
        out_specs=[VMEM] * 9,
        scratch_shapes=[pltpu.SemaphoreType.DMA((quads, 6))],
        compiler_params=params(8),
        cost_estimate=cost(4 * total * HEAD_WIDTH * width, 12 * MIB),
        name="project",
    )(*in_hbm(*streamed))
    late_own = pltpu.VMEM((held, rows, span), f32)
    early_own = pltpu.VMEM((held, half, span), f32)
    ahead = pl.pallas_call(
        functools.partial(ahead_kernel, scale),
        out_shape=(late_own, early_own, late_own, early_own),
        in_specs=[VMEM] * 3,
        out_specs=[VMEM] * 4,
        compiler_params=params(4),
        cost_estimate=cost(MIB, MIB),
        name="ahead",
    )(qx, do_lat, own)
    mine, found, *ahead = lax.optimization_barrier((mine, found, *ahead))
    other = with_partner(mine)
    qx, do_lat, stats = pl.pallas_call(
        functools.partial(project_rest_kernel, range(held, quads)),
        out_shape=(qx_shape, do_shape, pltpu.VMEM((4, heads // 2, rows), f32)),
        in_specs=[VMEM] * 9 + [HBM],
        out_specs=[VMEM] * 3,
        input_output_aliases={0: 0, 1: 1},
        scratch_shapes=[pltpu.VMEM((2, HEAD_WIDTH, rows), f32), pltpu.SemaphoreType.DMA],
        compiler_params=params(8),
        cost_estimate=cost(total * HEAD_WIDTH * width, 4 * MIB),
        name="project_rest",
    )(qx, do_lat, found, *loaded, *in_hbm(jnp.transpose(lse_rest)))
    other, stats = lax.optimization_barrier((other, stats))

    late = pltpu.VMEM((3 * rows, quads * span), bf16)
    early = pltpu.VMEM((rows + half, quads * span), bf16)
    slots = pltpu.VMEM((SLOTS, 3 * rows, span), f32)
    *terms, keep, give = pl.pallas_call(
        functools.partial(scores_kernel, scale),
        out_shape=(
            late, early, late, early,
            jax.ShapeDtypeStruct((rows, wide), f32),
            jax.ShapeDtypeStruct((rows, wide), bf16),
        ),
        in_specs=[VMEM] * 10,
        out_specs=[VMEM] * 6,
        scratch_shapes=[
            pltpu.VMEM((3 * rows, wide), bf16),
            pltpu.VMEM((rows + half, wide), bf16),
            slots,
            slots,
        ],
        compiler_params=params(16),
        cost_estimate=cost(8 * total * rows * width, 16 * MIB),
        name="scores",
    )(qx, do_lat, stats, own, mine, other, *ahead)
    got = with_partner(give)
    def own_part(kernel, name, work, *given):
        return pl.pallas_call(
            kernel,
            out_shape=pltpu.VMEM((rows, wide), f32),
            in_specs=[VMEM] * len(given),
            out_specs=VMEM,
            compiler_params=params(8),
            cost_estimate=work,
            name=name,
        )(*given)

    grad = own_part(own_early_kernel, "own_early", cost(MIB, MIB), qx, do_lat, *terms)
    got, grad = lax.optimization_barrier((got, grad))
    summed = pl.pallas_call(
        pair_kernel,
        out_shape=jax.ShapeDtypeStruct((rows, wide), bf16),
        in_specs=[VMEM] * 2,
        out_specs=VMEM,
        compiler_params=params(4),
        name="pair",
    )(keep, got)
    summed, grad = lax.optimization_barrier((summed, grad))
    arrived = between_groups(summed, -1)
    work = cost(4 * total * rows * width, 16 * MIB)
    grad = own_part(own_late_kernel, "own", work, qx, do_lat, *terms, grad)

    def queries(name, chosen, *made):
        shapes = (rows, heads * HEAD_WIDTH), (rows, heads * narrow)
        kind = functools.partial(jax.ShapeDtypeStruct, dtype=bf16) if made else functools.partial(pltpu.VMEM, dtype=bf16)
        own_copies = [pltpu.VMEM(shape, bf16) for shape in shapes] + [pltpu.SemaphoreType.DMA((quads, 2))]
        return pl.pallas_call(
            functools.partial(query_kernel, chosen),
            out_shape=tuple(kind(shape) for shape in shapes),
            in_specs=[VMEM] * (6 + len(made)),
            out_specs=[HBM if made else VMEM] * 2,
            scratch_shapes=[
                pltpu.VMEM((3 * rows, wide), bf16),
                pltpu.VMEM((rows + half, wide), bf16),
                pltpu.VMEM((2, 2, span, wide), bf16),
            ]
            + (own_copies if made else []),
            compiler_params=params(12),
            cost_estimate=cost(3 * total * rows * width, 8 * MIB),
            name=name,
        )(terms[0], terms[1], own, mine, other, loaded[4], *made)

    sharers = lax.axis_size("head")
    bit = 1
    while 2 * bit < sharers:
        grad = grad + with_partner(grad, bit)
        bit *= 2
    grad_other = with_partner(grad, bit)
    cut = quads - 1
    made = queries("query", range(cut))
    arrived, *made = lax.optimization_barrier((arrived, *made))
    bit = 1
    while 2 * bit < sharers:
        arrived = (arrived.astype(f32) + with_partner(arrived, bit).astype(f32)).astype(bf16)
        bit *= 2
    arrived_other = with_partner(arrived, bit)
    d_q_nope, d_q_rope = queries("query_rest", range(cut, quads), *made)
    arrived_other, d_q_nope = lax.optimization_barrier((arrived_other, d_q_nope))
    latent_gradient, d_k_rope = pl.pallas_call(
        finish_kernel,
        out_shape=(
            jax.ShapeDtypeStruct((rows, width), f32),
            jax.ShapeDtypeStruct((narrow, rows), f32),
        ),
        in_specs=[VMEM] * 4,
        out_specs=[VMEM] * 2,
        compiler_params=params(4),
        name="finish",
    )(grad, grad_other, arrived, arrived_other)
    return d_q_nope, d_q_rope, latent_gradient, jnp.transpose(d_k_rope)


def solution(mesh):
    placed = (
        P("ctx", "head"),
        P("ctx", "head"),
        P("ctx", None),
        P("ctx", None),
        P("ctx", "head"),
        P("ctx", "head"),
        P("ctx", "head"),
        P(None, "head"),
        P(None, "head"),
    )
    return jax.shard_map(
        per_device,
        mesh=mesh,
        in_specs=placed,
        out_specs=(P("ctx", "head"), P("ctx", "head"), P("ctx", None), P("ctx", None)),
        check_vma=False,
    )
```

```python
import functools

import jax
import jax.numpy as jnp
from jax import lax
from jax.experimental import pallas as pl
from jax.experimental.pallas import tpu as pltpu
from jax.sharding import PartitionSpec as P

HEAD_WIDTH = 128
HOPS = 3
GROUP = 4
SLOTS = 4
MIB = 1 << 20

NT = (((1,), (1,)), ((), ()))
TN = (((0,), (0,)), ((), ()))


def dot(a, b, dims=(((1,), (0,)), ((), ()))):
    return lax.dot_general(a, b, dims, preferred_element_type=jnp.float32)


def between_groups(block, direction):
    groups, sharers = lax.axis_size("ctx"), lax.axis_size("head")
    route = []
    for group in range(groups):
        for head in range(sharers):
            to = (group + direction * (1 + head % 2)) % groups
            route.append((group * sharers + head, to * sharers + head))
    return lax.ppermute(block, ("ctx", "head"), route)


def with_partner(block, bit=1):
    return lax.ppermute(block, "head", [(i, i ^ bit) for i in range(lax.axis_size("head"))])


def params(limit_mib):
    return pltpu.CompilerParams(vmem_limit_bytes=limit_mib * MIB)


def cost(flops, moved):
    return pl.CostEstimate(flops=int(flops), bytes_accessed=int(moved), transcendentals=0)


def pack_kernel(lat_ref, rot_ref, out_ref):
    width = lat_ref.shape[1]
    rot = jnp.transpose(rot_ref[...].astype(jnp.float32)).astype(out_ref.dtype)
    out_ref[:, :width] = lat_ref[...]
    out_ref[:, width:] = jnp.concatenate([rot, rot], axis=1)


def project_quads(chosen, arrive, found, nope, rope, dout, saved, wk, wv, qx_ref, do_ref):
    rows = nope.shape[0]
    width = wk.shape[0]
    half = rows // 2
    lanes = lax.broadcasted_iota(jnp.int32, (rows, HEAD_WIDTH), 1)
    for quad in chosen:
        arrive(quad)
        for g in range(GROUP):
            at = quad * GROUP + g
            cols = slice(at * HEAD_WIDTH, (at + 1) * HEAD_WIDTH)
            place = slice(g * half, (g + 1) * half)
            d_out = dout[:, cols]
            q_abs = dot(nope[:, cols], wk[:, cols], NT).astype(jnp.bfloat16)
            d_lat = dot(d_out, wv[:, cols], NT).astype(jnp.bfloat16)
            pair = rope[:, (at // 2) * HEAD_WIDTH : (at // 2 + 1) * HEAD_WIDTH]
            mine = (lanes < HEAD_WIDTH // 2) if g % 2 == 0 else (lanes >= HEAD_WIDTH // 2)
            pair = jnp.where(mine, pair, jnp.zeros_like(pair))
            for late, part in ((0, slice(0, half)), (1, slice(half, rows))):
                qx_ref[late, quad, place, :width] = q_abs[part]
                qx_ref[late, quad, place, width:] = pair[part]
                do_ref[late, quad, place] = d_lat[part]
            prod = d_out.astype(jnp.float32) * saved[:, cols].astype(jnp.float32)
            delta = jnp.sum(prod, axis=1, keepdims=True)
            found = jnp.where(lanes == at, delta, found)
    return found


def project_kernel(chosen, *refs):
    sources, (qx_ref, do_ref, found_ref), targets, (sems,) = refs[:6], refs[6:9], refs[9:15], refs[15:]
    quads = qx_ref.shape[1]
    groups = [(0, 1), (1, 2)] + [(i, min(i + 2, quads)) for i in range(2, quads, 2)]

    def copies(index):
        start, stop = groups[index]
        for i in (4, 0, 5, 2, 3, 1):
            size = sources[i].shape[1] // quads
            cols = slice(start * size, stop * size)
            yield pltpu.make_async_copy(sources[i].at[:, cols], targets[i].at[:, cols], sems.at[index, i])

    def arrive(quad):
        for index, (start, _) in enumerate(groups):
            if start == quad:
                for copy in copies(index):
                    copy.wait()

    for index in range(len(groups)):
        for copy in copies(index):
            copy.start()
    found = jnp.zeros(found_ref.shape, jnp.float32)
    found_ref[...] = project_quads(chosen, arrive, found, *targets, qx_ref, do_ref)
    for quad in range(len(chosen), quads):
        arrive(quad)


def project_rest_kernel(chosen, *refs):
    (_, _, found_ref), arrays, (rest_hbm,), (qx_ref, do_ref, stats_ref) = refs[:3], refs[3:9], refs[9:10], refs[10:13]
    flat_ref, rest_sem = refs[13:]
    rows = arrays[0].shape[0]
    half = rows // 2
    heads = qx_ref.shape[1] * GROUP
    rest_copy = pltpu.make_async_copy(rest_hbm, flat_ref.at[0, pl.ds(0, heads)], rest_sem)
    rest_copy.start()
    found = project_quads(chosen, lambda quad: None, found_ref[...], *arrays, qx_ref, do_ref)
    flat_ref[1] = jnp.transpose(found)
    rest_copy.wait()
    low = lax.broadcasted_iota(jnp.int32, (heads // 2, rows), 1) < half
    for kind in range(2):
        even = flat_ref[kind, pl.ds(0, heads // 2, 2), :]
        odd = flat_ref[kind, pl.ds(1, heads // 2, 2), :]
        stats_ref[2 * kind] = jnp.where(low, even, pltpu.roll(odd, half, 1))
        stats_ref[2 * kind + 1] = jnp.where(low, pltpu.roll(even, half, 1), odd)


def place_keys(keys_ref, mine_ref, other_ref):
    half = mine_ref.shape[0] // 2
    even = lax.axis_index("head") % 2 == 0

    def place(near, far):
        for at, (ref, start) in enumerate(((near, 0), (far, 0), (far, half), (near, half))):
            keys_ref[at * half : (at + 1) * half] = ref[start : start + half]

    @pl.when(even)
    def _():
        place(mine_ref, other_ref)

    @pl.when(jnp.logical_not(even))
    def _():
        place(other_ref, mine_ref)


def weigh_quad(scale, rest_of, delta_of, parts, span, lane_tile, start, ds_ref, pt_ref):
    for i in range(span // lane_tile):
        lanes = slice(i * lane_tile, (i + 1) * lane_tile)
        rest, delta = rest_of(i), delta_of(i)
        met = [part(lanes) for part in parts]
        top = rest
        for s, _ in met:
            top = jnp.maximum(top, jnp.max(s, axis=0, keepdims=True))
        exps = [jnp.exp(s - top) for s, _ in met]
        mass = jnp.exp(rest - top)
        for e in exps:
            mass = mass + jnp.sum(e, axis=0, keepdims=True)
        inverse = 1.0 / mass
        cols = slice(start + i * lane_tile, start + (i + 1) * lane_tile)
        at = 0
        for e, (_, p) in zip(exps, met):
            prob = e * inverse
            place = slice(at, at + e.shape[0])
            pt_ref[place, cols] = prob.astype(jnp.bfloat16)
            ds_ref[place, cols] = (prob * (p - delta) * scale).astype(jnp.bfloat16)
            at += e.shape[0]


def key_terms(qx_ref, do_ref, late, picked, ds_ref, pt_ref):
    quads, span, wide = qx_ref.shape[1:]
    width = do_ref.shape[3]
    q = qx_ref[late].reshape(quads * span, wide)
    d = do_ref[late].reshape(quads * span, width)
    lat = dot(ds_ref[picked], q[:, :width]) + dot(pt_ref[picked], d)
    return lat, dot(ds_ref[picked], q[:, width:])


def put(ref, place, terms, picked):
    width = terms[0].shape[1]
    ref[place, :width] = terms[0][picked].astype(ref.dtype)
    ref[place, width:] = terms[1][picked].astype(ref.dtype)


def ahead_kernel(scale, qx_ref, do_ref, own_ref, sl_ref, se_ref, pl_ref, pe_ref):
    quads, rows, span = sl_ref.shape
    half = rows // 2
    width = do_ref.shape[3]

    @pl.when(lax.axis_index("ctx") == 0)
    def _():
        key = lax.broadcasted_iota(jnp.int32, (half, span), 0)
        causal = key <= lax.broadcasted_iota(jnp.int32, (half, span), 1) % half
        for quad in range(quads):
            s = dot(own_ref[...], qx_ref[1, quad], NT) * scale
            sl_ref[quad, :half] = s[:half]
            sl_ref[quad, half:] = jnp.where(causal, s[half:], -jnp.inf)
            pl_ref[quad] = dot(own_ref[:, :width], do_ref[1, quad], NT)
            s = dot(own_ref[:half], qx_ref[0, quad], NT) * scale
            se_ref[quad] = jnp.where(causal, s, -jnp.inf)
            pe_ref[quad] = dot(own_ref[:half, :width], do_ref[0, quad], NT)


def scores_kernel(
    scale, qx_ref, do_ref, stats_ref, own_ref, mine_ref, other_ref, sl_ref, se_ref, pl_ref, pe_ref,
    dsl_ref, dse_ref, ptl_ref, pte_ref, keep_ref, give_ref, keys_ref, first_ref, s_ref, p_ref,
):
    rank = lax.axis_index("ctx")
    quads, span, _ = qx_ref.shape[1:]
    width = do_ref.shape[3]
    rows = own_ref.shape[0]
    half = rows // 2
    place_keys(keys_ref.at[pl.ds(rows, 2 * rows)], mine_ref, other_ref)
    keys_ref[:rows] = own_ref[...]
    first_ref[:half] = own_ref[:half]
    first_ref[half:] = keys_ref[rows : 2 * rows]
    key = lax.broadcasted_iota(jnp.int32, (half, rows), 0)
    causal = key <= lax.broadcasted_iota(jnp.int32, (half, rows), 1) % half

    def multiply(slot, late, quad, count):
        keys = keys_ref if late else first_ref
        s_ref[slot, :count] = dot(keys[:count], qx_ref[late, quad], NT)
        p_ref[slot, :count] = dot(keys[:count, :width], do_ref[late, quad], NT)

    def multiply_away(slot, late, quad):
        if late:
            s_ref[slot, : 2 * rows] = dot(keys_ref[rows:], qx_ref[late, quad], NT)
            p_ref[slot, : 2 * rows] = dot(keys_ref[rows:, :width], do_ref[late, quad], NT)

    def plain_of(slot):
        def plain(start, stop):
            return lambda lanes: (s_ref[slot, start:stop, lanes] * scale, p_ref[slot, start:stop, lanes])

        return plain

    def weigh_away(slot, late, quad):
        own_s, own_p = (sl_ref, pl_ref) if late else (se_ref, pe_ref)
        ready = lambda lanes: (own_s[quad, :, lanes], own_p[quad, :, lanes])
        weigh_parts(late, quad, [ready] + ([plain_of(slot)(0, 2 * rows)] if late else []))

    def weigh_parts(late, quad, parts):
        ds_ref, pt_ref = (dsl_ref, ptl_ref) if late else (dse_ref, pte_ref)
        tiles = span // rows
        weigh_quad(
            scale,
            lambda i: stats_ref[late, tiles * quad + i : tiles * quad + i + 1],
            lambda i: stats_ref[2 + late, tiles * quad + i : tiles * quad + i + 1],
            parts, span, rows, quad * span, ds_ref, pt_ref,
        )

    def weigh(slot, late, quad, count):
        diagonal = half if late else 0
        plain = plain_of(slot)

        def masked(lanes):
            s, p = plain(diagonal, diagonal + half)(lanes)
            return jnp.where(causal, s, -jnp.inf), p

        parts = [plain(0, half)] if late else []
        parts.append(masked)
        if count > diagonal + half:
            parts.append(plain(diagonal + half, count))
        weigh_parts(late, quad, parts)

    def run(late_count, early_count, known=0):
        items = []
        for quad in range(quads):
            for late, count in ((1, rows + late_count), (0, half + early_count)):
                if quad < known:
                    items.append((multiply_away, weigh_away, (late, quad)))
                else:
                    items.append((multiply, weigh, (late, quad, count)))
        items[0][0](0, *items[0][2])
        for i, (_, weigh_item, item) in enumerate(items):
            if i + 1 < len(items):
                items[i + 1][0]((i + 1) % SLOTS, *items[i + 1][2])
            weigh_item(i % SLOTS, *item)

    first, second = slice(0, half), slice(half, rows)
    terms = functools.partial(key_terms, qx_ref, do_ref)

    even = lax.axis_index("head") % 2 == 0

    def share(place, of, near, far):
        @pl.when(even)
        def _():
            put(keep_ref, place, of, near)
            put(give_ref, place, of, far)

        @pl.when(jnp.logical_not(even))
        def _():
            put(keep_ref, place, of, far)
            put(give_ref, place, of, near)

    @pl.when(rank >= HOPS - 1)
    def _():
        run(rows, rows)
        late = terms(1, pl.ds(rows, rows), dsl_ref, ptl_ref)
        early = terms(0, pl.ds(half, rows), dse_ref, pte_ref)
        share(first, (late[0] + early[0], late[1] + early[1]), first, second)
        for ref in (keep_ref, give_ref):
            ref[second] = jnp.zeros_like(ref[second])

    @pl.when(rank == 1)
    def _():
        dse_ref[rows:] = jnp.zeros_like(dse_ref[rows:])
        dsl_ref[2 * rows + half :] = jnp.zeros_like(dsl_ref[2 * rows + half :])
        run(rows + half, half)
        late = terms(1, pl.ds(rows, rows + half), dsl_ref, ptl_ref)
        early = terms(0, pl.ds(half, half), dse_ref, pte_ref)
        seconds = slice(rows, rows + half)
        both = tuple(
            jnp.concatenate([a[first] + b, a[second], a[seconds], jnp.zeros_like(b)], axis=0)
            for a, b in zip(late, early)
        )
        share(first, both, first, second)
        share(second, both, slice(rows + half, 2 * rows), seconds)

    @pl.when(rank == 0)
    def _():
        dse_ref[half:] = jnp.zeros_like(dse_ref[half:])
        run(2 * rows, 0, sl_ref.shape[0])
        late = terms(1, pl.ds(rows, 2 * rows), dsl_ref, ptl_ref)
        share(first, late, first, second)
        share(second, late, slice(rows + half, 2 * rows), slice(rows, rows + half))


def own_terms(qx_ref, do_ref, dsl_ref, dse_ref, ptl_ref, pte_ref, grad_ref):
    rows = grad_ref.shape[0]
    half = rows // 2
    first, second = slice(0, half), slice(half, rows)
    late = key_terms(qx_ref, do_ref, 1, pl.ds(0, rows), dsl_ref, ptl_ref)
    early = key_terms(qx_ref, do_ref, 0, pl.ds(0, half), dse_ref, pte_ref)
    put(grad_ref, first, (late[0][first] + early[0], late[1][first] + early[1]), first)
    put(grad_ref, second, late, second)


def own_early_kernel(*refs):
    @pl.when(lax.axis_index("ctx") < HOPS - 1)
    def _():
        own_terms(*refs)


def own_late_kernel(*refs):
    *given, made_ref, grad_ref = refs
    wrapped = lax.axis_index("ctx") < HOPS - 1

    @pl.when(wrapped)
    def _():
        grad_ref[...] = made_ref[...]

    @pl.when(jnp.logical_not(wrapped))
    def _():
        own_terms(*given, grad_ref)


def pair_kernel(keep_ref, got_ref, out_ref):
    out_ref[...] = (keep_ref[...] + got_ref[...].astype(jnp.float32)).astype(out_ref.dtype)


def query_kernel(chosen, dsl_ref, dse_ref, own_ref, mine_ref, other_ref, wk_ref, *rest):
    last = len(rest) > 5
    if last:
        made_nope, made_rope, dnope_hbm, drope_hbm, keys_ref, first_ref, dq_ref, dnope, drope, sems = rest
    else:
        dnope, drope, keys_ref, first_ref, dq_ref = rest
    rank = lax.axis_index("ctx")
    rows, wide = own_ref.shape
    width = wk_ref.shape[0]
    half = rows // 2
    span = GROUP * half
    quads = dsl_ref.shape[1] // span
    lanes = lax.broadcasted_iota(jnp.int32, (rows, HEAD_WIDTH), 1)
    place_keys(keys_ref.at[pl.ds(rows, 2 * rows)], mine_ref, other_ref)
    keys_ref[:rows] = own_ref[...]
    first_ref[:half] = own_ref[:half]
    first_ref[half:] = keys_ref[rows : 2 * rows]

    def copies(quad):
        sources = (dnope, drope) if quad in chosen else (made_nope, made_rope)
        for i, (source, target) in enumerate(zip(sources, (dnope_hbm, drope_hbm))):
            size = source.shape[1] // quads
            cols = slice(quad * size, (quad + 1) * size)
            yield pltpu.make_async_copy(source.at[:, cols], target.at[:, cols], sems.at[quad, i])

    if last:
        for quad in range(chosen[0]):
            for copy in copies(quad):
                copy.start()

    def meet(quad, late_count):
        cols = slice(quad * span, (quad + 1) * span)
        slot = quad % 2
        late = dot(dsl_ref[:late_count, cols], keys_ref[:late_count], TN)
        early = dot(dse_ref[:, cols], first_ref[...], TN)
        dq_ref[slot, 1] = late.astype(jnp.bfloat16)
        dq_ref[slot, 0] = early.astype(jnp.bfloat16)

    def leave(quad):
        slot = quad % 2

        def head(g, place):
            mine = slice(g * half, (g + 1) * half)
            return jnp.concatenate([dq_ref[slot, 0, mine, place], dq_ref[slot, 1, mine, place]], axis=0)

        for g in range(GROUP):
            at = quad * GROUP + g
            out = slice(at * HEAD_WIDTH, (at + 1) * HEAD_WIDTH)
            dnope[:, out] = dot(head(g, slice(0, width)), wk_ref[:, out]).astype(jnp.bfloat16)
            if g % 2 == 1:
                both = slice(width, wide)
                pair = jnp.where(lanes < HEAD_WIDTH // 2, head(g - 1, both), head(g, both))
                drope[:, (at // 2) * HEAD_WIDTH : (at // 2 + 1) * HEAD_WIDTH] = pair
        if last:
            for copy in copies(quad):
                copy.start()

    def run(late_count):
        meet(chosen[0], late_count)
        for quad in chosen:
            if quad + 1 in chosen:
                meet(quad + 1, late_count)
            leave(quad)

    @pl.when(rank >= HOPS - 1)
    def _():
        run(2 * rows)

    @pl.when(rank < HOPS - 1)
    def _():
        run(3 * rows)

    if last:
        for quad in range(quads):
            for copy in copies(quad):
                copy.wait()


def finish_kernel(own_ref, other_ref, mine_ref, sent_ref, lat_ref, rot_ref):
    width = lat_ref.shape[1]
    narrow = rot_ref.shape[0]
    away = mine_ref[...].astype(jnp.float32) + sent_ref[...].astype(jnp.float32)
    total = (own_ref[...] + other_ref[...]) + away
    lat_ref[...] = total[:, :width]
    rot_ref[...] = jnp.transpose(total[:, width : width + narrow] + total[:, width + narrow :])


VMEM = pl.BlockSpec(memory_space=pltpu.VMEM)
HBM = pl.BlockSpec(memory_space=pltpu.HBM)


def in_hbm(*arrays):
    return [pltpu.with_memory_space_constraint(array, pltpu.HBM) for array in arrays]


def per_device(
    q_nope, q_rope, latent, k_rope, d_out, out_heads, lse_rest, key_up_weight, value_up_weight
):
    rows, width = latent.shape
    narrow = k_rope.shape[1]
    wide = width + 2 * narrow
    half = rows // 2
    heads = key_up_weight.shape[1] // HEAD_WIDTH
    quads, span = heads // GROUP, GROUP * half
    scale = (HEAD_WIDTH + narrow) ** (-0.5)
    bf16, f32 = jnp.bfloat16, jnp.float32
    total = heads * rows

    own = pl.pallas_call(
        pack_kernel,
        out_shape=jax.ShapeDtypeStruct((rows, wide), bf16),
        in_specs=[VMEM, VMEM],
        out_specs=VMEM,
        compiler_params=params(4),
        name="pack",
    )(*in_hbm(latent, jnp.transpose(k_rope)))
    mine = between_groups(own, 1)

    qx_shape = pltpu.VMEM((2, quads, span, wide), bf16)
    do_shape = pltpu.VMEM((2, quads, span, width), bf16)
    streamed = (q_nope, q_rope, d_out, out_heads, key_up_weight, value_up_weight)
    held = quads - quads // 4
    qx, do_lat, found, *loaded = pl.pallas_call(
        functools.partial(project_kernel, range(held)),
        out_shape=(qx_shape, do_shape, pltpu.VMEM((rows, HEAD_WIDTH), f32))
        + tuple(pltpu.VMEM(array.shape, bf16) for array in streamed),
        in_specs=[HBM] * 6,
        out_specs=[VMEM] * 9,
        scratch_shapes=[pltpu.SemaphoreType.DMA((quads, 6))],
        compiler_params=params(8),
        cost_estimate=cost(4 * total * HEAD_WIDTH * width, 12 * MIB),
        name="project",
    )(*in_hbm(*streamed))
    late_own = pltpu.VMEM((held, rows, span), f32)
    early_own = pltpu.VMEM((held, half, span), f32)
    ahead = pl.pallas_call(
        functools.partial(ahead_kernel, scale),
        out_shape=(late_own, early_own, late_own, early_own),
        in_specs=[VMEM] * 3,
        out_specs=[VMEM] * 4,
        compiler_params=params(4),
        cost_estimate=cost(MIB, MIB),
        name="ahead",
    )(qx, do_lat, own)
    mine, found, *ahead = lax.optimization_barrier((mine, found, *ahead))
    other = with_partner(mine)
    qx, do_lat, stats = pl.pallas_call(
        functools.partial(project_rest_kernel, range(held, quads)),
        out_shape=(qx_shape, do_shape, pltpu.VMEM((4, heads // 2, rows), f32)),
        in_specs=[VMEM] * 9 + [HBM],
        out_specs=[VMEM] * 3,
        input_output_aliases={0: 0, 1: 1},
        scratch_shapes=[pltpu.VMEM((2, HEAD_WIDTH, rows), f32), pltpu.SemaphoreType.DMA],
        compiler_params=params(8),
        cost_estimate=cost(total * HEAD_WIDTH * width, 4 * MIB),
        name="project_rest",
    )(qx, do_lat, found, *loaded, *in_hbm(jnp.transpose(lse_rest)))
    other, stats = lax.optimization_barrier((other, stats))

    late = pltpu.VMEM((3 * rows, quads * span), bf16)
    early = pltpu.VMEM((rows + half, quads * span), bf16)
    slots = pltpu.VMEM((SLOTS, 3 * rows, span), f32)
    *terms, keep, give = pl.pallas_call(
        functools.partial(scores_kernel, scale),
        out_shape=(
            late, early, late, early,
            jax.ShapeDtypeStruct((rows, wide), f32),
            jax.ShapeDtypeStruct((rows, wide), bf16),
        ),
        in_specs=[VMEM] * 10,
        out_specs=[VMEM] * 6,
        scratch_shapes=[
            pltpu.VMEM((3 * rows, wide), bf16),
            pltpu.VMEM((rows + half, wide), bf16),
            slots,
            slots,
        ],
        compiler_params=params(16),
        cost_estimate=cost(8 * total * rows * width, 16 * MIB),
        name="scores",
    )(qx, do_lat, stats, own, mine, other, *ahead)
    got = with_partner(give)
    def own_part(kernel, name, work, *given):
        return pl.pallas_call(
            kernel,
            out_shape=pltpu.VMEM((rows, wide), f32),
            in_specs=[VMEM] * len(given),
            out_specs=VMEM,
            compiler_params=params(8),
            cost_estimate=work,
            name=name,
        )(*given)

    grad = own_part(own_early_kernel, "own_early", cost(MIB, MIB), qx, do_lat, *terms)
    got, grad = lax.optimization_barrier((got, grad))
    summed = pl.pallas_call(
        pair_kernel,
        out_shape=jax.ShapeDtypeStruct((rows, wide), bf16),
        in_specs=[VMEM] * 2,
        out_specs=VMEM,
        compiler_params=params(4),
        name="pair",
    )(keep, got)
    summed, grad = lax.optimization_barrier((summed, grad))
    arrived = between_groups(summed, -1)
    work = cost(4 * total * rows * width, 16 * MIB)
    grad = own_part(own_late_kernel, "own", work, qx, do_lat, *terms, grad)

    def queries(name, chosen, *made):
        shapes = (rows, heads * HEAD_WIDTH), (rows, heads * narrow)
        kind = functools.partial(jax.ShapeDtypeStruct, dtype=bf16) if made else functools.partial(pltpu.VMEM, dtype=bf16)
        own_copies = [pltpu.VMEM(shape, bf16) for shape in shapes] + [pltpu.SemaphoreType.DMA((quads, 2))]
        return pl.pallas_call(
            functools.partial(query_kernel, chosen),
            out_shape=tuple(kind(shape) for shape in shapes),
            in_specs=[VMEM] * (6 + len(made)),
            out_specs=[HBM if made else VMEM] * 2,
            scratch_shapes=[
                pltpu.VMEM((3 * rows, wide), bf16),
                pltpu.VMEM((rows + half, wide), bf16),
                pltpu.VMEM((2, 2, span, wide), bf16),
            ]
            + (own_copies if made else []),
            compiler_params=params(12),
            cost_estimate=cost(3 * total * rows * width, 8 * MIB),
            name=name,
        )(terms[0], terms[1], own, mine, other, loaded[4], *made)

    sharers = lax.axis_size("head")
    bit = 1
    while 2 * bit < sharers:
        grad = grad + with_partner(grad, bit)
        bit *= 2
    grad_other = with_partner(grad, bit)
    cut = quads - 1
    made = queries("query", range(cut))
    arrived, *made = lax.optimization_barrier((arrived, *made))
    bit = 1
    while 2 * bit < sharers:
        arrived = (arrived.astype(f32) + with_partner(arrived, bit).astype(f32)).astype(bf16)
        bit *= 2
    arrived_other = with_partner(arrived, bit)
    d_q_nope, d_q_rope = queries("query_rest", range(cut, quads), *made)
    arrived_other, d_q_nope = lax.optimization_barrier((arrived_other, d_q_nope))
    latent_gradient, d_k_rope = pl.pallas_call(
        finish_kernel,
        out_shape=(
            jax.ShapeDtypeStruct((rows, width), f32),
            jax.ShapeDtypeStruct((narrow, rows), f32),
        ),
        in_specs=[VMEM] * 4,
        out_specs=[VMEM] * 2,
        compiler_params=params(4),
        name="finish",
    )(grad, grad_other, arrived, arrived_other)
    return d_q_nope, d_q_rope, latent_gradient, jnp.transpose(d_k_rope)


def solution(mesh):
    placed = (
        P("ctx", "head"),
        P("ctx", "head"),
        P("ctx", None),
        P("ctx", None),
        P("ctx", "head"),
        P("ctx", "head"),
        P("ctx", "head"),
        P(None, "head"),
        P(None, "head"),
    )
    return jax.shard_map(
        per_device,
        mesh=mesh,
        in_specs=placed,
        out_specs=(P("ctx", "head"), P("ctx", "head"), P("ctx", None), P("ctx", None)),
        check_vma=False,
    )
```
